32 devices in a mesh: freq: 4 (over y, x), tile: 8 (over z, core).
Axes of the slice: x: 2, y: 2, z: 4, core: 2. Of those that a mesh axis runs over, the one named last changes fastest.
Arguments:
- x_field: bfloat16 [4, 2, 5120, 256], P('freq', None, 'tile'), may hold values from -6 to 6
- data: bfloat16 [4, 2, 5120, 256], P('freq', None, 'tile'), may hold values from -6 to 6
- u_bases: bfloat16 [4, 8, 8, 128, 2, 640], P('freq', 'tile'), may hold values from -0.21875 to 0.21875
- v_bases: bfloat16 [4, 8, 8, 128, 2, 640], P('freq', None, 'tile'), may hold values from -0.15625 to 0.15625
- ranks: int32 [4, 8, 8], P('freq'), may hold values from 49 to 96, as said below
- onset: int32 [5120, 256], P(('tile', 'freq')), may hold values from 0 to 3
Outputs:
- gradient: float32 [8, 5120, 256], P(None, ('tile', 'freq'))
The draws below stay inside these ranges and needn't reach their ends.
Inputs may be any that keep to these rules, and one draw needn't show every extreme that they name: ranks[f,r,c] is the rank of tile (r, c) at frequency f; it is at most 96, and equal to 96 for some tile of every frequency.
All inputs are finite; a program needn't handle non-finite values.
Results may differ from the reference program's by a relative error of at most 0.0055.
Values may be sent and summed in bfloat16 or wider, within the bound.
No kernel may reach another device: no remote copies, remote signals or barrier semaphores. Data moves between devices by JAX's collectives and lax.ppermute only.
A program may use at most 64 MiB of HBM per device.

```python
import math
import jax
import jax.numpy as jnp
from jax import lax

TILE = 640
RPAD = 128
RMAX = 96
RMIN = 49
NVIRT = 256
NTILE = 8
NS = 5120
NF = 4
NT = 8


def draw_ranks(key, part):
    first_key, second_key = jax.random.split(jax.random.fold_in(key, 17))
    sampled = jax.random.randint(first_key, (NF, NTILE * NTILE), RMIN, RMAX + 1)
    chosen = jax.random.randint(second_key, (NF, 1), 0, NTILE * NTILE)
    tile_slots = jnp.arange(NTILE * NTILE, dtype=jnp.int32)[None, :]
    return jnp.where(tile_slots == chosen, RMAX, sampled).reshape(NF, NTILE, NTILE).astype(jnp.int32)


def set_ends(array, own_key, least, top_value):
    longest = array.shape.index(max(array.shape))
    spots = []
    for shift in (0, 1):
        where = [jax.random.randint(jax.random.fold_in(own_key, axis), (), 0, length) for axis, length in enumerate(array.shape)]
        where[longest] = (where[longest] + shift) % array.shape[longest]
        spots.append(tuple(where))
    return array.at[spots[0]].set(least).at[spots[1]].set(top_value)


def level_of(own_key, dims, cuts, least, top_value):
    def one(axis_at, shards_of):
        heights = jax.random.uniform(jax.random.fold_in(jax.random.fold_in(own_key, 6), axis_at), (shards_of,), jnp.float32, least / len(cuts), top_value / len(cuts))
        return jnp.repeat(jnp.exp(heights), dims[axis_at] // shards_of).reshape((-1,) + (1,) * (len(dims) - axis_at - 1))

    level = one(*cuts[0])
    for cut in cuts[1:]:
        level = level * one(*cut)
    return level


def centred(own_key, shape, width, bound, cuts=(), kind=jnp.bfloat16):
    factor_of = level_of(own_key, shape, cuts, -0.22, 0.18) if cuts else 1.0
    result = jax.random.normal(own_key, shape, jnp.float32) * width * factor_of
    return jnp.minimum(jnp.maximum(result, -bound), bound).astype(kind)


def setup_inputs(seed: int = 0) -> dict:
    keys = jax.random.split(jax.random.key(seed), 7)
    return {
        "x_field": centred(keys[0], (NF, 2, NS, NVIRT), 1.0, 6.0, ((0, 4), (2, 8))),
        "data": centred(keys[1], (NF, 2, NS, NVIRT), 1.0, 6.0, ((0, 4), (2, 8))),
        "u_bases": centred(keys[2], (NF, NTILE, NTILE, RPAD, 2, TILE), (NTILE * RMAX) ** -0.5, 0.21875, ((0, 4), (1, 8))),
        "v_bases": centred(keys[3], (NF, NTILE, NTILE, RPAD, 2, TILE), (2 * TILE) ** -0.5, 0.15625, ((0, 4), (2, 8))),
        "ranks": draw_ranks(jax.random.fold_in(keys[6], 71), 0),
        "onset": set_ends(jax.random.randint(keys[5], (NS, NVIRT), 0, NT // 2), jax.random.fold_in(keys[5], 1), 0, (NT // 2) - 1).astype(jnp.int32),
    }


PRECISE = lax.Precision.HIGHEST

def conj_apply(factors, vectors):
    partner = jnp.stack([vectors[1], -vectors[0]])
    stacked = jnp.stack([vectors, partner], axis=2)
    return jnp.einsum('nkps,psov->nkov', factors.astype(jnp.float32), stacked.astype(jnp.float32), precision=PRECISE)

def apply_factors(factors, weights):
    real_part = weights[:, :, 0]
    imag_part = weights[:, :, 1]
    blended = jnp.stack([jnp.stack([real_part, imag_part], axis=2), jnp.stack([-imag_part, real_part], axis=2)], axis=2)
    return jnp.einsum('nkps,nkpov->osv', factors.astype(jnp.float32), blended.astype(jnp.float32), precision=PRECISE)

def column_step(operands):
    return conj_apply(operands[0], operands[1])

def row_step(operands):
    return apply_factors(operands[0], operands[1])

def one_frequency(operands):
    u_freq, v_freq, x_freq, d_freq, rank_freq = operands
    rank_mask = (jnp.arange(RPAD, dtype=jnp.int32)[None, None, :] < rank_freq[:, :, None]).astype(jnp.float32)
    x_blocks = jnp.transpose(x_freq.reshape(2, NTILE, TILE, NVIRT), (1, 0, 2, 3))
    d_blocks = jnp.transpose(d_freq.reshape(2, NTILE, TILE, NVIRT), (1, 0, 2, 3))
    v_columns = jnp.moveaxis(v_freq, 1, 0)
    coeffs = jnp.moveaxis(lax.map(column_step, (v_columns, x_blocks)), 0, 1)
    coeffs = (coeffs * rank_mask[:, :, :, None, None]).astype(jnp.bfloat16)
    predicted = lax.map(row_step, (u_freq, coeffs))
    residual = (predicted - d_blocks.astype(jnp.float32)).astype(jnp.bfloat16)
    adjoint = lax.map(column_step, (u_freq, residual))
    adjoint = (adjoint * rank_mask[:, :, :, None, None]).astype(jnp.bfloat16)
    spectra = lax.map(row_step, (v_columns, jnp.moveaxis(adjoint, 0, 1)))
    return spectra.astype(jnp.bfloat16)

def reference(x_field, data, u_bases, v_bases, ranks, onset):
    spectra = lax.map(one_frequency, (u_bases, v_bases, x_field, data, ranks))
    spectra = jnp.transpose(spectra, (0, 2, 1, 3, 4)).reshape(NF, 2, NS, NVIRT).astype(jnp.float32)
    moments = jnp.arange(NT, dtype=jnp.int32)
    orders = jnp.arange(1, NF + 1, dtype=jnp.int32)
    phases = moments[:, None] * orders[None, :] % NT
    angles = 2.0 * math.pi / NT * phases.astype(jnp.float32)
    cosine = jnp.cos(angles)
    sine_part = jnp.sin(angles)
    traces = jnp.dot(cosine, spectra[:, 0].reshape(NF, -1), precision=PRECISE) - jnp.dot(sine_part, spectra[:, 1].reshape(NF, -1), precision=PRECISE)
    traces = (traces * (1.0 / math.sqrt(NF))).reshape(NT, NS, NVIRT)
    return jnp.where(moments[:, None, None] >= onset[None], traces, jnp.float32(0.0))
```

```python
import functools
import math

import jax
import jax.numpy as jnp
from jax import lax
from jax.experimental import pallas as pl
from jax.experimental.pallas import tpu as pltpu
from jax.sharding import PartitionSpec as P

RMAX = 96
LANES = 128
BF16 = jnp.bfloat16
F32 = jnp.float32
VMEM = pl.BlockSpec(memory_space=pltpu.VMEM)
SMEM = pl.BlockSpec(memory_space=pltpu.SMEM)
ANY = pl.BlockSpec(memory_space=pl.ANY)


def params():
    return pltpu.CompilerParams(vmem_limit_bytes=48 * 1024 * 1024)


def masked(rows, value, rank):
    level = lax.broadcasted_iota(jnp.int32, (rows, value.shape[1]), 0)
    return jnp.where(level < rank, value, 0.0).astype(BF16)


def coeff_kernel(count, ks, group, *refs):
    rank_ref, v_hbm, x_hbm = refs[:3]
    outs = refs[3 : 3 + len(ks)]
    factors, field, wide, product, sems, field_sem = refs[3 + len(ks) :]
    me = lax.axis_index("tile")
    stations = field.shape[1]
    virtual = field.shape[2]
    copies = []
    for i, k in enumerate(ks):
        copy = pltpu.make_async_copy(
            v_hbm.at[me ^ k, pl.ds(0, RMAX)], factors.at[i], sems.at[i]
        )
        copies.append(copy)
    field_copy = pltpu.make_async_copy(x_hbm, field, field_sem)
    field_copy.start()
    for copy in copies:
        copy.start()
    field_copy.wait()
    wide[:, :virtual] = field[0]
    wide[:, virtual:] = field[1]
    parts = 2 * virtual // LANES
    half = parts // 2
    for start in range(0, len(ks), group):
        for i in range(start, start + group):
            copies[i].wait()
        left = factors[pl.ds(start, group)].reshape(group * 2 * RMAX, stations)
        result = jnp.dot(left, wide[...], preferred_element_type=F32)
        for j in range(parts):
            product[j] = result[:, j * LANES : (j + 1) * LANES]
        for i in range(group):
            k = ks[start + i]
            rank = rank_ref[me ^ k, me]
            base = i * 2 * RMAX
            even = [product[j, pl.ds(base, RMAX, stride=2), :] for j in range(parts)]
            odd = [product[j, pl.ds(base + 1, RMAX, stride=2), :] for j in range(parts)]
            for j in range(half):
                outs[start + i][:, j * LANES : (j + 1) * LANES] = masked(
                    RMAX, even[j] + odd[half + j], rank
                )
                outs[start + i][:, (half + j) * LANES : (half + j + 1) * LANES] = masked(
                    RMAX, even[half + j] - odd[j], rank
                )


def coeff_blocks(ranks, v, x, ks, group):
    count = v.shape[0]
    stations, virtual = x.shape[1], x.shape[2]
    return pl.pallas_call(
        functools.partial(coeff_kernel, count, ks, group),
        out_shape=[jax.ShapeDtypeStruct((RMAX, 2 * virtual), BF16) for _ in ks],
        in_specs=[SMEM, ANY, ANY],
        out_specs=[VMEM for _ in ks],
        scratch_shapes=[
            pltpu.VMEM((len(ks), RMAX, 2, stations), BF16),
            pltpu.VMEM((2, stations, virtual), BF16),
            pltpu.VMEM((stations, 2 * virtual), BF16),
            pltpu.VMEM((2 * virtual // LANES, group * 2 * RMAX, LANES), F32),
            pltpu.SemaphoreType.DMA((len(ks),)),
            pltpu.SemaphoreType.DMA,
        ],
        compiler_params=params(),
        cost_estimate=pl.CostEstimate(flops=10**9, bytes_accessed=10**7, transcendentals=0),
        name="coeff_blocks",
    )(ranks, v, x)


def prepare_kernel(want_rows, *refs):
    w_hbm, _ = refs[:2]
    if want_rows:
        rows_ref, turned_ref, factors, spread, sems = refs[2:]
    else:
        turned_ref, factors, spread, rows_ref, sems = refs[2:]
    count = factors.shape[0]
    stations = factors.shape[3]
    copies = [
        pltpu.make_async_copy(w_hbm.at[r, pl.ds(0, RMAX)], factors.at[r], sems.at[r])
        for r in range(count)
    ]
    for copy in copies:
        copy.start()
    for r in range(count):
        copies[r].wait()
        flat = factors[r].reshape(2 * RMAX, stations).astype(F32)
        for j in range(stations // LANES):
            spread[j] = flat[:, j * LANES : (j + 1) * LANES]
        for p in range(2):
            for j in range(stations // LANES):
                rows_ref[
                    r * RMAX : (r + 1) * RMAX,
                    p * stations + j * LANES : p * stations + (j + 1) * LANES,
                ] = spread[j, pl.ds(p, RMAX, stride=2), :].astype(BF16)
    total = count * RMAX
    for p in range(2):
        for i in range(total // LANES):
            block = rows_ref[i * LANES : (i + 1) * LANES, p * stations : (p + 1) * stations]
            turned_ref[:, p * total + i * LANES : p * total + (i + 1) * LANES] = block.T


def prepare(w, after, want_rows):
    count, _, _, stations = w.shape
    rows_shape = (count * RMAX, 2 * stations)
    turned_shape = (stations, 2 * count * RMAX)
    outs = [jax.ShapeDtypeStruct(turned_shape, BF16)]
    scratch = [
        pltpu.VMEM((count, RMAX, 2, stations), BF16),
        pltpu.VMEM((stations // LANES, 2 * RMAX, LANES), F32),
    ]
    if want_rows:
        outs = [jax.ShapeDtypeStruct(rows_shape, BF16)] + outs
    else:
        scratch.append(pltpu.VMEM(rows_shape, BF16))
    scratch.append(pltpu.SemaphoreType.DMA((count,)))
    return pl.pallas_call(
        functools.partial(prepare_kernel, want_rows),
        out_shape=outs,
        in_specs=[ANY, ANY],
        out_specs=[VMEM for _ in outs],
        scratch_shapes=scratch,
        compiler_params=params(),
        cost_estimate=pl.CostEstimate(flops=10**9, bytes_accessed=10**7, transcendentals=0),
        name="prepare",
    )(w, after)


def stack_blocks(me, blocks, first, second):
    virtual = blocks[0].shape[1] // 2
    for k, block in enumerate(blocks):
        rows = pl.ds(pl.multiple_of((me ^ k) * RMAX, RMAX), RMAX)
        first[rows, :] = block[...]
        second[rows, :virtual] = -block[:, virtual:]
        second[rows, virtual:] = block[:, :virtual]


def residual_kernel(count, *refs):
    rank_ref, rows_ref, turned_ref, data_ref = refs[:4]
    blocks = refs[4 : 4 + count]
    outs = refs[4 + count : 4 + 2 * count]
    first, second, stacked, adjoint = refs[4 + 2 * count :]
    me = lax.axis_index("tile")
    stations, virtual = data_ref.shape[1], data_ref.shape[2]
    total = count * RMAX
    stack_blocks(me, blocks, first, second)
    predicted = jnp.dot(turned_ref[:, :total], first[...], preferred_element_type=F32)
    predicted += jnp.dot(turned_ref[:, total:], second[...], preferred_element_type=F32)
    real = (predicted[:, :virtual] - data_ref[0].astype(F32)).astype(BF16)
    imag = (predicted[:, virtual:] - data_ref[1].astype(F32)).astype(BF16)
    stacked[:stations, :virtual] = real
    stacked[:stations, virtual:] = imag
    stacked[stations:, :virtual] = imag
    stacked[stations:, virtual:] = -real
    result = jnp.dot(rows_ref[...], stacked[...], preferred_element_type=F32)
    for c in range(count):
        adjoint[c * RMAX : (c + 1) * RMAX, :] = masked(
            RMAX, result[c * RMAX : (c + 1) * RMAX, :], rank_ref[me, c]
        )
    for k in range(count):
        rows = pl.ds(pl.multiple_of((me ^ k) * RMAX, RMAX), RMAX)
        outs[k][...] = adjoint[rows, :]


def residual_blocks(ranks, rows, turned, data, blocks):
    count = len(blocks)
    stations, virtual = data.shape[1], data.shape[2]
    return pl.pallas_call(
        functools.partial(residual_kernel, count),
        out_shape=[jax.ShapeDtypeStruct((RMAX, 2 * virtual), BF16) for _ in blocks],
        in_specs=[SMEM] + [VMEM] * (3 + count),
        out_specs=[VMEM for _ in blocks],
        scratch_shapes=[
            pltpu.VMEM((count * RMAX, 2 * virtual), BF16),
            pltpu.VMEM((count * RMAX, 2 * virtual), BF16),
            pltpu.VMEM((2 * stations, 2 * virtual), BF16),
            pltpu.VMEM((count * RMAX, 2 * virtual), BF16),
        ],
        compiler_params=params(),
        cost_estimate=pl.CostEstimate(flops=2 * 10**9, bytes_accessed=10**7, transcendentals=0),
        name="residual_blocks",
    )(ranks, rows, turned, data, *blocks)


def spectrum_kernel(count, freqs, *refs):
    turned_ref = refs[0]
    blocks = refs[1 : 1 + count]
    outs = refs[1 + count : 1 + count + freqs]
    first, second, spectrum = refs[1 + count + freqs :]
    me = lax.axis_index("tile")
    mine = lax.axis_index("freq")
    total = count * RMAX
    stack_blocks(me, blocks, first, second)
    result = jnp.dot(turned_ref[:, :total], first[...], preferred_element_type=F32)
    result += jnp.dot(turned_ref[:, total:], second[...], preferred_element_type=F32)
    spectrum[...] = result
    share = outs[0].shape[0]
    for k in range(freqs):
        rows = pl.ds(pl.multiple_of((mine ^ k) * share, 8), share)
        outs[k][...] = spectrum[rows, :].astype(BF16)


def spectrum_blocks(turned, blocks, freqs):
    count = len(blocks)
    stations = turned.shape[0]
    width = blocks[0].shape[1]
    return pl.pallas_call(
        functools.partial(spectrum_kernel, count, freqs),
        out_shape=[jax.ShapeDtypeStruct((stations // freqs, width), BF16) for _ in range(freqs)],
        in_specs=[VMEM] * (1 + count),
        out_specs=[VMEM] * freqs,
        scratch_shapes=[
            pltpu.VMEM((count * RMAX, width), BF16),
            pltpu.VMEM((count * RMAX, width), BF16),
            pltpu.VMEM((stations, width), F32),
        ],
        compiler_params=params(),
        cost_estimate=pl.CostEstimate(flops=10**9, bytes_accessed=10**7, transcendentals=0),
        name="spectrum_blocks",
    )(turned, *blocks)


def traces_kernel(freqs, *refs):
    onset_ref = refs[0]
    blocks = refs[1 : 1 + freqs]
    out_ref, gathered = refs[1 + freqs :]
    mine = lax.axis_index("freq")
    virtual = onset_ref.shape[1]
    for k in range(freqs):
        gathered[mine ^ k] = blocks[k][...]
    times = 2 * freqs
    scaling = 1.0 / math.sqrt(freqs)
    onset = onset_ref[...]
    for t in range(freqs):
        sums = [None, None]
        for f in range(freqs):
            turn = (f + 1) * t % times
            angle = 2.0 * math.pi * turn / times
            quarter = 4 * turn % times == 0
            terms = []
            for part, weight in ((0, math.cos(angle)), (1, -math.sin(angle))):
                if quarter:
                    weight = float(round(weight))
                if weight != 0.0:
                    value = gathered[f, :, part * virtual : (part + 1) * virtual]
                    terms.append(value.astype(F32) * (weight * scaling))
            for term in terms:
                old = sums[f % 2]
                sums[f % 2] = term if old is None else old + term
        odd, even = sums
        out_ref[t] = jnp.where(t >= onset, even + odd, 0.0)
        out_ref[t + freqs] = jnp.where(t + freqs >= onset, even - odd, 0.0)


def gated_traces(onset, blocks):
    freqs = len(blocks)
    share, virtual = onset.shape
    return pl.pallas_call(
        functools.partial(traces_kernel, freqs),
        out_shape=jax.ShapeDtypeStruct((2 * freqs, share, virtual), F32),
        in_specs=[VMEM] * (1 + freqs),
        out_specs=VMEM,
        scratch_shapes=[pltpu.VMEM((freqs, share, 2 * virtual), BF16)],
        compiler_params=params(),
        name="gated_traces",
    )(onset, *blocks)


def exchange(blocks, axis):
    count = lax.axis_size(axis)
    received = [blocks[0]]
    for k in range(1, count):
        received.append(lax.ppermute(blocks[k], axis, [(i, i ^ k) for i in range(count)]))
    return received


def body(x_field, data, u_bases, v_bases, ranks, onset):
    count = lax.axis_size("tile")
    freqs = lax.axis_size("freq")
    table = ranks[0]
    u = u_bases[0, 0]
    v = v_bases[0, :, 0]
    coeffs = coeff_blocks(table, v, x_field[0], tuple(range(count)), 4)
    arrived = exchange(coeffs, "tile")
    u_rows, u_turned = prepare(u, coeffs[0], True)
    (v_turned,) = prepare(v, u_turned, False)
    adjoint = residual_blocks(table, u_rows, u_turned, data[0], arrived)
    returned = exchange(adjoint, "tile")
    spectrum = spectrum_blocks(v_turned, returned, freqs)
    return gated_traces(onset, exchange(spectrum, "freq"))


def solution(mesh):
    in_specs = (
        P("freq", None, "tile", None),
        P("freq", None, "tile", None),
        P("freq", "tile", None, None, None, None),
        P("freq", None, "tile", None, None, None),
        P("freq", None, None),
        P(("tile", "freq"), None),
    )
    out_specs = P(None, ("tile", "freq"), None)
    return jax.shard_map(body, mesh=mesh, in_specs=in_specs, out_specs=out_specs, check_vma=False)
```

```python
import functools
import math

import jax
import jax.numpy as jnp
from jax import lax
from jax.experimental import pallas as pl
from jax.experimental.pallas import tpu as pltpu
from jax.sharding import PartitionSpec as P


RMAX = 96
LANES = 128
BF16 = jnp.bfloat16
F32 = jnp.float32
VMEM = pl.BlockSpec(memory_space=pltpu.VMEM)
SMEM = pl.BlockSpec(memory_space=pltpu.SMEM)
ANY = pl.BlockSpec(memory_space=pl.ANY)
HBM = pl.BlockSpec(memory_space=pltpu.MemorySpace.HBM)


def params():
    return pltpu.CompilerParams(vmem_limit_bytes=48 * 1024 * 1024)


def masked(value, rank):
    level = lax.broadcasted_iota(jnp.int32, value.shape, 0)
    return jnp.where(level < rank, value, 0.0).astype(BF16)


def cost(flops):
    return pl.CostEstimate(flops=flops, bytes_accessed=10**7, transcendentals=0)


def coeff_kernel(ks, group, *refs):
    rank_hbm, v_hbm, x_hbm, _ = refs[:4]
    outs = refs[4 : 4 + len(ks)]
    rank_ref, factors, field, wide, product, sems, field_sem, rank_sem = refs[4 + len(ks) :]
    me = lax.axis_index("tile")
    stations = field.shape[1]
    virtual = field.shape[2]
    rank_copy = pltpu.make_async_copy(rank_hbm, rank_ref, rank_sem)
    field_copy = pltpu.make_async_copy(x_hbm, field, field_sem)
    copies = [
        pltpu.make_async_copy(v_hbm.at[me ^ k, pl.ds(0, RMAX)], factors.at[i], sems.at[i])
        for i, k in enumerate(ks)
    ]
    field_copy.start()
    for copy in copies:
        copy.start()
    rank_copy.start()
    field_copy.wait()
    wide[:, :virtual] = field[0]
    wide[:, virtual:] = field[1]
    rank_copy.wait()
    parts = 2 * virtual // LANES
    half = parts // 2
    for start in range(0, len(ks), group):
        for i in range(start, start + group):
            copies[i].wait()
        left = factors[pl.ds(start, group)].reshape(group * 2 * RMAX, stations)
        result = jnp.dot(left, wide[...], preferred_element_type=F32)
        for j in range(parts):
            product[j] = result[:, j * LANES : (j + 1) * LANES]
        for i in range(group):
            out = outs[start + i]
            rank = rank_ref[me ^ ks[start + i], me]
            base = i * 2 * RMAX
            even = [product[j, pl.ds(base, RMAX, stride=2), :] for j in range(parts)]
            odd = [product[j, pl.ds(base + 1, RMAX, stride=2), :] for j in range(parts)]
            for j in range(half):
                real = masked(even[j] + odd[half + j], rank)
                imag = masked(even[half + j] - odd[j], rank)
                out[:, j * LANES : (j + 1) * LANES] = real
                out[:, (half + j) * LANES : (half + j + 1) * LANES] = imag


def coeff_blocks(ranks, v, x, after, ks, group):
    stations, virtual = x.shape[1], x.shape[2]
    return pl.pallas_call(
        functools.partial(coeff_kernel, ks, group),
        out_shape=[jax.ShapeDtypeStruct((RMAX, 2 * virtual), BF16) for _ in ks],
        in_specs=[HBM, HBM, HBM, ANY],
        out_specs=[VMEM for _ in ks],
        scratch_shapes=[
            pltpu.SMEM(ranks.shape, jnp.int32),
            pltpu.VMEM((len(ks), RMAX, 2, stations), BF16),
            pltpu.VMEM((2, stations, virtual), BF16),
            pltpu.VMEM((stations, 2 * virtual), BF16),
            pltpu.VMEM((2 * virtual // LANES, group * 2 * RMAX, LANES), F32),
            pltpu.SemaphoreType.DMA((len(ks),)),
            pltpu.SemaphoreType.DMA,
            pltpu.SemaphoreType.DMA,
        ],
        compiler_params=params(),
        cost_estimate=cost(10**9),
        name="coeff_blocks",
    )(ranks, v, x, after)


def prepare_kernel(want_rows, *refs):
    w_hbm, _ = refs[:2]
    turned_ref = refs[2]
    if want_rows:
        rows_ref = refs[3]
        factors, spread, paired, sems = refs[4:]
    else:
        rows_ref = None
        factors, spread, paired, sems = refs[3:]
    count = factors.shape[0]
    stations = factors.shape[3]
    columns = stations // LANES
    copies = [
        pltpu.make_async_copy(w_hbm.at[r, pl.ds(0, RMAX)], factors.at[r], sems.at[r])
        for r in range(count)
    ]
    for copy in copies:
        copy.start()
    for r in range(count):
        copies[r].wait()
        flat = factors[r].reshape(2 * RMAX, stations).astype(F32)
        for j in range(columns):
            spread[j] = flat[:, j * LANES : (j + 1) * LANES]
        for p in range(2):
            for j in range(columns):
                piece = spread[j, pl.ds(p, RMAX, stride=2), :].astype(BF16)
                row = (2 * p + r % 2) * RMAX
                paired[row : row + RMAX, j * LANES : (j + 1) * LANES] = piece
                if rows_ref is not None:
                    column = p * stations + j * LANES
                    rows_ref[r * RMAX : (r + 1) * RMAX, column : column + LANES] = piece
        if r % 2:
            for i in range(4 * RMAX // LANES):
                block = paired[i * LANES : (i + 1) * LANES, :]
                turned_ref[r // 2, :, i * LANES : (i + 1) * LANES] = block.T


def prepare(w, after, want_rows):
    count, _, _, stations = w.shape
    outs = [jax.ShapeDtypeStruct((count // 2, stations, 4 * RMAX), BF16)]
    if want_rows:
        outs.append(jax.ShapeDtypeStruct((count * RMAX, 2 * stations), BF16))
    return pl.pallas_call(
        functools.partial(prepare_kernel, want_rows),
        out_shape=outs,
        in_specs=[HBM, ANY],
        out_specs=[VMEM for _ in outs],
        scratch_shapes=[
            pltpu.VMEM((count, RMAX, 2, stations), BF16),
            pltpu.VMEM((stations // LANES, 2 * RMAX, LANES), F32),
            pltpu.VMEM((4 * RMAX, stations), BF16),
            pltpu.SemaphoreType.DMA((count,)),
        ],
        compiler_params=params(),
        cost_estimate=cost(10**9),
        name="prepare",
    )(w, after)


def apply_pairs(bases, blocks, turned_ref, stack):
    me = lax.axis_index("tile")
    virtual = blocks[0].shape[1] // 2
    total = None
    for i, base in enumerate(bases):
        for b in range(2):
            block = blocks[2 * i + b]
            slot = (me ^ b) & 1
            rows = pl.ds(pl.multiple_of(slot * RMAX, RMAX), RMAX)
            stack[i, rows, :] = block[...]
            rows = pl.ds(pl.multiple_of((slot + 2) * RMAX, RMAX), RMAX)
            stack[i, rows, :virtual] = -block[:, virtual:]
            stack[i, rows, virtual:] = block[:, :virtual]
        term = jnp.dot(
            turned_ref[(me ^ base) >> 1], stack[i], preferred_element_type=F32
        )
        total = term if total is None else total + term
    return total


def partial_kernel(bases, *refs):
    turned_ref = refs[0]
    blocks = refs[1 : 1 + 2 * len(bases)]
    out_ref, stack = refs[1 + 2 * len(bases) :]
    out_ref[...] = apply_pairs(bases, blocks, turned_ref, stack)


def partial_sum(turned, bases, blocks):
    stations = turned.shape[1]
    width = blocks[0].shape[1]
    return pl.pallas_call(
        functools.partial(partial_kernel, bases),
        out_shape=jax.ShapeDtypeStruct((stations, width), F32),
        in_specs=[VMEM] * (1 + len(blocks)),
        out_specs=VMEM,
        scratch_shapes=[pltpu.VMEM((len(bases), 4 * RMAX, width), BF16)],
        compiler_params=params(),
        cost_estimate=cost(10**9),
        name="partial_sum",
    )(turned, *blocks)


def adjoint_outputs(ks, rank_ref, rows_ref, stacked, result, outs):
    me = lax.axis_index("tile")
    for i in range(0, len(ks), 2):
        pair = (me ^ ks[i]) >> 1
        rows = pl.ds(pl.multiple_of(pair * 2 * RMAX, 2 * RMAX), 2 * RMAX)
        product = jnp.dot(rows_ref[rows, :], stacked[...], preferred_element_type=F32)
        for b in range(2):
            result[b * RMAX : (b + 1) * RMAX, :] = masked(
                product[b * RMAX : (b + 1) * RMAX, :], rank_ref[me, 2 * pair + b]
            )
        for b in range(2):
            slot = (me ^ ks[i + b]) & 1
            outs[i + b][...] = result[pl.ds(pl.multiple_of(slot * RMAX, RMAX), RMAX), :]


def residual_kernel(base, ks, *refs):
    rank_ref, rows_ref, turned_ref, data_ref, partial_ref = refs[:5]
    blocks = refs[5:7]
    outs = refs[7 : 7 + len(ks)]
    stacked, stack, result = refs[7 + len(ks) :]
    stations, virtual = data_ref.shape[1], data_ref.shape[2]
    predicted = partial_ref[...] + apply_pairs((base,), blocks, turned_ref, stack)
    real = (predicted[:, :virtual] - data_ref[0].astype(F32)).astype(BF16)
    imag = (predicted[:, virtual:] - data_ref[1].astype(F32)).astype(BF16)
    stacked[:stations, :virtual] = real
    stacked[:stations, virtual:] = imag
    stacked[stations:, :virtual] = imag
    stacked[stations:, virtual:] = -real
    adjoint_outputs(ks, rank_ref, rows_ref, stacked, result, outs)


def residual_blocks(ranks, rows, turned, data, partial, base, blocks, ks):
    stations, virtual = data.shape[1], data.shape[2]
    outs = [jax.ShapeDtypeStruct((RMAX, 2 * virtual), BF16) for _ in ks]
    outs.append(jax.ShapeDtypeStruct((2 * stations, 2 * virtual), BF16))
    return pl.pallas_call(
        functools.partial(residual_kernel, base, ks),
        out_shape=outs,
        in_specs=[SMEM] + [VMEM] * 6,
        out_specs=[VMEM for _ in outs],
        scratch_shapes=[
            pltpu.VMEM((1, 4 * RMAX, 2 * virtual), BF16),
            pltpu.VMEM((2 * RMAX, 2 * virtual), BF16),
        ],
        compiler_params=params(),
        cost_estimate=cost(10**9),
        name="residual_blocks",
    )(ranks, rows, turned, data, partial, *blocks)


def adjoint_kernel(ks, *refs):
    rank_ref, rows_ref, stacked = refs[:3]
    outs = refs[3 : 3 + len(ks)]
    (result,) = refs[3 + len(ks) :]
    adjoint_outputs(ks, rank_ref, rows_ref, stacked, result, outs)


def adjoint_blocks(ranks, rows, stacked, ks):
    width = stacked.shape[1]
    return pl.pallas_call(
        functools.partial(adjoint_kernel, ks),
        out_shape=[jax.ShapeDtypeStruct((RMAX, width), BF16) for _ in ks],
        in_specs=[SMEM, VMEM, VMEM],
        out_specs=[VMEM for _ in ks],
        scratch_shapes=[pltpu.VMEM((2 * RMAX, width), BF16)],
        compiler_params=params(),
        cost_estimate=cost(10**9),
        name="adjoint_blocks",
    )(ranks, rows, stacked)


def spectrum_kernel(base, freqs, *refs):
    turned_ref, partial_ref = refs[:2]
    blocks = refs[2:4]
    outs = refs[4 : 4 + freqs]
    stack, spectrum = refs[4 + freqs :]
    mine = lax.axis_index("freq")
    spectrum[...] = partial_ref[...] + apply_pairs((base,), blocks, turned_ref, stack)
    share = outs[0].shape[0]
    for k in range(freqs):
        rows = pl.ds(pl.multiple_of((mine ^ k) * share, 8), share)
        outs[k][...] = spectrum[rows, :].astype(BF16)


def spectrum_blocks(turned, partial, base, blocks, freqs):
    stations, width = partial.shape
    return pl.pallas_call(
        functools.partial(spectrum_kernel, base, freqs),
        out_shape=[jax.ShapeDtypeStruct((stations // freqs, width), BF16) for _ in range(freqs)],
        in_specs=[VMEM] * 4,
        out_specs=[VMEM] * freqs,
        scratch_shapes=[
            pltpu.VMEM((1, 4 * RMAX, width), BF16),
            pltpu.VMEM((stations, width), F32),
        ],
        compiler_params=params(),
        cost_estimate=cost(10**9),
        name="spectrum_blocks",
    )(turned, partial, *blocks)


def traces_kernel(freqs, *refs):
    onset_ref = refs[0]
    blocks = refs[1 : 1 + freqs]
    out_ref, gathered = refs[1 + freqs :]
    mine = lax.axis_index("freq")
    virtual = onset_ref.shape[1]
    for k in range(freqs):
        gathered[mine ^ k] = blocks[k][...]
    times = 2 * freqs
    scaling = 1.0 / math.sqrt(freqs)
    onset = onset_ref[...]
    for t in range(freqs):
        sums = [None, None]
        for f in range(freqs):
            turn = (f + 1) * t % times
            angle = 2.0 * math.pi * turn / times
            quarter = 4 * turn % times == 0
            terms = []
            for part, weight in ((0, math.cos(angle)), (1, -math.sin(angle))):
                if quarter:
                    weight = float(round(weight))
                if weight != 0.0:
                    value = gathered[f, :, part * virtual : (part + 1) * virtual]
                    terms.append(value.astype(F32) * (weight * scaling))
            for term in terms:
                old = sums[f % 2]
                sums[f % 2] = term if old is None else old + term
        odd, even = sums
        out_ref[t] = jnp.where(t >= onset, even + odd, 0.0)
        out_ref[t + freqs] = jnp.where(t + freqs >= onset, even - odd, 0.0)


def gated_traces(onset, blocks):
    freqs = len(blocks)
    share, virtual = onset.shape
    return pl.pallas_call(
        functools.partial(traces_kernel, freqs),
        out_shape=jax.ShapeDtypeStruct((2 * freqs, share, virtual), F32),
        in_specs=[VMEM] * (1 + freqs),
        out_specs=VMEM,
        scratch_shapes=[pltpu.VMEM((freqs, share, 2 * virtual), BF16)],
        compiler_params=params(),
        name="gated_traces",
    )(onset, *blocks)


def send(block, axis, k):
    count = lax.axis_size(axis)
    return lax.ppermute(block, axis, [(i, i ^ k) for i in range(count)])


def exchange(ks, blocks):
    return {k: send(b, "tile", k) if k else b for k, b in zip(ks, blocks)}


def pick(arrived, bases):
    return [arrived[base + b] for base in bases for b in range(2)]


def pair_bases(count):
    return list(range(count - 2, -1, -2))


def peer_order(count):
    bases = pair_bases(count)
    half = len(bases) // 2
    far = tuple(base + b for base in bases[:half] for b in range(2))
    near = tuple(base + b for base in bases[half:] for b in range(2))
    return far, near


def hbm(array):
    return pltpu.with_memory_space_constraint(array, pltpu.MemorySpace.HBM)


def body(x_field, data, u_bases, v_bases, ranks, onset):
    count = lax.axis_size("tile")
    freqs = lax.axis_size("freq")
    table = ranks[0]
    u = hbm(u_bases[0, 0])
    v = hbm(v_bases[0, :, 0])
    x = hbm(x_field[0])
    late = count // 2
    early = tuple(base for base in pair_bases(count) if base != late)
    far, near = peer_order(count)
    blocks = coeff_blocks(hbm(table), v, x, table, far, 2)
    arrived = exchange(far, blocks)
    blocks = coeff_blocks(hbm(table), v, x, blocks[0], near, 2)
    arrived |= exchange(near, blocks)
    u_turned, u_rows = prepare(u, blocks[0], True)
    partial = partial_sum(u_turned, early, pick(arrived, early))
    *blocks, stacked = residual_blocks(
        table, u_rows, u_turned, data[0], partial, late, pick(arrived, (late,)), far
    )
    returned = exchange(far, blocks)
    blocks = adjoint_blocks(table, u_rows, stacked, near)
    returned |= exchange(near, blocks)
    (v_turned,) = prepare(v, stacked, False)
    partial = partial_sum(v_turned, early, pick(returned, early))
    spectrum = spectrum_blocks(v_turned, partial, late, pick(returned, (late,)), freqs)
    spectra = [send(block, "freq", k) if k else block for k, block in enumerate(spectrum)]
    return gated_traces(onset, spectra)


def solution(mesh):
    in_specs = (
        P("freq", None, "tile", None),
        P("freq", None, "tile", None),
        P("freq", "tile", None, None, None, None),
        P("freq", None, "tile", None, None, None),
        P("freq", None, None),
        P(("tile", "freq"), None),
    )
    out_specs = P(None, ("tile", "freq"), None)

    return jax.shard_map(
        body, mesh=mesh, in_specs=in_specs, out_specs=out_specs, check_vma=False
    )
```

```python
import functools
import math

import jax
import jax.numpy as jnp
from jax import lax
from jax.experimental import pallas as pl
from jax.experimental.pallas import tpu as pltpu
from jax.sharding import PartitionSpec as P


RMAX = 96
LANES = 128
BF16 = jnp.bfloat16
F32 = jnp.float32
VMEM = pl.BlockSpec(memory_space=pltpu.VMEM)
SMEM = pl.BlockSpec(memory_space=pltpu.SMEM)
ANY = pl.BlockSpec(memory_space=pl.ANY)
HBM = pl.BlockSpec(memory_space=pltpu.MemorySpace.HBM)


def params():
    return pltpu.CompilerParams(vmem_limit_bytes=48 * 1024 * 1024)


def masked(value, rank):
    level = lax.broadcasted_iota(jnp.int32, value.shape, 0)
    return jnp.where(level < rank, value, 0.0).astype(BF16)


def cost(flops):
    return pl.CostEstimate(flops=flops, bytes_accessed=10**7, transcendentals=0)


def coeff_outputs(ks, rank_ref, factors, wide, product, outs):
    me = lax.axis_index("tile")
    stations = factors.shape[3]
    left = factors[...].reshape(len(ks) * 2 * RMAX, stations)
    result = jnp.dot(left, wide[...], preferred_element_type=F32)
    parts = wide.shape[1] // LANES
    half = parts // 2
    for j in range(parts):
        product[j] = result[:, j * LANES : (j + 1) * LANES]
    for i, k in enumerate(ks):
        rank = rank_ref[me ^ k, me]
        base = i * 2 * RMAX
        even = [product[j, pl.ds(base, RMAX, stride=2), :] for j in range(parts)]
        odd = [product[j, pl.ds(base + 1, RMAX, stride=2), :] for j in range(parts)]
        for j in range(half):
            real = masked(even[j] + odd[half + j], rank)
            imag = masked(even[half + j] - odd[j], rank)
            outs[i][:, j * LANES : (j + 1) * LANES] = real
            outs[i][:, (half + j) * LANES : (half + j + 1) * LANES] = imag


def coeff_far_kernel(far, near, *refs):
    rank_hbm, v_hbm, x_hbm = refs[:3]
    outs = refs[3 : 3 + len(far)]
    wide, near_factors = refs[3 + len(far) : 5 + len(far)]
    rank_ref, factors, field, product, sems, near_sems, field_sem, rank_sem = refs[5 + len(far) :]
    me = lax.axis_index("tile")
    virtual = field.shape[2]
    rank_copy = pltpu.make_async_copy(rank_hbm, rank_ref, rank_sem)
    field_copy = pltpu.make_async_copy(x_hbm, field, field_sem)
    far_copies = [
        pltpu.make_async_copy(v_hbm.at[me ^ k, pl.ds(0, RMAX)], factors.at[i], sems.at[i])
        for i, k in enumerate(far)
    ]
    near_copies = [
        pltpu.make_async_copy(
            v_hbm.at[me ^ k, pl.ds(0, RMAX)], near_factors.at[i], near_sems.at[i]
        )
        for i, k in enumerate(near)
    ]
    field_copy.start()
    for copy in far_copies:
        copy.start()
    rank_copy.start()
    for copy in near_copies:
        copy.start()
    field_copy.wait()
    wide[:, :virtual] = field[0]
    wide[:, virtual:] = field[1]
    rank_copy.wait()
    for copy in far_copies:
        copy.wait()
    coeff_outputs(far, rank_ref, factors, wide, product, outs)
    for copy in near_copies:
        copy.wait()


def coeff_far(ranks, v, x, far, near):
    stations, virtual = x.shape[1], x.shape[2]
    outs = [jax.ShapeDtypeStruct((RMAX, 2 * virtual), BF16) for _ in far]
    outs.append(jax.ShapeDtypeStruct((stations, 2 * virtual), BF16))
    outs.append(jax.ShapeDtypeStruct((len(near), RMAX, 2, stations), BF16))
    return pl.pallas_call(
        functools.partial(coeff_far_kernel, far, near),
        out_shape=outs,
        in_specs=[HBM, HBM, HBM],
        out_specs=[VMEM for _ in outs],
        scratch_shapes=[
            pltpu.SMEM(ranks.shape, jnp.int32),
            pltpu.VMEM((len(far), RMAX, 2, stations), BF16),
            pltpu.VMEM((2, stations, virtual), BF16),
            pltpu.VMEM((2 * virtual // LANES, len(far) * 2 * RMAX, LANES), F32),
            pltpu.SemaphoreType.DMA((len(far),)),
            pltpu.SemaphoreType.DMA((len(near),)),
            pltpu.SemaphoreType.DMA,
            pltpu.SemaphoreType.DMA,
        ],
        compiler_params=params(),
        cost_estimate=cost(10**9),
        name="coeff_far",
    )(ranks, v, x)


def coeff_near_kernel(near, *refs):
    rank_ref, wide, factors = refs[:3]
    coeff_outputs(near, rank_ref, factors, wide, refs[-1], refs[3 : 3 + len(near)])


def coeff_near(ranks, wide, factors, near):
    width = wide.shape[1]
    return pl.pallas_call(
        functools.partial(coeff_near_kernel, near),
        out_shape=[jax.ShapeDtypeStruct((RMAX, width), BF16) for _ in near],
        in_specs=[SMEM, VMEM, VMEM],
        out_specs=[VMEM for _ in near],
        scratch_shapes=[pltpu.VMEM((width // LANES, len(near) * 2 * RMAX, LANES), F32)],
        compiler_params=params(),
        cost_estimate=cost(10**9),
        name="coeff_near",
    )(ranks, wide, factors)


def prepare_kernel(want_rows, *refs):
    w_hbm, _ = refs[:2]
    turned_ref = refs[2]
    if want_rows:
        rows_ref = refs[3]
        factors, spread, paired, sems = refs[4:]
    else:
        rows_ref = None
        factors, spread, paired, sems = refs[3:]
    me = lax.axis_index("tile")
    count = factors.shape[0]
    stations = factors.shape[3]
    columns = stations // LANES
    copies = [
        pltpu.make_async_copy(w_hbm.at[me ^ k, pl.ds(0, RMAX)], factors.at[k], sems.at[k])
        for k in range(count)
    ]
    for copy in copies:
        copy.start()
    for k in range(count):
        copies[k].wait()
        flat = factors[k].reshape(2 * RMAX, stations).astype(F32)
        for j in range(columns):
            spread[j] = flat[:, j * LANES : (j + 1) * LANES]
        for p in range(2):
            for j in range(columns):
                piece = spread[j, pl.ds(p, RMAX, stride=2), :].astype(BF16)
                row = (2 * p + k % 2) * RMAX
                paired[row : row + RMAX, j * LANES : (j + 1) * LANES] = piece
                if rows_ref is not None:
                    column = p * stations + j * LANES
                    rows_ref[k * RMAX : (k + 1) * RMAX, column : column + LANES] = piece
        if k % 2:
            for i in range(4 * RMAX // LANES):
                block = paired[i * LANES : (i + 1) * LANES, :]
                turned_ref[k // 2, :, i * LANES : (i + 1) * LANES] = block.T


def prepare(w, after, want_rows):
    count, _, _, stations = w.shape
    outs = [jax.ShapeDtypeStruct((count // 2, stations, 4 * RMAX), BF16)]
    if want_rows:
        outs.append(jax.ShapeDtypeStruct((count * RMAX, 2 * stations), BF16))
    return pl.pallas_call(
        functools.partial(prepare_kernel, want_rows),
        out_shape=outs,
        in_specs=[HBM, ANY],
        out_specs=[VMEM for _ in outs],
        scratch_shapes=[
            pltpu.VMEM((count, RMAX, 2, stations), BF16),
            pltpu.VMEM((stations // LANES, 2 * RMAX, LANES), F32),
            pltpu.VMEM((4 * RMAX, stations), BF16),
            pltpu.SemaphoreType.DMA((count,)),
        ],
        compiler_params=params(),
        cost_estimate=cost(10**9),
        name="prepare",
    )(w, after)


def apply_pairs(bases, blocks, turned_ref):
    virtual = blocks[0].shape[1] // 2
    total = None
    for i, base in enumerate(bases):
        pair = [blocks[2 * i][...], blocks[2 * i + 1][...]]
        turned = [jnp.concatenate([-b[:, virtual:], b[:, :virtual]], axis=1) for b in pair]
        stack = jnp.concatenate(pair + turned, axis=0)
        term = jnp.dot(turned_ref[base // 2], stack, preferred_element_type=F32)
        total = term if total is None else total + term
    return total


def partial_kernel(bases, *refs):
    turned_ref = refs[0]
    out_ref = refs[-1]
    out_ref[...] = apply_pairs(bases, refs[1:-1], turned_ref)


def partial_sum(turned, bases, blocks):
    stations = turned.shape[1]
    width = blocks[0].shape[1]
    return pl.pallas_call(
        functools.partial(partial_kernel, bases),
        out_shape=jax.ShapeDtypeStruct((stations, width), F32),
        in_specs=[VMEM] * (1 + len(blocks)),
        out_specs=VMEM,
        compiler_params=params(),
        cost_estimate=cost(10**9),
        name="partial_sum",
    )(turned, *blocks)


def adjoint_outputs(ks, rank_ref, rows_ref, stacked, outs):
    me = lax.axis_index("tile")
    low = min(ks)
    rows = rows_ref[low * RMAX : (low + len(ks)) * RMAX, :]
    product = jnp.dot(rows, stacked[...], preferred_element_type=F32)
    for i, k in enumerate(ks):
        block = product[(k - low) * RMAX : (k - low + 1) * RMAX, :]
        outs[i][...] = masked(block, rank_ref[me, me ^ k])


def residual_kernel(base, ks, *refs):
    rank_ref, rows_ref, turned_ref, data_ref, partial_ref = refs[:5]
    blocks = refs[5:7]
    outs = refs[7 : 7 + len(ks)]
    stacked = refs[7 + len(ks)]
    stations, virtual = data_ref.shape[1], data_ref.shape[2]
    predicted = partial_ref[...] + apply_pairs((base,), blocks, turned_ref)
    real = (predicted[:, :virtual] - data_ref[0].astype(F32)).astype(BF16)
    imag = (predicted[:, virtual:] - data_ref[1].astype(F32)).astype(BF16)
    stacked[:stations, :virtual] = real
    stacked[:stations, virtual:] = imag
    stacked[stations:, :virtual] = imag
    stacked[stations:, virtual:] = -real
    adjoint_outputs(ks, rank_ref, rows_ref, stacked, outs)


def residual_blocks(ranks, rows, turned, data, partial, base, blocks, ks):
    stations, virtual = data.shape[1], data.shape[2]
    outs = [jax.ShapeDtypeStruct((RMAX, 2 * virtual), BF16) for _ in ks]
    outs.append(jax.ShapeDtypeStruct((2 * stations, 2 * virtual), BF16))
    return pl.pallas_call(
        functools.partial(residual_kernel, base, ks),
        out_shape=outs,
        in_specs=[SMEM] + [VMEM] * 6,
        out_specs=[VMEM for _ in outs],
        compiler_params=params(),
        cost_estimate=cost(10**9),
        name="residual_blocks",
    )(ranks, rows, turned, data, partial, *blocks)


def adjoint_kernel(ks, *refs):
    adjoint_outputs(ks, *refs[:3], refs[3:])


def adjoint_blocks(ranks, rows, stacked, ks):
    width = stacked.shape[1]
    return pl.pallas_call(
        functools.partial(adjoint_kernel, ks),
        out_shape=[jax.ShapeDtypeStruct((RMAX, width), BF16) for _ in ks],
        in_specs=[SMEM, VMEM, VMEM],
        out_specs=[VMEM for _ in ks],
        compiler_params=params(),
        cost_estimate=cost(10**9),
        name="adjoint_blocks",
    )(ranks, rows, stacked)


def spectrum_kernel(base, freqs, *refs):
    turned_ref, partial_ref = refs[:2]
    outs = refs[4 : 4 + freqs]
    spectrum = refs[4 + freqs]
    mine = lax.axis_index("freq")
    spectrum[...] = partial_ref[...] + apply_pairs((base,), refs[2:4], turned_ref)
    share = outs[0].shape[0]
    for k in range(freqs):
        rows = pl.ds(pl.multiple_of((mine ^ k) * share, 8), share)
        outs[k][...] = spectrum[rows, :].astype(BF16)


def spectrum_blocks(turned, partial, base, blocks, freqs):
    stations, width = partial.shape
    return pl.pallas_call(
        functools.partial(spectrum_kernel, base, freqs),
        out_shape=[jax.ShapeDtypeStruct((stations // freqs, width), BF16) for _ in range(freqs)],
        in_specs=[VMEM] * 4,
        out_specs=[VMEM] * freqs,
        scratch_shapes=[pltpu.VMEM((stations, width), F32)],
        compiler_params=params(),
        cost_estimate=cost(10**9),
        name="spectrum_blocks",
    )(turned, partial, *blocks)


def traces_kernel(freqs, *refs):
    onset_ref = refs[0]
    blocks = refs[1 : 1 + freqs]
    out_hbm, gathered, traces, sems = refs[1 + freqs :]
    mine = lax.axis_index("freq")
    virtual = onset_ref.shape[1]
    for k in range(freqs):
        gathered[mine ^ k] = blocks[k][...]
    times = 2 * freqs
    scaling = 1.0 / math.sqrt(freqs)
    copies = [
        pltpu.make_async_copy(traces.at[t], out_hbm.at[t], sems.at[t]) for t in range(times)
    ]
    onset = onset_ref[...]
    for t in range(freqs):
        sums = [None, None]
        for f in range(freqs):
            turn = (f + 1) * t % times
            angle = 2.0 * math.pi * turn / times
            quarter = 4 * turn % times == 0
            for part, weight in ((0, math.cos(angle)), (1, -math.sin(angle))):
                if quarter:
                    weight = float(round(weight))
                if weight != 0.0:
                    value = gathered[f, :, part * virtual : (part + 1) * virtual]
                    term = value.astype(F32) * (weight * scaling)
                    old = sums[f % 2]
                    sums[f % 2] = term if old is None else old + term
        odd, even = sums
        traces[t] = jnp.where(t >= onset, even + odd, 0.0)
        copies[t].start()
        traces[t + freqs] = jnp.where(t + freqs >= onset, even - odd, 0.0)
        copies[t + freqs].start()
    for copy in copies:
        copy.wait()


def gated_traces(onset, blocks):
    freqs = len(blocks)
    share, virtual = onset.shape
    return pl.pallas_call(
        functools.partial(traces_kernel, freqs),
        out_shape=jax.ShapeDtypeStruct((2 * freqs, share, virtual), F32),
        in_specs=[VMEM] * (1 + freqs),
        out_specs=HBM,
        scratch_shapes=[
            pltpu.VMEM((freqs, share, 2 * virtual), BF16),
            pltpu.VMEM((2 * freqs, share, virtual), F32),
            pltpu.SemaphoreType.DMA((2 * freqs,)),
        ],
        compiler_params=params(),
        name="gated_traces",
    )(onset, *blocks)


def send(block, axis, k):
    count = lax.axis_size(axis)
    return lax.ppermute(block, axis, [(i, i ^ k) for i in range(count)])


def exchange(ks, blocks):
    return {k: send(b, "tile", k) if k else b for k, b in zip(ks, blocks)}


def pick(arrived, bases):
    return [arrived[base + b] for base in bases for b in range(2)]


def pair_bases(count):
    return list(range(count - 2, -1, -2))


def peer_order(count):
    bases = pair_bases(count)
    half = len(bases) // 2
    far = tuple(base + b for base in bases[:half] for b in range(2))
    near = tuple(base + b for base in bases[half:] for b in range(2))
    return far, near


def hbm(array):
    return pltpu.with_memory_space_constraint(array, pltpu.MemorySpace.HBM)


def body(x_field, data, u_bases, v_bases, ranks, onset):
    count = lax.axis_size("tile")
    freqs = lax.axis_size("freq")
    table = ranks[0]
    u = hbm(u_bases[0, 0])
    v = hbm(v_bases[0, :, 0])
    x = hbm(x_field[0])
    late = count // 2
    early = tuple(base for base in pair_bases(count) if base != late)
    far, near = peer_order(count)
    *blocks, wide, near_factors = coeff_far(hbm(table), v, x, far, near)
    arrived = exchange(far, blocks)
    blocks = coeff_near(table, wide, near_factors, near)
    arrived |= exchange(near, blocks)
    u_turned, u_rows = prepare(u, blocks[0], True)
    partial = partial_sum(u_turned, early, pick(arrived, early))
    *blocks, stacked = residual_blocks(
        table, u_rows, u_turned, data[0], partial, late, pick(arrived, (late,)), far
    )
    returned = exchange(far, blocks)
    blocks = adjoint_blocks(table, u_rows, stacked, near)
    returned |= exchange(near, blocks)
    (v_turned,) = prepare(v, stacked, False)
    partial = partial_sum(v_turned, early, pick(returned, early))
    spectrum = spectrum_blocks(v_turned, partial, late, pick(returned, (late,)), freqs)
    spectra = [send(block, "freq", k) if k else block for k, block in enumerate(spectrum)]
    return gated_traces(onset, spectra)


def solution(mesh):
    in_specs = (
        P("freq", None, "tile", None),
        P("freq", None, "tile", None),
        P("freq", "tile", None, None, None, None),
        P("freq", None, "tile", None, None, None),
        P("freq", None, None),
        P(("tile", "freq"), None),
    )
    out_specs = P(None, ("tile", "freq"), None)

    return jax.shard_map(
        body, mesh=mesh, in_specs=in_specs, out_specs=out_specs, check_vma=False
    )
```

```python
import functools
import math

import jax
import jax.numpy as jnp
from jax import lax
from jax.experimental import pallas as pl
from jax.experimental.pallas import tpu as pltpu
from jax.sharding import PartitionSpec as P


RMAX = 96
LANES = 128
BF16 = jnp.bfloat16
F32 = jnp.float32
VMEM = pl.BlockSpec(memory_space=pltpu.VMEM)
SMEM = pl.BlockSpec(memory_space=pltpu.SMEM)
ANY = pl.BlockSpec(memory_space=pl.ANY)
HBM = pl.BlockSpec(memory_space=pltpu.MemorySpace.HBM)


def params():
    return pltpu.CompilerParams(vmem_limit_bytes=20 * 1024 * 1024)


def level_mask(rank):
    level = lax.broadcasted_iota(jnp.int32, (RMAX, LANES), 0)
    return (level < rank).astype(F32)


def masked(value, mask):
    copies = value.shape[1] // LANES
    return (value * jnp.concatenate([mask] * copies, axis=1)).astype(BF16)


def cost(flops):
    return pl.CostEstimate(flops=flops, bytes_accessed=10**7, transcendentals=0)


def coeff_outputs(ks, masks, factors, wide, product, outs):
    stations = factors.shape[3]
    left = factors[...].reshape(len(ks) * 2 * RMAX, stations)
    result = jnp.dot(left, wide[...], preferred_element_type=F32)
    parts = wide.shape[1] // LANES
    half = parts // 2
    for j in range(parts):
        product[j] = result[:, j * LANES : (j + 1) * LANES]
    for i, k in enumerate(ks):
        mask = masks[i]
        base = i * 2 * RMAX
        even = [product[j, pl.ds(base, RMAX, stride=2), :] for j in range(parts)]
        odd = [product[j, pl.ds(base + 1, RMAX, stride=2), :] for j in range(parts)]
        for j in range(half):
            real = masked(even[j] + odd[half + j], mask)
            imag = masked(even[half + j] - odd[j], mask)
            outs[i][:, j * LANES : (j + 1) * LANES] = real
            outs[i][:, (half + j) * LANES : (half + j + 1) * LANES] = imag


def coeff_first_kernel(first, rest, *refs):
    rank_hbm, v_hbm, x_hbm = refs[:3]
    outs = refs[3 : 3 + len(first)]
    wide, rest_factors, rest_masks = refs[3 + len(first) : 6 + len(first)]
    rank_ref, factors, field, product, sems, rest_sems, field_sem, rank_sem = refs[
        6 + len(first) :
    ]
    me = lax.axis_index("tile")
    virtual = field.shape[2]

    def load(k, target, sem):
        return pltpu.make_async_copy(v_hbm.at[me ^ k, pl.ds(0, RMAX)], target, sem)

    rank_copy = pltpu.make_async_copy(rank_hbm, rank_ref, rank_sem)
    field_copy = pltpu.make_async_copy(x_hbm, field, field_sem)
    copies = [load(k, factors.at[i], sems.at[i]) for i, k in enumerate(first)]
    rest_copies = [load(k, rest_factors.at[i], rest_sems.at[i]) for i, k in enumerate(rest)]
    field_copy.start()
    for copy in copies:
        copy.start()
    rank_copy.start()
    for copy in rest_copies:
        copy.start()
    rank_copy.wait()
    for i, k in enumerate(rest):
        rest_masks[i] = level_mask(rank_ref[me ^ k, me])
    field_copy.wait()
    wide[:, :virtual] = field[0]
    wide[:, virtual:] = field[1]
    for copy in copies:
        copy.wait()
    masks = [level_mask(rank_ref[me ^ k, me]) for k in first]
    coeff_outputs(first, masks, factors, wide, product, outs)
    for copy in rest_copies:
        copy.wait()


def coeff_first(ranks, v, x, first, rest):
    stations, virtual = x.shape[1], x.shape[2]
    outs = [jax.ShapeDtypeStruct((RMAX, 2 * virtual), BF16) for _ in first]
    outs.append(jax.ShapeDtypeStruct((stations, 2 * virtual), BF16))
    outs.append(jax.ShapeDtypeStruct((len(rest), RMAX, 2, stations), BF16))
    outs.append(jax.ShapeDtypeStruct((len(rest), RMAX, LANES), F32))
    return pl.pallas_call(
        functools.partial(coeff_first_kernel, first, rest),
        out_shape=outs,
        in_specs=[HBM, HBM, HBM],
        out_specs=[VMEM for _ in outs],
        scratch_shapes=[
            pltpu.SMEM(ranks.shape, jnp.int32),
            pltpu.VMEM((len(first), RMAX, 2, stations), BF16),
            pltpu.VMEM((2, stations, virtual), BF16),
            pltpu.VMEM((2 * virtual // LANES, len(first) * 2 * RMAX, LANES), F32),
            pltpu.SemaphoreType.DMA((len(first),)),
            pltpu.SemaphoreType.DMA((len(rest),)),
            pltpu.SemaphoreType.DMA,
            pltpu.SemaphoreType.DMA,
        ],
        compiler_params=params(),
        cost_estimate=cost(10**9),
        name="coeff_first",
    )(ranks, v, x)


def coeff_rest_kernel(rest, *refs):
    masks, wide, factors = refs[:3]
    outs = refs[3 : 3 + len(rest)]
    coeff_outputs(rest, [masks[i] for i in range(len(rest))], factors, wide, refs[-1], outs)


def coeff_rest(masks, wide, factors, rest):
    width = wide.shape[1]
    return pl.pallas_call(
        functools.partial(coeff_rest_kernel, rest),
        out_shape=[jax.ShapeDtypeStruct((RMAX, width), BF16) for _ in rest],
        in_specs=[VMEM, VMEM, VMEM],
        out_specs=[VMEM for _ in rest],
        scratch_shapes=[pltpu.VMEM((width // LANES, len(rest) * 2 * RMAX, LANES), F32)],
        compiler_params=params(),
        cost_estimate=cost(10**9),
        name="coeff_rest",
    )(masks, wide, factors)


def prepare_kernel(want_rows, *refs):
    w_hbm, rank_ref = refs[:2]
    turned_ref = refs[3]
    if want_rows:
        rows_ref, masks = refs[4:6]
        factors, spread, paired, sems = refs[6:]
    else:
        rows_ref = masks = None
        factors, spread, paired, sems = refs[4:]
    me = lax.axis_index("tile")
    count = factors.shape[0]
    stations = factors.shape[3]
    columns = stations // LANES
    copies = [
        pltpu.make_async_copy(w_hbm.at[me ^ k, pl.ds(0, RMAX)], factors.at[k], sems.at[k])
        for k in range(count)
    ]
    for copy in copies:
        copy.start()
    if masks is not None:
        for k in range(count):
            masks[k] = level_mask(rank_ref[me, me ^ k])
    for k in range(count):
        copies[k].wait()
        flat = factors[k].reshape(2 * RMAX, stations).astype(F32)
        for j in range(columns):
            spread[j] = flat[:, j * LANES : (j + 1) * LANES]
        for p in range(2):
            for j in range(columns):
                piece = spread[j, pl.ds(p, RMAX, stride=2), :].astype(BF16)
                row = (2 * p + k % 2) * RMAX
                paired[row : row + RMAX, j * LANES : (j + 1) * LANES] = piece
                if rows_ref is not None:
                    column = p * stations + j * LANES
                    rows_ref[k * RMAX : (k + 1) * RMAX, column : column + LANES] = piece
        if k % 2:
            for i in range(4 * RMAX // LANES):
                block = paired[i * LANES : (i + 1) * LANES, :]
                turned_ref[k // 2, :, i * LANES : (i + 1) * LANES] = block.T


def prepare(w, ranks, after, want_rows):
    count, _, _, stations = w.shape
    outs = [jax.ShapeDtypeStruct((count // 2, stations, 4 * RMAX), BF16)]
    if want_rows:
        outs.append(jax.ShapeDtypeStruct((count * RMAX, 2 * stations), BF16))
        outs.append(jax.ShapeDtypeStruct((count, RMAX, LANES), F32))
    return pl.pallas_call(
        functools.partial(prepare_kernel, want_rows),
        out_shape=outs,
        in_specs=[HBM, SMEM, ANY],
        out_specs=[VMEM for _ in outs],
        scratch_shapes=[
            pltpu.VMEM((count, RMAX, 2, stations), BF16),
            pltpu.VMEM((stations // LANES, 2 * RMAX, LANES), F32),
            pltpu.VMEM((4 * RMAX, stations), BF16),
            pltpu.SemaphoreType.DMA((count,)),
        ],
        compiler_params=params(),
        cost_estimate=cost(10**9),
        name="prepare",
    )(w, ranks, after)


def apply_pairs(bases, blocks, turned_ref):
    virtual = blocks[0].shape[1] // 2
    total = None
    for i, base in enumerate(bases):
        pair = [blocks[2 * i][...], blocks[2 * i + 1][...]]
        turned = [jnp.concatenate([-b[:, virtual:], b[:, :virtual]], axis=1) for b in pair]
        stack = jnp.concatenate(pair + turned, axis=0)
        term = jnp.dot(turned_ref[base // 2], stack, preferred_element_type=F32)
        total = term if total is None else total + term
    return total


def partial_kernel(bases, *refs):
    turned_ref = refs[0]
    out_ref = refs[-1]
    out_ref[...] = apply_pairs(bases, refs[1:-1], turned_ref)


def partial_sum(turned, bases, blocks):
    stations = turned.shape[1]
    width = blocks[0].shape[1]
    return pl.pallas_call(
        functools.partial(partial_kernel, bases),
        out_shape=jax.ShapeDtypeStruct((stations, width), F32),
        in_specs=[VMEM] * (1 + len(blocks)),
        out_specs=VMEM,
        compiler_params=params(),
        cost_estimate=cost(10**9),
        name="partial_sum",
    )(turned, *blocks)


def adjoint_outputs(ks, masks, rows_ref, stacked, outs):
    low = min(ks)
    rows = rows_ref[low * RMAX : (low + len(ks)) * RMAX, :]
    product = jnp.dot(rows, stacked[...], preferred_element_type=F32)
    for i, k in enumerate(ks):
        block = product[(k - low) * RMAX : (k - low + 1) * RMAX, :]
        outs[i][...] = masked(block, masks[k])


def residual_kernel(base, ks, *refs):
    masks, rows_ref, turned_ref, data_ref, partial_ref = refs[:5]
    blocks = refs[5:7]
    outs = refs[7 : 7 + len(ks)]
    stacked = refs[7 + len(ks)]
    stations, virtual = data_ref.shape[1], data_ref.shape[2]
    predicted = partial_ref[...] + apply_pairs((base,), blocks, turned_ref)
    real = (predicted[:, :virtual] - data_ref[0].astype(F32)).astype(BF16)
    imag = (predicted[:, virtual:] - data_ref[1].astype(F32)).astype(BF16)
    stacked[:stations, :virtual] = real
    stacked[:stations, virtual:] = imag
    stacked[stations:, :virtual] = imag
    stacked[stations:, virtual:] = -real
    adjoint_outputs(ks, masks, rows_ref, stacked, outs)


def residual_blocks(masks, rows, turned, data, partial, base, blocks, ks):
    stations, virtual = data.shape[1], data.shape[2]
    outs = [jax.ShapeDtypeStruct((RMAX, 2 * virtual), BF16) for _ in ks]
    outs.append(jax.ShapeDtypeStruct((2 * stations, 2 * virtual), BF16))
    return pl.pallas_call(
        functools.partial(residual_kernel, base, ks),
        out_shape=outs,
        in_specs=[VMEM] * 7,
        out_specs=[VMEM for _ in outs],
        compiler_params=params(),
        cost_estimate=cost(10**9),
        name="residual_blocks",
    )(masks, rows, turned, data, partial, *blocks)


def adjoint_kernel(ks, *refs):
    adjoint_outputs(ks, *refs[:3], refs[3:])


def adjoint_blocks(masks, rows, stacked, ks):
    width = stacked.shape[1]
    return pl.pallas_call(
        functools.partial(adjoint_kernel, ks),
        out_shape=[jax.ShapeDtypeStruct((RMAX, width), BF16) for _ in ks],
        in_specs=[VMEM, VMEM, VMEM],
        out_specs=[VMEM for _ in ks],
        compiler_params=params(),
        cost_estimate=cost(10**9),
        name="adjoint_blocks",
    )(masks, rows, stacked)


def spectrum_kernel(base, freqs, *refs):
    turned_ref, partial_ref = refs[:2]
    outs = refs[4 : 4 + freqs]
    spectrum = refs[4 + freqs]
    mine = lax.axis_index("freq")
    spectrum[...] = partial_ref[...] + apply_pairs((base,), refs[2:4], turned_ref)
    share = outs[0].shape[0]
    for k in range(freqs):
        rows = pl.ds(pl.multiple_of((mine ^ k) * share, 8), share)
        outs[k][...] = spectrum[rows, :].astype(BF16)


def spectrum_blocks(turned, partial, base, blocks, freqs):
    stations, width = partial.shape
    return pl.pallas_call(
        functools.partial(spectrum_kernel, base, freqs),
        out_shape=[jax.ShapeDtypeStruct((stations // freqs, width), BF16) for _ in range(freqs)],
        in_specs=[VMEM] * 4,
        out_specs=[VMEM] * freqs,
        scratch_shapes=[pltpu.VMEM((stations, width), F32)],
        compiler_params=params(),
        cost_estimate=cost(10**9),
        name="spectrum_blocks",
    )(turned, partial, *blocks)


def traces_kernel(freqs, *refs):
    onset_ref = refs[0]
    blocks = refs[1 : 1 + freqs]
    out_hbm, gathered, traces, sems = refs[1 + freqs :]
    mine = lax.axis_index("freq")
    virtual = onset_ref.shape[1]
    for k in range(freqs):
        gathered[mine ^ k] = blocks[k][...]
    times = 2 * freqs
    scaling = 1.0 / math.sqrt(freqs)
    copies = [
        pltpu.make_async_copy(traces.at[t], out_hbm.at[t], sems.at[t]) for t in range(times)
    ]
    onset = onset_ref[...]
    for t in range(freqs):
        sums = [None, None]
        for f in range(freqs):
            turn = (f + 1) * t % times
            angle = 2.0 * math.pi * turn / times
            quarter = 4 * turn % times == 0
            for part, weight in ((0, math.cos(angle)), (1, -math.sin(angle))):
                if quarter:
                    weight = float(round(weight))
                if weight != 0.0:
                    value = gathered[f, :, part * virtual : (part + 1) * virtual]
                    term = value.astype(F32) * (weight * scaling)
                    old = sums[f % 2]
                    sums[f % 2] = term if old is None else old + term
        odd, even = sums
        traces[t] = jnp.where(t >= onset, even + odd, 0.0)
        copies[t].start()
        traces[t + freqs] = jnp.where(t + freqs >= onset, even - odd, 0.0)
        copies[t + freqs].start()
    for copy in copies:
        copy.wait()


def gated_traces(onset, blocks):
    freqs = len(blocks)
    share, virtual = onset.shape
    return pl.pallas_call(
        functools.partial(traces_kernel, freqs),
        out_shape=jax.ShapeDtypeStruct((2 * freqs, share, virtual), F32),
        in_specs=[VMEM] * (1 + freqs),
        out_specs=HBM,
        scratch_shapes=[
            pltpu.VMEM((freqs, share, 2 * virtual), BF16),
            pltpu.VMEM((2 * freqs, share, virtual), F32),
            pltpu.SemaphoreType.DMA((2 * freqs,)),
        ],
        compiler_params=params(),
        name="gated_traces",
    )(onset, *blocks)


def send(block, axis, k):
    count = lax.axis_size(axis)
    return lax.ppermute(block, axis, [(i, i ^ k) for i in range(count)])


def exchange(ks, blocks):
    return {k: send(b, "tile", k) if k else b for k, b in zip(ks, blocks)}


def pick(arrived, bases):
    return [arrived[base + b] for base in bases for b in range(2)]


def pair_bases(count):
    return list(range(count - 2, -1, -2))


def peer_order(count):
    far = [base + b for base in pair_bases(count) if base >= count // 2 for b in range(2)]
    near = [base + b for base in pair_bases(count) if 0 < base < count // 2 for b in range(2)]
    return tuple(far[:2]), tuple(near + far[2:] + [1, 0])


def hbm(array):
    return pltpu.with_memory_space_constraint(array, pltpu.MemorySpace.HBM)


def body(x_field, data, u_bases, v_bases, ranks, onset):
    count = lax.axis_size("tile")
    freqs = lax.axis_size("freq")
    table = ranks[0]
    u = hbm(u_bases[0, 0])
    v = hbm(v_bases[0, :, 0])
    x = hbm(x_field[0])
    late = count // 2
    early = tuple(base for base in pair_bases(count) if base != late)
    first, rest = peer_order(count)
    *blocks, wide, rest_factors, rest_masks = coeff_first(hbm(table), v, x, first, rest)
    arrived = exchange(first, blocks)
    blocks = coeff_rest(rest_masks, wide, rest_factors, rest)
    arrived |= exchange(rest, blocks)
    u_turned, u_rows, masks = prepare(u, table, blocks[0], True)
    partial = partial_sum(u_turned, early, pick(arrived, early))
    *blocks, stacked = residual_blocks(
        masks, u_rows, u_turned, data[0], partial, late, pick(arrived, (late,)), first
    )
    returned = exchange(first, blocks)
    blocks = adjoint_blocks(masks, u_rows, stacked, rest)
    returned |= exchange(rest, blocks)
    (v_turned,) = prepare(v, table, stacked, False)
    partial = partial_sum(v_turned, early, pick(returned, early))
    spectrum = spectrum_blocks(v_turned, partial, late, pick(returned, (late,)), freqs)
    spectra = [send(block, "freq", k) if k else block for k, block in enumerate(spectrum)]
    return gated_traces(onset, spectra)


def solution(mesh):
    in_specs = (
        P("freq", None, "tile", None),
        P("freq", None, "tile", None),
        P("freq", "tile", None, None, None, None),
        P("freq", None, "tile", None, None, None),
        P("freq", None, None),
        P(("tile", "freq"), None),
    )
    out_specs = P(None, ("tile", "freq"), None)

    return jax.shard_map(body, mesh=mesh, in_specs=in_specs, out_specs=out_specs, check_vma=False)
```

```python
import functools
import math

import jax
import jax.numpy as jnp
from jax import lax
from jax.experimental import pallas as pl
from jax.experimental.pallas import tpu as pltpu
from jax.sharding import PartitionSpec as P


RMAX = 96
LANES = 128
BF16 = jnp.bfloat16
F32 = jnp.float32
VMEM = pl.BlockSpec(memory_space=pltpu.VMEM)
SMEM = pl.BlockSpec(memory_space=pltpu.SMEM)
ANY = pl.BlockSpec(memory_space=pl.ANY)
HBM = pl.BlockSpec(memory_space=pltpu.MemorySpace.HBM)


def params():
    return pltpu.CompilerParams(vmem_limit_bytes=20 * 1024 * 1024)


def level_mask(rank):
    level = lax.broadcasted_iota(jnp.int32, (RMAX, LANES), 0)
    return (level < rank).astype(F32)


def masked(value, mask):
    copies = value.shape[1] // LANES
    return (value * jnp.concatenate([mask] * copies, axis=1)).astype(BF16)


def cost(flops):
    return pl.CostEstimate(flops=flops, bytes_accessed=10**7, transcendentals=0)


def coeff_outputs(ks, masks, factors, field, product, outs):
    stations = factors.shape[3]
    left = factors[...].reshape(len(ks) * 2 * RMAX, stations)
    half = field.shape[2] // LANES
    parts = 2 * half
    for p in range(2):
        result = jnp.dot(left, field[p], preferred_element_type=F32)
        for j in range(half):
            product[p * half + j] = result[:, j * LANES : (j + 1) * LANES]
    for i, k in enumerate(ks):
        mask = masks[i]
        base = i * 2 * RMAX
        even = [product[j, pl.ds(base, RMAX, stride=2), :] for j in range(parts)]
        odd = [product[j, pl.ds(base + 1, RMAX, stride=2), :] for j in range(parts)]
        for j in range(half):
            real = masked(even[j] + odd[half + j], mask)
            imag = masked(even[half + j] - odd[j], mask)
            outs[i][:, j * LANES : (j + 1) * LANES] = real
            outs[i][:, (half + j) * LANES : (half + j + 1) * LANES] = imag


def coeff_first_kernel(first, rest, *refs):
    rank_hbm, v_hbm, x_hbm = refs[:3]
    outs = refs[3 : 3 + len(first)]
    field, rest_factors, rest_masks = refs[3 + len(first) : 6 + len(first)]
    rank_ref, factors, product, sems, rest_sems, field_sem, rank_sem = refs[6 + len(first) :]
    me = lax.axis_index("tile")

    def load(k, target, sem):
        return pltpu.make_async_copy(v_hbm.at[me ^ k, pl.ds(0, RMAX)], target, sem)

    rank_copy = pltpu.make_async_copy(rank_hbm, rank_ref, rank_sem)
    field_copy = pltpu.make_async_copy(x_hbm, field, field_sem)
    copies = [load(k, factors.at[i], sems.at[i]) for i, k in enumerate(first)]
    rest_copies = [load(k, rest_factors.at[i], rest_sems.at[i]) for i, k in enumerate(rest)]
    field_copy.start()
    for copy in copies:
        copy.start()
    rank_copy.start()
    for copy in rest_copies:
        copy.start()
    rank_copy.wait()
    for i, k in enumerate(rest):
        rest_masks[i] = level_mask(rank_ref[me ^ k, me])
    masks = [level_mask(rank_ref[me ^ k, me]) for k in first]
    field_copy.wait()
    for copy in copies:
        copy.wait()
    coeff_outputs(first, masks, factors, field, product, outs)
    for copy in rest_copies:
        copy.wait()


def coeff_first(ranks, v, x, first, rest):
    stations, virtual = x.shape[1], x.shape[2]
    outs = [jax.ShapeDtypeStruct((RMAX, 2 * virtual), BF16) for _ in first]
    outs.append(jax.ShapeDtypeStruct(x.shape, BF16))
    outs.append(jax.ShapeDtypeStruct((len(rest), RMAX, 2, stations), BF16))
    outs.append(jax.ShapeDtypeStruct((len(rest), RMAX, LANES), F32))
    return pl.pallas_call(
        functools.partial(coeff_first_kernel, first, rest),
        out_shape=outs,
        in_specs=[HBM, HBM, HBM],
        out_specs=[VMEM for _ in outs],
        scratch_shapes=[
            pltpu.SMEM(ranks.shape, jnp.int32),
            pltpu.VMEM((len(first), RMAX, 2, stations), BF16),
            pltpu.VMEM((2 * virtual // LANES, len(first) * 2 * RMAX, LANES), F32),
            pltpu.SemaphoreType.DMA((len(first),)),
            pltpu.SemaphoreType.DMA((len(rest),)),
            pltpu.SemaphoreType.DMA,
            pltpu.SemaphoreType.DMA,
        ],
        compiler_params=params(),
        cost_estimate=cost(10**9),
        name="coeff_first",
    )(ranks, v, x)


def coeff_rest_kernel(rest, *refs):
    masks, field, factors = refs[:3]
    outs = refs[3 : 3 + len(rest)]
    coeff_outputs(rest, [masks[i] for i in range(len(rest))], factors, field, refs[-1], outs)


def coeff_rest(masks, field, factors, rest):
    width = 2 * field.shape[2]
    return pl.pallas_call(
        functools.partial(coeff_rest_kernel, rest),
        out_shape=[jax.ShapeDtypeStruct((RMAX, width), BF16) for _ in rest],
        in_specs=[VMEM, VMEM, VMEM],
        out_specs=[VMEM for _ in rest],
        scratch_shapes=[pltpu.VMEM((width // LANES, len(rest) * 2 * RMAX, LANES), F32)],
        compiler_params=params(),
        cost_estimate=cost(10**9),
        name="coeff_rest",
    )(masks, field, factors)


def prepare_kernel(want_rows, *refs):
    w_hbm, rank_ref = refs[:2]
    turned_ref = refs[3]
    if want_rows:
        rows_ref, masks = refs[4:6]
        factors, spread, paired, sems = refs[6:]
    else:
        rows_ref = masks = None
        factors, spread, paired, sems = refs[4:]
    me = lax.axis_index("tile")
    count = factors.shape[0]
    stations = factors.shape[3]
    columns = stations // LANES
    copies = [
        pltpu.make_async_copy(w_hbm.at[me ^ k, pl.ds(0, RMAX)], factors.at[k], sems.at[k])
        for k in range(count)
    ]
    for copy in copies:
        copy.start()
    if masks is not None:
        for k in range(count):
            masks[k] = level_mask(rank_ref[me, me ^ k])
    for k in range(count):
        copies[k].wait()
        flat = factors[k].reshape(2 * RMAX, stations).astype(F32)
        for j in range(columns):
            spread[j] = flat[:, j * LANES : (j + 1) * LANES]
        for p in range(2):
            for j in range(columns):
                piece = spread[j, pl.ds(p, RMAX, stride=2), :].astype(BF16)
                row = (2 * p + k % 2) * RMAX
                paired[row : row + RMAX, j * LANES : (j + 1) * LANES] = piece
                if rows_ref is not None:
                    column = p * stations + j * LANES
                    rows_ref[k * RMAX : (k + 1) * RMAX, column : column + LANES] = piece
        if k % 2:
            for i in range(4 * RMAX // LANES):
                block = paired[i * LANES : (i + 1) * LANES, :]
                turned_ref[k // 2, :, i * LANES : (i + 1) * LANES] = block.T


def prepare(w, ranks, after, want_rows):
    count, _, _, stations = w.shape
    outs = [jax.ShapeDtypeStruct((count // 2, stations, 4 * RMAX), BF16)]
    if want_rows:
        outs.append(jax.ShapeDtypeStruct((count * RMAX, 2 * stations), BF16))
        outs.append(jax.ShapeDtypeStruct((count, RMAX, LANES), F32))
    return pl.pallas_call(
        functools.partial(prepare_kernel, want_rows),
        out_shape=outs,
        in_specs=[HBM, SMEM, ANY],
        out_specs=[VMEM for _ in outs],
        scratch_shapes=[
            pltpu.VMEM((count, RMAX, 2, stations), BF16),
            pltpu.VMEM((stations // LANES, 2 * RMAX, LANES), F32),
            pltpu.VMEM((4 * RMAX, stations), BF16),
            pltpu.SemaphoreType.DMA((count,)),
        ],
        compiler_params=params(),
        cost_estimate=cost(10**9),
        name="prepare",
    )(w, ranks, after)


def apply_pairs(bases, blocks, turned_ref):
    virtual = blocks[0].shape[1] // 2
    total = None
    for i, base in enumerate(bases):
        pair = [blocks[2 * i][...], blocks[2 * i + 1][...]]
        turned = [jnp.concatenate([-b[:, virtual:], b[:, :virtual]], axis=1) for b in pair]
        stack = jnp.concatenate(pair + turned, axis=0)
        term = jnp.dot(turned_ref[base // 2], stack, preferred_element_type=F32)
        total = term if total is None else total + term
    return total


def partial_kernel(bases, *refs):
    turned_ref = refs[0]
    out_ref = refs[-1]
    out_ref[...] = apply_pairs(bases, refs[1:-1], turned_ref)


def partial_sum(turned, bases, blocks):
    stations = turned.shape[1]
    width = blocks[0].shape[1]
    return pl.pallas_call(
        functools.partial(partial_kernel, bases),
        out_shape=jax.ShapeDtypeStruct((stations, width), F32),
        in_specs=[VMEM] * (1 + len(blocks)),
        out_specs=VMEM,
        compiler_params=params(),
        cost_estimate=cost(10**9),
        name="partial_sum",
    )(turned, *blocks)


def adjoint_outputs(ks, masks, rows_ref, stacked, outs):
    low = min(ks)
    rows = rows_ref[low * RMAX : (low + len(ks)) * RMAX, :]
    product = jnp.dot(rows, stacked[...], preferred_element_type=F32)
    for i, k in enumerate(ks):
        block = product[(k - low) * RMAX : (k - low + 1) * RMAX, :]
        outs[i][...] = masked(block, masks[k])


def residual_kernel(base, ks, *refs):
    masks, rows_ref, turned_ref, data_ref, partial_ref = refs[:5]
    blocks = refs[5:7]
    outs = refs[7 : 7 + len(ks)]
    stacked = refs[7 + len(ks)]
    stations, virtual = data_ref.shape[1], data_ref.shape[2]
    predicted = partial_ref[...] + apply_pairs((base,), blocks, turned_ref)
    real = (predicted[:, :virtual] - data_ref[0].astype(F32)).astype(BF16)
    imag = (predicted[:, virtual:] - data_ref[1].astype(F32)).astype(BF16)
    stacked[:stations, :virtual] = real
    stacked[:stations, virtual:] = imag
    stacked[stations:, :virtual] = imag
    stacked[stations:, virtual:] = -real
    adjoint_outputs(ks, masks, rows_ref, stacked, outs)


def residual_blocks(masks, rows, turned, data, partial, base, blocks, ks):
    stations, virtual = data.shape[1], data.shape[2]
    outs = [jax.ShapeDtypeStruct((RMAX, 2 * virtual), BF16) for _ in ks]
    outs.append(jax.ShapeDtypeStruct((2 * stations, 2 * virtual), BF16))
    return pl.pallas_call(
        functools.partial(residual_kernel, base, ks),
        out_shape=outs,
        in_specs=[VMEM] * 7,
        out_specs=[VMEM for _ in outs],
        compiler_params=params(),
        cost_estimate=cost(10**9),
        name="residual_blocks",
    )(masks, rows, turned, data, partial, *blocks)


def adjoint_kernel(ks, *refs):
    adjoint_outputs(ks, *refs[:3], refs[3:])


def adjoint_blocks(masks, rows, stacked, ks):
    width = stacked.shape[1]
    return pl.pallas_call(
        functools.partial(adjoint_kernel, ks),
        out_shape=[jax.ShapeDtypeStruct((RMAX, width), BF16) for _ in ks],
        in_specs=[VMEM, VMEM, VMEM],
        out_specs=[VMEM for _ in ks],
        compiler_params=params(),
        cost_estimate=cost(10**9),
        name="adjoint_blocks",
    )(masks, rows, stacked)


def spectrum_kernel(base, freqs, chunk, *refs):
    turned_ref, partial_ref = refs[:2]
    pair = refs[2:4]
    outs = refs[4 : 4 + freqs]
    spectrum = refs[4 + freqs]
    mine = lax.axis_index("freq")
    virtual = partial_ref.shape[1] // 2
    real = slice(chunk * LANES, (chunk + 1) * LANES)
    imag = slice(virtual + chunk * LANES, virtual + (chunk + 1) * LANES)
    stack = [jnp.concatenate([b[:, real], b[:, imag]], axis=1) for b in pair]
    stack += [jnp.concatenate([-b[:, imag], b[:, real]], axis=1) for b in pair]
    late = jnp.dot(
        turned_ref[base // 2], jnp.concatenate(stack, axis=0), preferred_element_type=F32
    )
    spectrum[:, :LANES] = partial_ref[:, real] + late[:, :LANES]
    spectrum[:, LANES:] = partial_ref[:, imag] + late[:, LANES:]
    share = outs[0].shape[0]
    for k in range(freqs):
        rows = pl.ds(pl.multiple_of((mine ^ k) * share, 8), share)
        outs[k][...] = spectrum[rows, :].astype(BF16)


def spectrum_blocks(turned, partial, base, blocks, freqs, chunk):
    stations = partial.shape[0]
    return pl.pallas_call(
        functools.partial(spectrum_kernel, base, freqs, chunk),
        out_shape=[
            jax.ShapeDtypeStruct((stations // freqs, 2 * LANES), BF16) for _ in range(freqs)
        ],
        in_specs=[VMEM] * 4,
        out_specs=[VMEM] * freqs,
        scratch_shapes=[pltpu.VMEM((stations, 2 * LANES), F32)],
        compiler_params=params(),
        cost_estimate=cost(5 * 10**8),
        name="spectrum_blocks",
    )(turned, partial, *blocks)


def traces_kernel(freqs, chunk, *refs):
    onset_ref = refs[0]
    blocks = refs[1 : 1 + freqs]
    out_hbm, gathered, traces, sems = refs[-4:]
    mine = lax.axis_index("freq")
    for k in range(freqs):
        gathered[mine ^ k] = blocks[k][...]
    times = 2 * freqs
    scaling = 1.0 / math.sqrt(freqs)
    lanes = pl.ds(chunk * LANES, LANES)
    copies = [
        pltpu.make_async_copy(traces.at[t], out_hbm.at[t, :, lanes], sems.at[t])
        for t in range(times)
    ]
    onset = onset_ref[:, lanes]
    for t in range(freqs):
        sums = [None, None]
        for f in range(freqs):
            turn = (f + 1) * t % times
            angle = 2.0 * math.pi * turn / times
            quarter = 4 * turn % times == 0
            for part, weight in ((0, math.cos(angle)), (1, -math.sin(angle))):
                if quarter:
                    weight = float(round(weight))
                if weight != 0.0:
                    value = gathered[f, :, part * LANES : (part + 1) * LANES]
                    term = value.astype(F32) * (weight * scaling)
                    old = sums[f % 2]
                    sums[f % 2] = term if old is None else old + term
        odd, even = sums
        traces[t] = jnp.where(t >= onset, even + odd, 0.0)
        copies[t].start()
        traces[t + freqs] = jnp.where(t + freqs >= onset, even - odd, 0.0)
        copies[t + freqs].start()
    for copy in copies:
        copy.wait()


def gated_traces(onset, blocks, chunk, before):
    freqs = len(blocks)
    share, virtual = onset.shape
    operands = (onset, *blocks)
    specs = [VMEM] * (1 + freqs)
    aliases = {}
    if before is not None:
        aliases = {len(operands): 0}
        operands += (before,)
        specs.append(HBM)
    return pl.pallas_call(
        functools.partial(traces_kernel, freqs, chunk),
        out_shape=jax.ShapeDtypeStruct((2 * freqs, share, virtual), F32),
        in_specs=specs,
        out_specs=HBM,
        scratch_shapes=[
            pltpu.VMEM((freqs, share, 2 * LANES), BF16),
            pltpu.VMEM((2 * freqs, share, LANES), F32),
            pltpu.SemaphoreType.DMA((2 * freqs,)),
        ],
        input_output_aliases=aliases,
        compiler_params=params(),
        cost_estimate=cost(5 * 10**8),
        name="gated_traces",
    )(*operands)


def send(block, axis, k):
    count = lax.axis_size(axis)
    return lax.ppermute(block, axis, [(i, i ^ k) for i in range(count)])


def exchange(ks, blocks):
    return {k: send(b, "tile", k) if k else b for k, b in zip(ks, blocks)}


def pick(arrived, bases):
    return [arrived[base + b] for base in bases for b in range(2)]


def pair_bases(count):
    return list(range(count - 2, -1, -2))


def peer_order(count):
    far = [base + b for base in pair_bases(count) if base >= count // 2 for b in range(2)]
    near = [base + b for base in pair_bases(count) if 0 < base < count // 2 for b in range(2)]
    return tuple(far[:2]), tuple(far[2:3] + near + far[3:] + [1, 0])


def hbm(array):
    return pltpu.with_memory_space_constraint(array, pltpu.MemorySpace.HBM)


def body(x_field, data, u_bases, v_bases, ranks, onset):
    count = lax.axis_size("tile")
    freqs = lax.axis_size("freq")
    table = ranks[0]
    u = hbm(u_bases[0, 0])
    v = hbm(v_bases[0, :, 0])
    x = hbm(x_field[0])
    late = count // 2
    early = tuple(base for base in pair_bases(count) if base != late)
    first, rest = peer_order(count)
    *blocks, field, rest_factors, rest_masks = coeff_first(hbm(table), v, x, first, rest)
    arrived = exchange(first, blocks)
    blocks = coeff_rest(rest_masks, field, rest_factors, rest)
    arrived |= exchange(rest, blocks)
    u_turned, u_rows, masks = prepare(u, table, blocks[0], True)
    partial = partial_sum(u_turned, early, pick(arrived, early))
    *blocks, stacked = residual_blocks(
        masks, u_rows, u_turned, data[0], partial, late, pick(arrived, (late,)), first
    )
    returned = exchange(first, blocks)
    blocks = adjoint_blocks(masks, u_rows, stacked, rest)
    returned |= exchange(rest, blocks)
    (v_turned,) = prepare(v, table, stacked, False)
    partial = partial_sum(v_turned, early, pick(returned, early))
    spectra = []
    for chunk in range(x.shape[2] // LANES):
        blocks = spectrum_blocks(
            v_turned, partial, late, pick(returned, (late,)), freqs, chunk
        )
        spectra.append([send(b, "freq", k) if k else b for k, b in enumerate(blocks)])
    result = None
    for chunk, blocks in enumerate(spectra):
        result = gated_traces(onset, blocks, chunk, result)
    return result


def solution(mesh):
    in_specs = (
        P("freq", None, "tile", None),
        P("freq", None, "tile", None),
        P("freq", "tile", None, None, None, None),
        P("freq", None, "tile", None, None, None),
        P("freq", None, None),
        P(("tile", "freq"), None),
    )
    out_specs = P(None, ("tile", "freq"), None)

    return jax.shard_map(body, mesh=mesh, in_specs=in_specs, out_specs=out_specs, check_vma=False)
```

```python
import functools
import math

import jax
import jax.numpy as jnp
from jax import lax
from jax.experimental import pallas as pl
from jax.experimental.pallas import tpu as pltpu
from jax.sharding import PartitionSpec as P


RMAX = 96
LANES = 128
BF16 = jnp.bfloat16
F32 = jnp.float32
VMEM = pl.BlockSpec(memory_space=pltpu.VMEM)
SMEM = pl.BlockSpec(memory_space=pltpu.SMEM)
ANY = pl.BlockSpec(memory_space=pl.ANY)
HBM = pl.BlockSpec(memory_space=pltpu.MemorySpace.HBM)


def params():
    return pltpu.CompilerParams(vmem_limit_bytes=20 * 1024 * 1024)


def chip_rounds(chips):
    if chips == 4:
        return [[0, 1, 2, 3], [1, 3, 0, 2], [3, 2, 1, 0], [2, 0, 3, 1]]
    return [[chip ^ turn for chip in range(chips)] for turn in range(chips)]


def targets(count):
    return [
        [2 * dest[tile // 2] + (tile % 2 ^ cross) for tile in range(count)]
        for dest in chip_rounds(count // 2)
        for cross in range(2)
    ]


def sources(count):
    return [[row.index(tile) for tile in range(count)] for row in targets(count)]


def lookup(row, me):
    result = jnp.int32(row[0])
    for tile in range(1, len(row)):
        result = jnp.where(me == tile, row[tile], result)
    return result


def level_mask(rank):
    level = lax.broadcasted_iota(jnp.int32, (RMAX, LANES), 0)
    return (level < rank).astype(F32)


def masked(value, mask):
    copies = value.shape[1] // LANES
    return (value * jnp.concatenate([mask] * copies, axis=1)).astype(BF16)


def cost(flops):
    return pl.CostEstimate(flops=flops, bytes_accessed=10**7, transcendentals=0)


def coeff_outputs(ks, masks, factors, field, product, outs):
    stations = factors.shape[3]
    left = factors[...].reshape(len(ks) * 2 * RMAX, stations)
    half = field.shape[2] // LANES
    parts = 2 * half
    for p in range(2):
        result = jnp.dot(left, field[p], preferred_element_type=F32)
        for j in range(half):
            product[p * half + j] = result[:, j * LANES : (j + 1) * LANES]
    for i, k in enumerate(ks):
        mask = masks[i]
        base = i * 2 * RMAX
        even = [product[j, pl.ds(base, RMAX, stride=2), :] for j in range(parts)]
        odd = [product[j, pl.ds(base + 1, RMAX, stride=2), :] for j in range(parts)]
        for j in range(half):
            real = masked(even[j] + odd[half + j], mask)
            imag = masked(even[half + j] - odd[j], mask)
            outs[i][:, j * LANES : (j + 1) * LANES] = real
            outs[i][:, (half + j) * LANES : (half + j + 1) * LANES] = imag


def coeff_first_kernel(first, rest, *refs):
    rank_hbm, v_hbm, x_hbm = refs[:3]
    outs = refs[3 : 3 + len(first)]
    field, rest_factors, rest_masks = refs[3 + len(first) : 6 + len(first)]
    rank_ref, factors, product, sems, rest_sems, field_sem, rank_sem = refs[6 + len(first) :]
    me = lax.axis_index("tile")

    def load(k, target, sem):
        return pltpu.make_async_copy(v_hbm.at[tiles[k], pl.ds(0, RMAX)], target, sem)

    tiles = [lookup(row, me) for row in targets(len(first) + len(rest))]
    rank_copy = pltpu.make_async_copy(rank_hbm, rank_ref, rank_sem)
    field_copy = pltpu.make_async_copy(x_hbm, field, field_sem)
    copies = [load(k, factors.at[i], sems.at[i]) for i, k in enumerate(first)]
    rest_copies = [load(k, rest_factors.at[i], rest_sems.at[i]) for i, k in enumerate(rest)]
    field_copy.start()
    for copy in copies:
        copy.start()
    rank_copy.start()
    for copy in rest_copies:
        copy.start()
    rank_copy.wait()
    for i, k in enumerate(rest):
        rest_masks[i] = level_mask(rank_ref[tiles[k], me])
    masks = [level_mask(rank_ref[tiles[k], me]) for k in first]
    field_copy.wait()
    for copy in copies:
        copy.wait()
    coeff_outputs(first, masks, factors, field, product, outs)
    for copy in rest_copies:
        copy.wait()


def coeff_first(ranks, v, x, first, rest):
    stations, virtual = x.shape[1], x.shape[2]
    outs = [jax.ShapeDtypeStruct((RMAX, 2 * virtual), BF16) for _ in first]
    outs.append(jax.ShapeDtypeStruct(x.shape, BF16))
    outs.append(jax.ShapeDtypeStruct((len(rest), RMAX, 2, stations), BF16))
    outs.append(jax.ShapeDtypeStruct((len(rest), RMAX, LANES), F32))
    return pl.pallas_call(
        functools.partial(coeff_first_kernel, first, rest),
        out_shape=outs,
        in_specs=[HBM, HBM, HBM],
        out_specs=[VMEM for _ in outs],
        scratch_shapes=[
            pltpu.SMEM(ranks.shape, jnp.int32),
            pltpu.VMEM((len(first), RMAX, 2, stations), BF16),
            pltpu.VMEM((2 * virtual // LANES, len(first) * 2 * RMAX, LANES), F32),
            pltpu.SemaphoreType.DMA((len(first),)),
            pltpu.SemaphoreType.DMA((len(rest),)),
            pltpu.SemaphoreType.DMA,
            pltpu.SemaphoreType.DMA,
        ],
        compiler_params=params(),
        cost_estimate=cost(10**9),
        name="coeff_first",
    )(ranks, v, x)


def coeff_rest_kernel(rest, *refs):
    masks, field, factors = refs[:3]
    outs = refs[3 : 3 + len(rest)]
    coeff_outputs(rest, [masks[i] for i in range(len(rest))], factors, field, refs[-1], outs)


def coeff_rest(masks, field, factors, rest):
    width = 2 * field.shape[2]
    return pl.pallas_call(
        functools.partial(coeff_rest_kernel, rest),
        out_shape=[jax.ShapeDtypeStruct((RMAX, width), BF16) for _ in rest],
        in_specs=[VMEM, VMEM, VMEM],
        out_specs=[VMEM for _ in rest],
        scratch_shapes=[pltpu.VMEM((width // LANES, len(rest) * 2 * RMAX, LANES), F32)],
        compiler_params=params(),
        cost_estimate=cost(10**9),
        name="coeff_rest",
    )(masks, field, factors)


def prepare_kernel(want_rows, *refs):
    w_hbm, rank_ref = refs[:2]
    turned_ref = refs[3]
    if want_rows:
        rows_ref, masks = refs[4:6]
        factors, spread, paired, sems = refs[6:]
    else:
        rows_ref = masks = None
        factors, spread, paired, sems = refs[4:]
    me = lax.axis_index("tile")
    count = factors.shape[0]
    stations = factors.shape[3]
    columns = stations // LANES
    slots = sources(count) if want_rows else targets(count)
    tiles = [lookup(row, me) for row in slots]
    copies = [
        pltpu.make_async_copy(w_hbm.at[tiles[k], pl.ds(0, RMAX)], factors.at[k], sems.at[k])
        for k in range(count)
    ]
    for copy in copies:
        copy.start()
    if masks is not None:
        for k in range(count):
            masks[k] = level_mask(rank_ref[me, tiles[k]])
    for k in range(count):
        copies[k].wait()
        flat = factors[k].reshape(2 * RMAX, stations).astype(F32)
        for j in range(columns):
            spread[j] = flat[:, j * LANES : (j + 1) * LANES]
        for p in range(2):
            for j in range(columns):
                piece = spread[j, pl.ds(p, RMAX, stride=2), :].astype(BF16)
                row = (2 * p + k % 2) * RMAX
                paired[row : row + RMAX, j * LANES : (j + 1) * LANES] = piece
                if rows_ref is not None:
                    column = p * stations + j * LANES
                    rows_ref[k * RMAX : (k + 1) * RMAX, column : column + LANES] = piece
        if k % 2:
            for i in range(4 * RMAX // LANES):
                block = paired[i * LANES : (i + 1) * LANES, :]
                turned_ref[k // 2, :, i * LANES : (i + 1) * LANES] = block.T


def prepare(w, ranks, after, want_rows):
    count, _, _, stations = w.shape
    outs = [jax.ShapeDtypeStruct((count // 2, stations, 4 * RMAX), BF16)]
    if want_rows:
        outs.append(jax.ShapeDtypeStruct((count * RMAX, 2 * stations), BF16))
        outs.append(jax.ShapeDtypeStruct((count, RMAX, LANES), F32))
    return pl.pallas_call(
        functools.partial(prepare_kernel, want_rows),
        out_shape=outs,
        in_specs=[HBM, SMEM, ANY],
        out_specs=[VMEM for _ in outs],
        scratch_shapes=[
            pltpu.VMEM((count, RMAX, 2, stations), BF16),
            pltpu.VMEM((stations // LANES, 2 * RMAX, LANES), F32),
            pltpu.VMEM((4 * RMAX, stations), BF16),
            pltpu.SemaphoreType.DMA((count,)),
        ],
        compiler_params=params(),
        cost_estimate=cost(10**9),
        name="prepare",
    )(w, ranks, after)


def apply_pairs(bases, blocks, turned_ref):
    virtual = blocks[0].shape[1] // 2
    total = None
    for i, base in enumerate(bases):
        pair = [blocks[2 * i][...], blocks[2 * i + 1][...]]
        turned = [jnp.concatenate([-b[:, virtual:], b[:, :virtual]], axis=1) for b in pair]
        stack = jnp.concatenate(pair + turned, axis=0)
        term = jnp.dot(turned_ref[base // 2], stack, preferred_element_type=F32)
        total = term if total is None else total + term
    return total


def partial_kernel(bases, *refs):
    turned_ref = refs[0]
    out_ref = refs[-1]
    out_ref[...] = apply_pairs(bases, refs[1:-1], turned_ref)


def partial_sum(turned, bases, blocks):
    stations = turned.shape[1]
    width = blocks[0].shape[1]
    return pl.pallas_call(
        functools.partial(partial_kernel, bases),
        out_shape=jax.ShapeDtypeStruct((stations, width), F32),
        in_specs=[VMEM] * (1 + len(blocks)),
        out_specs=VMEM,
        compiler_params=params(),
        cost_estimate=cost(10**9),
        name="partial_sum",
    )(turned, *blocks)


def adjoint_outputs(ks, masks, rows_ref, stacked, outs):
    low = min(ks)
    rows = rows_ref[low * RMAX : (low + len(ks)) * RMAX, :]
    product = jnp.dot(rows, stacked[...], preferred_element_type=F32)
    for i, k in enumerate(ks):
        block = product[(k - low) * RMAX : (k - low + 1) * RMAX, :]
        outs[i][...] = masked(block, masks[k])


def residual_kernel(base, ks, *refs):
    masks, rows_ref, turned_ref, data_ref, partial_ref = refs[:5]
    blocks = refs[5:7]
    outs = refs[7 : 7 + len(ks)]
    stacked = refs[7 + len(ks)]
    stations, virtual = data_ref.shape[1], data_ref.shape[2]
    predicted = partial_ref[...] + apply_pairs((base,), blocks, turned_ref)
    real = (predicted[:, :virtual] - data_ref[0].astype(F32)).astype(BF16)
    imag = (predicted[:, virtual:] - data_ref[1].astype(F32)).astype(BF16)
    stacked[:stations, :virtual] = real
    stacked[:stations, virtual:] = imag
    stacked[stations:, :virtual] = imag
    stacked[stations:, virtual:] = -real
    adjoint_outputs(ks, masks, rows_ref, stacked, outs)


def residual_blocks(masks, rows, turned, data, partial, base, blocks, ks):
    stations, virtual = data.shape[1], data.shape[2]
    outs = [jax.ShapeDtypeStruct((RMAX, 2 * virtual), BF16) for _ in ks]
    outs.append(jax.ShapeDtypeStruct((2 * stations, 2 * virtual), BF16))
    return pl.pallas_call(
        functools.partial(residual_kernel, base, ks),
        out_shape=outs,
        in_specs=[VMEM] * 7,
        out_specs=[VMEM for _ in outs],
        compiler_params=params(),
        cost_estimate=cost(10**9),
        name="residual_blocks",
    )(masks, rows, turned, data, partial, *blocks)


def adjoint_kernel(ks, *refs):
    adjoint_outputs(ks, *refs[:3], refs[3:])


def adjoint_blocks(masks, rows, stacked, ks):
    width = stacked.shape[1]
    return pl.pallas_call(
        functools.partial(adjoint_kernel, ks),
        out_shape=[jax.ShapeDtypeStruct((RMAX, width), BF16) for _ in ks],
        in_specs=[VMEM, VMEM, VMEM],
        out_specs=[VMEM for _ in ks],
        compiler_params=params(),
        cost_estimate=cost(10**9),
        name="adjoint_blocks",
    )(masks, rows, stacked)


def spectrum_kernel(base, freqs, chunk, *refs):
    turned_ref, partial_ref = refs[:2]
    pair = refs[2:4]
    outs = refs[4 : 4 + freqs]
    spectrum = refs[4 + freqs]
    mine = lax.axis_index("freq")
    virtual = partial_ref.shape[1] // 2
    real = slice(chunk * LANES, (chunk + 1) * LANES)
    imag = slice(virtual + chunk * LANES, virtual + (chunk + 1) * LANES)
    stack = [jnp.concatenate([b[:, real], b[:, imag]], axis=1) for b in pair]
    stack += [jnp.concatenate([-b[:, imag], b[:, real]], axis=1) for b in pair]
    late = jnp.dot(
        turned_ref[base // 2], jnp.concatenate(stack, axis=0), preferred_element_type=F32
    )
    spectrum[:, :LANES] = partial_ref[:, real] + late[:, :LANES]
    spectrum[:, LANES:] = partial_ref[:, imag] + late[:, LANES:]
    share = outs[0].shape[0]
    for k in range(freqs):
        rows = pl.ds(pl.multiple_of((mine ^ k) * share, 8), share)
        outs[k][...] = spectrum[rows, :].astype(BF16)


def spectrum_blocks(turned, partial, base, blocks, freqs, chunk):
    stations = partial.shape[0]
    return pl.pallas_call(
        functools.partial(spectrum_kernel, base, freqs, chunk),
        out_shape=[
            jax.ShapeDtypeStruct((stations // freqs, 2 * LANES), BF16) for _ in range(freqs)
        ],
        in_specs=[VMEM] * 4,
        out_specs=[VMEM] * freqs,
        scratch_shapes=[pltpu.VMEM((stations, 2 * LANES), F32)],
        compiler_params=params(),
        cost_estimate=cost(5 * 10**8),
        name="spectrum_blocks",
    )(turned, partial, *blocks)


def traces_kernel(freqs, chunk, *refs):
    onset_ref = refs[0]
    blocks = refs[1 : 1 + freqs]
    out_hbm, gathered, traces, sems = refs[-4:]
    mine = lax.axis_index("freq")
    for k in range(freqs):
        gathered[mine ^ k] = blocks[k][...]
    times = 2 * freqs
    scaling = 1.0 / math.sqrt(freqs)
    lanes = pl.ds(chunk * LANES, LANES)
    copies = [
        pltpu.make_async_copy(traces.at[t], out_hbm.at[t, :, lanes], sems.at[t])
        for t in range(times)
    ]
    onset = onset_ref[:, lanes]
    for t in range(freqs):
        sums = [None, None]
        for f in range(freqs):
            turn = (f + 1) * t % times
            angle = 2.0 * math.pi * turn / times
            quarter = 4 * turn % times == 0
            for part, weight in ((0, math.cos(angle)), (1, -math.sin(angle))):
                if quarter:
                    weight = float(round(weight))
                if weight != 0.0:
                    value = gathered[f, :, part * LANES : (part + 1) * LANES]
                    term = value.astype(F32) * (weight * scaling)
                    old = sums[f % 2]
                    sums[f % 2] = term if old is None else old + term
        odd, even = sums
        traces[t] = jnp.where(t >= onset, even + odd, 0.0)
        copies[t].start()
        traces[t + freqs] = jnp.where(t + freqs >= onset, even - odd, 0.0)
        copies[t + freqs].start()
    for copy in copies:
        copy.wait()


def gated_traces(onset, blocks, chunk, before):
    freqs = len(blocks)
    share, virtual = onset.shape
    operands = (onset, *blocks)
    specs = [VMEM] * (1 + freqs)
    aliases = {}
    if before is not None:
        aliases = {len(operands): 0}
        operands += (before,)
        specs.append(HBM)
    return pl.pallas_call(
        functools.partial(traces_kernel, freqs, chunk),
        out_shape=jax.ShapeDtypeStruct((2 * freqs, share, virtual), F32),
        in_specs=specs,
        out_specs=HBM,
        scratch_shapes=[
            pltpu.VMEM((freqs, share, 2 * LANES), BF16),
            pltpu.VMEM((2 * freqs, share, LANES), F32),
            pltpu.SemaphoreType.DMA((2 * freqs,)),
        ],
        input_output_aliases=aliases,
        compiler_params=params(),
        cost_estimate=cost(5 * 10**8),
        name="gated_traces",
    )(*operands)


def send(block, axis, row):
    return lax.ppermute(block, axis, list(enumerate(row)))


def exchange(rows, ks, blocks):
    return {k: send(b, "tile", rows[k]) if k else b for k, b in zip(ks, blocks)}


def pick(arrived, bases):
    return [arrived[base + b] for base in bases for b in range(2)]


def slot_order(bases):
    slots = [base + b for base in bases for b in range(2)]
    return tuple(slots[:2]), tuple(slots[2:] + [1, 0])


def hbm(array):
    return pltpu.with_memory_space_constraint(array, pltpu.MemorySpace.HBM)


def body(x_field, data, u_bases, v_bases, ranks, onset):
    count = lax.axis_size("tile")
    freqs = lax.axis_size("freq")
    table = ranks[0]
    u = hbm(u_bases[0, 0])
    v = hbm(v_bases[0, :, 0])
    x = hbm(x_field[0])
    bases = list(range(2, count, 2))
    first, rest = slot_order(bases)
    *blocks, field, rest_factors, rest_masks = coeff_first(hbm(table), v, x, first, rest)
    arrived = exchange(targets(count), first, blocks)
    blocks = coeff_rest(rest_masks, field, rest_factors, rest)
    arrived |= exchange(targets(count), rest, blocks)
    u_turned, u_rows, masks = prepare(u, table, blocks[0], True)
    late = bases[-1]
    early = (0, *bases[:-1])
    partial = partial_sum(u_turned, early, pick(arrived, early))
    first, rest = slot_order(bases[::-1])
    *blocks, stacked = residual_blocks(
        masks, u_rows, u_turned, data[0], partial, late, pick(arrived, (late,)), first
    )
    returned = exchange(sources(count), first, blocks)
    blocks = adjoint_blocks(masks, u_rows, stacked, rest)
    returned |= exchange(sources(count), rest, blocks)
    (v_turned,) = prepare(v, table, stacked, False)
    late = bases[0]
    early = (0, *bases[1:])
    partial = partial_sum(v_turned, early, pick(returned, early))
    spectra = []
    for chunk in range(x.shape[2] // LANES):
        blocks = spectrum_blocks(
            v_turned, partial, late, pick(returned, (late,)), freqs, chunk
        )
        spectra.append(
            [
                send(b, "freq", [f ^ k for f in range(freqs)]) if k else b
                for k, b in enumerate(blocks)
            ]
        )
    result = None
    for chunk, blocks in enumerate(spectra):
        result = gated_traces(onset, blocks, chunk, result)
    return result


def solution(mesh):
    in_specs = (
        P("freq", None, "tile", None),
        P("freq", None, "tile", None),
        P("freq", "tile", None, None, None, None),
        P("freq", None, "tile", None, None, None),
        P("freq", None, None),
        P(("tile", "freq"), None),
    )
    out_specs = P(None, ("tile", "freq"), None)

    return jax.shard_map(body, mesh=mesh, in_specs=in_specs, out_specs=out_specs, check_vma=False)
```

```python
import functools
import math

import jax
import jax.numpy as jnp
from jax import lax
from jax.experimental import pallas as pl
from jax.experimental.pallas import tpu as pltpu
from jax.sharding import PartitionSpec as P


RMAX = 96
LANES = 128
BF16 = jnp.bfloat16
F32 = jnp.float32
VMEM = pl.BlockSpec(memory_space=pltpu.VMEM)
SMEM = pl.BlockSpec(memory_space=pltpu.SMEM)
ANY = pl.BlockSpec(memory_space=pl.ANY)
HBM = pl.BlockSpec(memory_space=pltpu.MemorySpace.HBM)


def params():
    return pltpu.CompilerParams(vmem_limit_bytes=20 * 1024 * 1024)


def swapped(k, freqs):
    bits = freqs.bit_length() - 1
    if bits % 2:
        return k
    half = bits // 2
    return (k % (1 << half) << half) | (k >> half)


def freq_peer(k, freqs):
    turn = jnp.where(lax.axis_index("tile") % 2 == 0, k, swapped(k, freqs))
    return lax.axis_index("freq") ^ turn


def level_mask(rank):
    level = lax.broadcasted_iota(jnp.int32, (RMAX, LANES), 0)
    return (level < rank).astype(F32)


def masked(value, mask):
    copies = value.shape[1] // LANES
    return (value * jnp.concatenate([mask] * copies, axis=1)).astype(BF16)


def cost(flops):
    return pl.CostEstimate(flops=flops, bytes_accessed=10**7, transcendentals=0)


def coeff_outputs(ks, masks, factors, field, product, outs):
    stations = factors.shape[3]
    left = factors[...].reshape(len(ks) * 2 * RMAX, stations)
    half = field.shape[2] // LANES
    parts = 2 * half
    for p in range(2):
        result = jnp.dot(left, field[p], preferred_element_type=F32)
        for j in range(half):
            product[p * half + j] = result[:, j * LANES : (j + 1) * LANES]
    for i, k in enumerate(ks):
        mask = masks[i]
        base = i * 2 * RMAX
        even = [product[j, pl.ds(base, RMAX, stride=2), :] for j in range(parts)]
        odd = [product[j, pl.ds(base + 1, RMAX, stride=2), :] for j in range(parts)]
        for j in range(half):
            real = masked(even[j] + odd[half + j], mask)
            imag = masked(even[half + j] - odd[j], mask)
            outs[i][:, j * LANES : (j + 1) * LANES] = real
            outs[i][:, (half + j) * LANES : (half + j + 1) * LANES] = imag


def coeff_first_kernel(first, rest, *refs):
    rank_hbm, v_hbm, x_hbm = refs[:3]
    outs = refs[3 : 3 + len(first)]
    field, rest_factors, rest_masks = refs[3 + len(first) : 6 + len(first)]
    rank_ref, factors, product, sems, rest_sems, field_sem, rank_sem = refs[6 + len(first) :]
    me = lax.axis_index("tile")

    def load(k, target, sem):
        return pltpu.make_async_copy(v_hbm.at[me ^ k, pl.ds(0, RMAX)], target, sem)

    rank_copy = pltpu.make_async_copy(rank_hbm, rank_ref, rank_sem)
    field_copy = pltpu.make_async_copy(x_hbm, field, field_sem)
    copies = [load(k, factors.at[i], sems.at[i]) for i, k in enumerate(first)]
    rest_copies = [load(k, rest_factors.at[i], rest_sems.at[i]) for i, k in enumerate(rest)]
    field_copy.start()
    for copy in copies:
        copy.start()
    rank_copy.start()
    for copy in rest_copies:
        copy.start()
    rank_copy.wait()
    for i, k in enumerate(rest):
        rest_masks[i] = level_mask(rank_ref[me ^ k, me])
    masks = [level_mask(rank_ref[me ^ k, me]) for k in first]
    field_copy.wait()
    for copy in copies:
        copy.wait()
    coeff_outputs(first, masks, factors, field, product, outs)
    for copy in rest_copies:
        copy.wait()


def coeff_first(ranks, v, x, first, rest):
    stations, virtual = x.shape[1], x.shape[2]
    outs = [jax.ShapeDtypeStruct((RMAX, 2 * virtual), BF16) for _ in first]
    outs.append(jax.ShapeDtypeStruct(x.shape, BF16))
    outs.append(jax.ShapeDtypeStruct((len(rest), RMAX, 2, stations), BF16))
    outs.append(jax.ShapeDtypeStruct((len(rest), RMAX, LANES), F32))
    return pl.pallas_call(
        functools.partial(coeff_first_kernel, first, rest),
        out_shape=outs,
        in_specs=[HBM, HBM, HBM],
        out_specs=[VMEM for _ in outs],
        scratch_shapes=[
            pltpu.SMEM(ranks.shape, jnp.int32),
            pltpu.VMEM((len(first), RMAX, 2, stations), BF16),
            pltpu.VMEM((2 * virtual // LANES, len(first) * 2 * RMAX, LANES), F32),
            pltpu.SemaphoreType.DMA((len(first),)),
            pltpu.SemaphoreType.DMA((len(rest),)),
            pltpu.SemaphoreType.DMA,
            pltpu.SemaphoreType.DMA,
        ],
        compiler_params=params(),
        cost_estimate=cost(10**9),
        name="coeff_first",
    )(ranks, v, x)


def coeff_rest_kernel(rest, *refs):
    masks, field, factors = refs[:3]
    outs = refs[3 : 3 + len(rest)]
    coeff_outputs(rest, [masks[i] for i in range(len(rest))], factors, field, refs[-1], outs)


def coeff_rest(masks, field, factors, rest):
    width = 2 * field.shape[2]
    return pl.pallas_call(
        functools.partial(coeff_rest_kernel, rest),
        out_shape=[jax.ShapeDtypeStruct((RMAX, width), BF16) for _ in rest],
        in_specs=[VMEM, VMEM, VMEM],
        out_specs=[VMEM for _ in rest],
        scratch_shapes=[pltpu.VMEM((width // LANES, len(rest) * 2 * RMAX, LANES), F32)],
        compiler_params=params(),
        cost_estimate=cost(10**9),
        name="coeff_rest",
    )(masks, field, factors)


def prepare_kernel(want_rows, *refs):
    w_hbm, rank_ref = refs[:2]
    turned_ref = refs[3]
    if want_rows:
        rows_ref, masks = refs[4:6]
        factors, spread, paired, sems = refs[6:]
    else:
        rows_ref = masks = None
        factors, spread, paired, sems = refs[4:]
    me = lax.axis_index("tile")
    count = factors.shape[0]
    stations = factors.shape[3]
    columns = stations // LANES
    copies = [
        pltpu.make_async_copy(w_hbm.at[me ^ k, pl.ds(0, RMAX)], factors.at[k], sems.at[k])
        for k in range(count)
    ]
    for copy in copies:
        copy.start()
    if masks is not None:
        for k in range(count):
            masks[k] = level_mask(rank_ref[me, me ^ k])
    for k in range(count):
        copies[k].wait()
        flat = factors[k].reshape(2 * RMAX, stations).astype(F32)
        for j in range(columns):
            spread[j] = flat[:, j * LANES : (j + 1) * LANES]
        for p in range(2):
            for j in range(columns):
                piece = spread[j, pl.ds(p, RMAX, stride=2), :].astype(BF16)
                row = (2 * p + k % 2) * RMAX
                paired[row : row + RMAX, j * LANES : (j + 1) * LANES] = piece
                if rows_ref is not None:
                    column = p * stations + j * LANES
                    rows_ref[k * RMAX : (k + 1) * RMAX, column : column + LANES] = piece
        if k % 2:
            for i in range(4 * RMAX // LANES):
                block = paired[i * LANES : (i + 1) * LANES, :]
                turned_ref[k // 2, :, i * LANES : (i + 1) * LANES] = block.T


def prepare(w, ranks, after, want_rows):
    count, _, _, stations = w.shape
    outs = [jax.ShapeDtypeStruct((count // 2, stations, 4 * RMAX), BF16)]
    if want_rows:
        outs.append(jax.ShapeDtypeStruct((count * RMAX, 2 * stations), BF16))
        outs.append(jax.ShapeDtypeStruct((count, RMAX, LANES), F32))
    return pl.pallas_call(
        functools.partial(prepare_kernel, want_rows),
        out_shape=outs,
        in_specs=[HBM, SMEM, ANY],
        out_specs=[VMEM for _ in outs],
        scratch_shapes=[
            pltpu.VMEM((count, RMAX, 2, stations), BF16),
            pltpu.VMEM((stations // LANES, 2 * RMAX, LANES), F32),
            pltpu.VMEM((4 * RMAX, stations), BF16),
            pltpu.SemaphoreType.DMA((count,)),
        ],
        compiler_params=params(),
        cost_estimate=cost(10**9),
        name="prepare",
    )(w, ranks, after)


def apply_pairs(bases, blocks, turned_ref):
    virtual = blocks[0].shape[1] // 2
    total = None
    for i, base in enumerate(bases):
        pair = [blocks[2 * i][...], blocks[2 * i + 1][...]]
        turned = [jnp.concatenate([-b[:, virtual:], b[:, :virtual]], axis=1) for b in pair]
        stack = jnp.concatenate(pair + turned, axis=0)
        term = jnp.dot(turned_ref[base // 2], stack, preferred_element_type=F32)
        total = term if total is None else total + term
    return total


def partial_kernel(bases, *refs):
    turned_ref = refs[0]
    out_ref = refs[-1]
    out_ref[...] = apply_pairs(bases, refs[1:-1], turned_ref)


def partial_sum(turned, bases, blocks):
    stations = turned.shape[1]
    width = blocks[0].shape[1]
    return pl.pallas_call(
        functools.partial(partial_kernel, bases),
        out_shape=jax.ShapeDtypeStruct((stations, width), F32),
        in_specs=[VMEM] * (1 + len(blocks)),
        out_specs=VMEM,
        compiler_params=params(),
        cost_estimate=cost(10**9),
        name="partial_sum",
    )(turned, *blocks)


def adjoint_outputs(ks, masks, rows_ref, stacked, outs):
    low = min(ks)
    rows = rows_ref[low * RMAX : (low + len(ks)) * RMAX, :]
    product = jnp.dot(rows, stacked[...], preferred_element_type=F32)
    for i, k in enumerate(ks):
        block = product[(k - low) * RMAX : (k - low + 1) * RMAX, :]
        outs[i][...] = masked(block, masks[k])


def residual_kernel(base, ks, *refs):
    masks, rows_ref, turned_ref, data_ref, partial_ref = refs[:5]
    blocks = refs[5:7]
    outs = refs[7 : 7 + len(ks)]
    stacked = refs[7 + len(ks)]
    stations, virtual = data_ref.shape[1], data_ref.shape[2]
    predicted = partial_ref[...] + apply_pairs((base,), blocks, turned_ref)
    real = (predicted[:, :virtual] - data_ref[0].astype(F32)).astype(BF16)
    imag = (predicted[:, virtual:] - data_ref[1].astype(F32)).astype(BF16)
    stacked[:stations, :virtual] = real
    stacked[:stations, virtual:] = imag
    stacked[stations:, :virtual] = imag
    stacked[stations:, virtual:] = -real
    adjoint_outputs(ks, masks, rows_ref, stacked, outs)


def residual_blocks(masks, rows, turned, data, partial, base, blocks, ks):
    stations, virtual = data.shape[1], data.shape[2]
    outs = [jax.ShapeDtypeStruct((RMAX, 2 * virtual), BF16) for _ in ks]
    outs.append(jax.ShapeDtypeStruct((2 * stations, 2 * virtual), BF16))
    return pl.pallas_call(
        functools.partial(residual_kernel, base, ks),
        out_shape=outs,
        in_specs=[VMEM] * 7,
        out_specs=[VMEM for _ in outs],
        compiler_params=params(),
        cost_estimate=cost(10**9),
        name="residual_blocks",
    )(masks, rows, turned, data, partial, *blocks)


def adjoint_kernel(ks, *refs):
    adjoint_outputs(ks, *refs[:3], refs[3:])


def adjoint_blocks(masks, rows, stacked, ks):
    width = stacked.shape[1]
    return pl.pallas_call(
        functools.partial(adjoint_kernel, ks),
        out_shape=[jax.ShapeDtypeStruct((RMAX, width), BF16) for _ in ks],
        in_specs=[VMEM, VMEM, VMEM],
        out_specs=[VMEM for _ in ks],
        compiler_params=params(),
        cost_estimate=cost(10**9),
        name="adjoint_blocks",
    )(masks, rows, stacked)


def spectrum_kernel(base, freqs, chunk, *refs):
    turned_ref, partial_ref = refs[:2]
    pair = refs[2:4]
    outs = refs[4 : 4 + freqs]
    spectrum = refs[4 + freqs]
    virtual = partial_ref.shape[1] // 2
    real = slice(chunk * LANES, (chunk + 1) * LANES)
    imag = slice(virtual + chunk * LANES, virtual + (chunk + 1) * LANES)
    stack = [jnp.concatenate([b[:, real], b[:, imag]], axis=1) for b in pair]
    stack += [jnp.concatenate([-b[:, imag], b[:, real]], axis=1) for b in pair]
    late = jnp.dot(
        turned_ref[base // 2], jnp.concatenate(stack, axis=0), preferred_element_type=F32
    )
    spectrum[:, :LANES] = partial_ref[:, real] + late[:, :LANES]
    spectrum[:, LANES:] = partial_ref[:, imag] + late[:, LANES:]
    share = outs[0].shape[0]
    for k in range(freqs):
        rows = pl.ds(pl.multiple_of(freq_peer(k, freqs) * share, 8), share)
        outs[k][...] = spectrum[rows, :].astype(BF16)


def spectrum_blocks(turned, partial, base, blocks, freqs, chunk):
    stations = partial.shape[0]
    return pl.pallas_call(
        functools.partial(spectrum_kernel, base, freqs, chunk),
        out_shape=[
            jax.ShapeDtypeStruct((stations // freqs, 2 * LANES), BF16) for _ in range(freqs)
        ],
        in_specs=[VMEM] * 4,
        out_specs=[VMEM] * freqs,
        scratch_shapes=[pltpu.VMEM((stations, 2 * LANES), F32)],
        compiler_params=params(),
        cost_estimate=cost(5 * 10**8),
        name="spectrum_blocks",
    )(turned, partial, *blocks)


def traces_kernel(freqs, chunk, *refs):
    onset_ref = refs[0]
    blocks = refs[1 : 1 + freqs]
    out_hbm, gathered, traces, sems = refs[-4:]
    for k in range(freqs):
        gathered[freq_peer(k, freqs)] = blocks[k][...]
    times = 2 * freqs
    scaling = 1.0 / math.sqrt(freqs)
    lanes = pl.ds(chunk * LANES, LANES)
    copies = [
        pltpu.make_async_copy(traces.at[t], out_hbm.at[t, :, lanes], sems.at[t])
        for t in range(times)
    ]
    onset = onset_ref[:, lanes]
    for t in range(freqs):
        sums = [None, None]
        for f in range(freqs):
            turn = (f + 1) * t % times
            angle = 2.0 * math.pi * turn / times
            quarter = 4 * turn % times == 0
            for part, weight in ((0, math.cos(angle)), (1, -math.sin(angle))):
                if quarter:
                    weight = float(round(weight))
                if weight != 0.0:
                    value = gathered[f, :, part * LANES : (part + 1) * LANES]
                    term = value.astype(F32) * (weight * scaling)
                    old = sums[f % 2]
                    sums[f % 2] = term if old is None else old + term
        odd, even = sums
        traces[t] = jnp.where(t >= onset, even + odd, 0.0)
        copies[t].start()
        traces[t + freqs] = jnp.where(t + freqs >= onset, even - odd, 0.0)
        copies[t + freqs].start()
    for copy in copies:
        copy.wait()


def gated_traces(onset, blocks, chunk, before):
    freqs = len(blocks)
    share, virtual = onset.shape
    operands = (onset, *blocks)
    specs = [VMEM] * (1 + freqs)
    aliases = {}
    if before is not None:
        aliases = {len(operands): 0}
        operands += (before,)
        specs.append(HBM)
    return pl.pallas_call(
        functools.partial(traces_kernel, freqs, chunk),
        out_shape=jax.ShapeDtypeStruct((2 * freqs, share, virtual), F32),
        in_specs=specs,
        out_specs=HBM,
        scratch_shapes=[
            pltpu.VMEM((freqs, share, 2 * LANES), BF16),
            pltpu.VMEM((2 * freqs, share, LANES), F32),
            pltpu.SemaphoreType.DMA((2 * freqs,)),
        ],
        input_output_aliases=aliases,
        compiler_params=params(),
        cost_estimate=cost(5 * 10**8),
        name="gated_traces",
    )(*operands)


def send(block, axis, k):
    count = lax.axis_size(axis)
    return lax.ppermute(block, axis, [(i, i ^ k) for i in range(count)])


def send_freq(block, k):
    count = lax.axis_size("tile")
    freqs = lax.axis_size("freq")
    pairs = [
        (f * count + tile, (f ^ (swapped(k, freqs) if tile % 2 else k)) * count + tile)
        for f in range(freqs)
        for tile in range(count)
    ]
    return lax.ppermute(block, ("freq", "tile"), pairs)


def exchange(ks, blocks):
    return {k: send(b, "tile", k) if k else b for k, b in zip(ks, blocks)}


def pick(arrived, bases):
    return [arrived[base + b] for base in bases for b in range(2)]


def pair_bases(count):
    return list(range(count - 2, -1, -2))


def peer_order(count):
    far = [base + b for base in pair_bases(count) if base >= count // 2 for b in range(2)]
    near = [base + b for base in pair_bases(count) if 0 < base < count // 2 for b in range(2)]
    return tuple(far[:2]), tuple(far[2:3] + near + far[3:] + [1, 0])


def hbm(array):
    return pltpu.with_memory_space_constraint(array, pltpu.MemorySpace.HBM)


def body(x_field, data, u_bases, v_bases, ranks, onset):
    count = lax.axis_size("tile")
    freqs = lax.axis_size("freq")
    table = ranks[0]
    u = hbm(u_bases[0, 0])
    v = hbm(v_bases[0, :, 0])
    x = hbm(x_field[0])
    late = count // 2
    early = tuple(base for base in pair_bases(count) if base != late)
    first, rest = peer_order(count)
    *blocks, field, rest_factors, rest_masks = coeff_first(hbm(table), v, x, first, rest)
    arrived = exchange(first, blocks)
    blocks = coeff_rest(rest_masks, field, rest_factors, rest)
    arrived |= exchange(rest, blocks)
    u_turned, u_rows, masks = prepare(u, table, blocks[0], True)
    partial = partial_sum(u_turned, early, pick(arrived, early))
    *blocks, stacked = residual_blocks(
        masks, u_rows, u_turned, data[0], partial, late, pick(arrived, (late,)), first
    )
    returned = exchange(first, blocks)
    blocks = adjoint_blocks(masks, u_rows, stacked, rest)
    returned |= exchange(rest, blocks)
    (v_turned,) = prepare(v, table, stacked, False)
    partial = partial_sum(v_turned, early, pick(returned, early))
    spectra = []
    for chunk in range(x.shape[2] // LANES):
        blocks = spectrum_blocks(
            v_turned, partial, late, pick(returned, (late,)), freqs, chunk
        )
        spectra.append([send_freq(b, k) if k else b for k, b in enumerate(blocks)])
    result = None
    for chunk, blocks in enumerate(spectra):
        result = gated_traces(onset, blocks, chunk, result)
    return result


def solution(mesh):
    in_specs = (
        P("freq", None, "tile", None),
        P("freq", None, "tile", None),
        P("freq", "tile", None, None, None, None),
        P("freq", None, "tile", None, None, None),
        P("freq", None, None),
        P(("tile", "freq"), None),
    )
    out_specs = P(None, ("tile", "freq"), None)

    return jax.shard_map(body, mesh=mesh, in_specs=in_specs, out_specs=out_specs, check_vma=False)
```

```python
import functools
import math

import jax
import jax.numpy as jnp
from jax import lax
from jax.experimental import pallas as pl
from jax.experimental.pallas import tpu as pltpu
from jax.sharding import PartitionSpec as P


RMAX = 96
LANES = 128
CHUNKS = 1
BF16 = jnp.bfloat16
F32 = jnp.float32
VMEM = pl.BlockSpec(memory_space=pltpu.VMEM)
SMEM = pl.BlockSpec(memory_space=pltpu.SMEM)
ANY = pl.BlockSpec(memory_space=pl.ANY)
HBM = pl.BlockSpec(memory_space=pltpu.MemorySpace.HBM)


def params():
    return pltpu.CompilerParams(vmem_limit_bytes=20 * 1024 * 1024)


def swapped(k, freqs):
    bits = freqs.bit_length() - 1
    if bits % 2:
        return k
    half = bits // 2
    return (k % (1 << half) << half) | (k >> half)


def freq_peer(k, freqs):
    turn = jnp.where(lax.axis_index("tile") % 2 == 0, k, swapped(k, freqs))
    return lax.axis_index("freq") ^ turn


def level_mask(rank):
    level = lax.broadcasted_iota(jnp.int32, (RMAX, LANES), 0)
    return (level < rank).astype(F32)


def masked(value, mask):
    copies = value.shape[1] // LANES
    return (value * jnp.concatenate([mask] * copies, axis=1)).astype(BF16)


def cost(flops):
    return pl.CostEstimate(flops=flops, bytes_accessed=10**7, transcendentals=0)


def coeff_outputs(ks, masks, factors, field, product, outs):
    stations = factors.shape[3]
    left = factors[...].reshape(len(ks) * 2 * RMAX, stations)
    half = field.shape[2] // LANES
    parts = 2 * half
    for p in range(2):
        result = jnp.dot(left, field[p], preferred_element_type=F32)
        for j in range(half):
            product[p * half + j] = result[:, j * LANES : (j + 1) * LANES]
    for i, k in enumerate(ks):
        mask = masks[i]
        base = i * 2 * RMAX
        even = [product[j, pl.ds(base, RMAX, stride=2), :] for j in range(parts)]
        odd = [product[j, pl.ds(base + 1, RMAX, stride=2), :] for j in range(parts)]
        for j in range(half):
            real = masked(even[j] + odd[half + j], mask)
            imag = masked(even[half + j] - odd[j], mask)
            outs[i][:, j * LANES : (j + 1) * LANES] = real
            outs[i][:, (half + j) * LANES : (half + j + 1) * LANES] = imag


def coeff_first_kernel(first, rest, *refs):
    rank_hbm, v_hbm, x_hbm = refs[:3]
    outs = refs[3 : 3 + len(first)]
    field, rest_factors, rest_masks = refs[3 + len(first) : 6 + len(first)]
    rank_ref, factors, product, sems, rest_sems, field_sem, rank_sem = refs[6 + len(first) :]
    me = lax.axis_index("tile")

    def load(k, target, sem):
        return pltpu.make_async_copy(v_hbm.at[me ^ k, pl.ds(0, RMAX)], target, sem)

    rank_copy = pltpu.make_async_copy(rank_hbm, rank_ref, rank_sem)
    field_copy = pltpu.make_async_copy(x_hbm, field, field_sem)
    copies = [load(k, factors.at[i], sems.at[i]) for i, k in enumerate(first)]
    rest_copies = [load(k, rest_factors.at[i], rest_sems.at[i]) for i, k in enumerate(rest)]
    field_copy.start()
    for copy in copies:
        copy.start()
    rank_copy.start()
    for copy in rest_copies:
        copy.start()
    rank_copy.wait()
    for i, k in enumerate(rest):
        rest_masks[i] = level_mask(rank_ref[me ^ k, me])
    masks = [level_mask(rank_ref[me ^ k, me]) for k in first]
    field_copy.wait()
    for copy in copies:
        copy.wait()
    coeff_outputs(first, masks, factors, field, product, outs)
    for copy in rest_copies:
        copy.wait()


def coeff_first(ranks, v, x, first, rest):
    stations, virtual = x.shape[1], x.shape[2]
    outs = [jax.ShapeDtypeStruct((RMAX, 2 * virtual), BF16) for _ in first]
    outs.append(jax.ShapeDtypeStruct(x.shape, BF16))
    outs.append(jax.ShapeDtypeStruct((len(rest), RMAX, 2, stations), BF16))
    outs.append(jax.ShapeDtypeStruct((len(rest), RMAX, LANES), F32))
    return pl.pallas_call(
        functools.partial(coeff_first_kernel, first, rest),
        out_shape=outs,
        in_specs=[HBM, HBM, HBM],
        out_specs=[VMEM for _ in outs],
        scratch_shapes=[
            pltpu.SMEM(ranks.shape, jnp.int32),
            pltpu.VMEM((len(first), RMAX, 2, stations), BF16),
            pltpu.VMEM((2 * virtual // LANES, len(first) * 2 * RMAX, LANES), F32),
            pltpu.SemaphoreType.DMA((len(first),)),
            pltpu.SemaphoreType.DMA((len(rest),)),
            pltpu.SemaphoreType.DMA,
            pltpu.SemaphoreType.DMA,
        ],
        compiler_params=params(),
        cost_estimate=cost(10**9),
        name="coeff_first",
    )(ranks, v, x)


def coeff_rest_kernel(rest, *refs):
    masks, field, factors = refs[:3]
    outs = refs[3 : 3 + len(rest)]
    coeff_outputs(rest, [masks[i] for i in range(len(rest))], factors, field, refs[-1], outs)


def coeff_rest(masks, field, factors, rest):
    width = 2 * field.shape[2]
    return pl.pallas_call(
        functools.partial(coeff_rest_kernel, rest),
        out_shape=[jax.ShapeDtypeStruct((RMAX, width), BF16) for _ in rest],
        in_specs=[VMEM, VMEM, VMEM],
        out_specs=[VMEM for _ in rest],
        scratch_shapes=[pltpu.VMEM((width // LANES, len(rest) * 2 * RMAX, LANES), F32)],
        compiler_params=params(),
        cost_estimate=cost(10**9),
        name="coeff_rest",
    )(masks, field, factors)


def prepare_kernel(want_rows, *refs):
    w_hbm, rank_ref = refs[:2]
    turned_ref = refs[3]
    if want_rows:
        rows_ref, masks = refs[4:6]
        factors, spread, paired, sems = refs[6:]
    else:
        rows_ref = masks = None
        factors, spread, paired, sems = refs[4:]
    me = lax.axis_index("tile")
    count = factors.shape[0]
    stations = factors.shape[3]
    columns = stations // LANES
    copies = [
        pltpu.make_async_copy(w_hbm.at[me ^ k, pl.ds(0, RMAX)], factors.at[k], sems.at[k])
        for k in range(count)
    ]
    for copy in copies:
        copy.start()
    if masks is not None:
        for k in range(count):
            masks[k] = level_mask(rank_ref[me, me ^ k])
    for k in range(count):
        copies[k].wait()
        flat = factors[k].reshape(2 * RMAX, stations).astype(F32)
        for j in range(columns):
            spread[j] = flat[:, j * LANES : (j + 1) * LANES]
        for p in range(2):
            for j in range(columns):
                piece = spread[j, pl.ds(p, RMAX, stride=2), :].astype(BF16)
                row = (2 * p + k % 2) * RMAX
                paired[row : row + RMAX, j * LANES : (j + 1) * LANES] = piece
                if rows_ref is not None:
                    column = p * stations + j * LANES
                    rows_ref[k * RMAX : (k + 1) * RMAX, column : column + LANES] = piece
        if k % 2:
            for i in range(4 * RMAX // LANES):
                block = paired[i * LANES : (i + 1) * LANES, :]
                turned_ref[k // 2, :, i * LANES : (i + 1) * LANES] = block.T


def prepare(w, ranks, after, want_rows):
    count, _, _, stations = w.shape
    outs = [jax.ShapeDtypeStruct((count // 2, stations, 4 * RMAX), BF16)]
    if want_rows:
        outs.append(jax.ShapeDtypeStruct((count * RMAX, 2 * stations), BF16))
        outs.append(jax.ShapeDtypeStruct((count, RMAX, LANES), F32))
    return pl.pallas_call(
        functools.partial(prepare_kernel, want_rows),
        out_shape=outs,
        in_specs=[HBM, SMEM, ANY],
        out_specs=[VMEM for _ in outs],
        scratch_shapes=[
            pltpu.VMEM((count, RMAX, 2, stations), BF16),
            pltpu.VMEM((stations // LANES, 2 * RMAX, LANES), F32),
            pltpu.VMEM((4 * RMAX, stations), BF16),
            pltpu.SemaphoreType.DMA((count,)),
        ],
        compiler_params=params(),
        cost_estimate=cost(10**9),
        name="prepare",
    )(w, ranks, after)


def apply_pairs(bases, blocks, turned_ref):
    virtual = blocks[0].shape[1] // 2
    total = None
    for i, base in enumerate(bases):
        pair = [blocks[2 * i][...], blocks[2 * i + 1][...]]
        turned = [jnp.concatenate([-b[:, virtual:], b[:, :virtual]], axis=1) for b in pair]
        stack = jnp.concatenate(pair + turned, axis=0)
        term = jnp.dot(turned_ref[base // 2], stack, preferred_element_type=F32)
        total = term if total is None else total + term
    return total


def partial_kernel(bases, *refs):
    turned_ref = refs[0]
    out_ref = refs[-1]
    out_ref[...] = apply_pairs(bases, refs[1:-1], turned_ref)


def partial_sum(turned, bases, blocks):
    stations = turned.shape[1]
    width = blocks[0].shape[1]
    return pl.pallas_call(
        functools.partial(partial_kernel, bases),
        out_shape=jax.ShapeDtypeStruct((stations, width), F32),
        in_specs=[VMEM] * (1 + len(blocks)),
        out_specs=VMEM,
        compiler_params=params(),
        cost_estimate=cost(10**9),
        name="partial_sum",
    )(turned, *blocks)


def adjoint_outputs(ks, masks, rows_ref, stacked, outs):
    low = min(ks)
    rows = rows_ref[low * RMAX : (low + len(ks)) * RMAX, :]
    product = jnp.dot(rows, stacked[...], preferred_element_type=F32)
    for i, k in enumerate(ks):
        block = product[(k - low) * RMAX : (k - low + 1) * RMAX, :]
        outs[i][...] = masked(block, masks[k])


def residual_kernel(base, ks, *refs):
    masks, rows_ref, turned_ref, data_ref, partial_ref = refs[:5]
    blocks = refs[5:7]
    outs = refs[7 : 7 + len(ks)]
    stacked = refs[7 + len(ks)]
    stations, virtual = data_ref.shape[1], data_ref.shape[2]
    predicted = partial_ref[...] + apply_pairs((base,), blocks, turned_ref)
    real = (predicted[:, :virtual] - data_ref[0].astype(F32)).astype(BF16)
    imag = (predicted[:, virtual:] - data_ref[1].astype(F32)).astype(BF16)
    stacked[:stations, :virtual] = real
    stacked[:stations, virtual:] = imag
    stacked[stations:, :virtual] = imag
    stacked[stations:, virtual:] = -real
    adjoint_outputs(ks, masks, rows_ref, stacked, outs)


def residual_blocks(masks, rows, turned, data, partial, base, blocks, ks):
    stations, virtual = data.shape[1], data.shape[2]
    outs = [jax.ShapeDtypeStruct((RMAX, 2 * virtual), BF16) for _ in ks]
    outs.append(jax.ShapeDtypeStruct((2 * stations, 2 * virtual), BF16))
    return pl.pallas_call(
        functools.partial(residual_kernel, base, ks),
        out_shape=outs,
        in_specs=[VMEM] * 7,
        out_specs=[VMEM for _ in outs],
        compiler_params=params(),
        cost_estimate=cost(10**9),
        name="residual_blocks",
    )(masks, rows, turned, data, partial, *blocks)


def adjoint_kernel(ks, *refs):
    adjoint_outputs(ks, *refs[:3], refs[3:])


def adjoint_blocks(masks, rows, stacked, ks):
    width = stacked.shape[1]
    return pl.pallas_call(
        functools.partial(adjoint_kernel, ks),
        out_shape=[jax.ShapeDtypeStruct((RMAX, width), BF16) for _ in ks],
        in_specs=[VMEM, VMEM, VMEM],
        out_specs=[VMEM for _ in ks],
        compiler_params=params(),
        cost_estimate=cost(10**9),
        name="adjoint_blocks",
    )(masks, rows, stacked)


def spectrum_kernel(base, freqs, chunk, *refs):
    turned_ref, partial_ref = refs[:2]
    pair = refs[2:4]
    outs = refs[4 : 4 + freqs]
    spectrum = refs[4 + freqs]
    virtual = partial_ref.shape[1] // 2
    width = outs[0].shape[1] // 2
    real = slice(chunk * width, (chunk + 1) * width)
    imag = slice(virtual + chunk * width, virtual + (chunk + 1) * width)
    stack = [jnp.concatenate([b[:, real], b[:, imag]], axis=1) for b in pair]
    stack += [jnp.concatenate([-b[:, imag], b[:, real]], axis=1) for b in pair]
    late = jnp.dot(
        turned_ref[base // 2], jnp.concatenate(stack, axis=0), preferred_element_type=F32
    )
    spectrum[:, :width] = partial_ref[:, real] + late[:, :width]
    spectrum[:, width:] = partial_ref[:, imag] + late[:, width:]
    share = outs[0].shape[0]
    for k in range(freqs):
        rows = pl.ds(pl.multiple_of(freq_peer(k, freqs) * share, 8), share)
        outs[k][...] = spectrum[rows, :].astype(BF16)


def spectrum_blocks(turned, partial, base, blocks, freqs, chunk):
    stations, columns = partial.shape
    columns //= CHUNKS
    return pl.pallas_call(
        functools.partial(spectrum_kernel, base, freqs, chunk),
        out_shape=[
            jax.ShapeDtypeStruct((stations // freqs, columns), BF16) for _ in range(freqs)
        ],
        in_specs=[VMEM] * 4,
        out_specs=[VMEM] * freqs,
        scratch_shapes=[pltpu.VMEM((stations, columns), F32)],
        compiler_params=params(),
        cost_estimate=cost(5 * 10**8),
        name="spectrum_blocks",
    )(turned, partial, *blocks)


def traces_kernel(freqs, chunk, *refs):
    onset_ref = refs[0]
    blocks = refs[1 : 1 + freqs]
    out_hbm, gathered, traces, sems = refs[-4:]
    for k in range(freqs):
        gathered[freq_peer(k, freqs)] = blocks[k][...]
    times = 2 * freqs
    scaling = 1.0 / math.sqrt(freqs)
    width = blocks[0].shape[1] // 2
    lanes = pl.ds(chunk * width, width)
    copies = [
        pltpu.make_async_copy(traces.at[t], out_hbm.at[t, :, lanes], sems.at[t])
        for t in range(times)
    ]
    onset = onset_ref[:, lanes]
    for t in range(freqs):
        sums = [None, None]
        for f in range(freqs):
            turn = (f + 1) * t % times
            angle = 2.0 * math.pi * turn / times
            quarter = 4 * turn % times == 0
            for part, weight in ((0, math.cos(angle)), (1, -math.sin(angle))):
                if quarter:
                    weight = float(round(weight))
                if weight != 0.0:
                    value = gathered[f, :, part * width : (part + 1) * width]
                    term = value.astype(F32) * (weight * scaling)
                    old = sums[f % 2]
                    sums[f % 2] = term if old is None else old + term
        odd, even = sums
        traces[t] = jnp.where(t >= onset, even + odd, 0.0)
        copies[t].start()
        traces[t + freqs] = jnp.where(t + freqs >= onset, even - odd, 0.0)
        copies[t + freqs].start()
    for copy in copies:
        copy.wait()


def gated_traces(onset, blocks, chunk, before):
    freqs = len(blocks)
    share, virtual = onset.shape
    operands = (onset, *blocks)
    specs = [VMEM] * (1 + freqs)
    aliases = {}
    if before is not None:
        aliases = {len(operands): 0}
        operands += (before,)
        specs.append(HBM)
    return pl.pallas_call(
        functools.partial(traces_kernel, freqs, chunk),
        out_shape=jax.ShapeDtypeStruct((2 * freqs, share, virtual), F32),
        in_specs=specs,
        out_specs=HBM,
        scratch_shapes=[
            pltpu.VMEM((freqs, *blocks[0].shape), BF16),
            pltpu.VMEM((2 * freqs, share, blocks[0].shape[1] // 2), F32),
            pltpu.SemaphoreType.DMA((2 * freqs,)),
        ],
        input_output_aliases=aliases,
        compiler_params=params(),
        cost_estimate=cost(5 * 10**8),
        name="gated_traces",
    )(*operands)


def send(block, axis, k):
    count = lax.axis_size(axis)
    return lax.ppermute(block, axis, [(i, i ^ k) for i in range(count)])


def send_freq(block, k):
    count = lax.axis_size("tile")
    freqs = lax.axis_size("freq")
    pairs = [
        (f * count + tile, (f ^ (swapped(k, freqs) if tile % 2 else k)) * count + tile)
        for f in range(freqs)
        for tile in range(count)
    ]
    return lax.ppermute(block, ("freq", "tile"), pairs)


def exchange(ks, blocks):
    return {k: send(b, "tile", k) if k else b for k, b in zip(ks, blocks)}


def pick(arrived, bases):
    return [arrived[base + b] for base in bases for b in range(2)]


def pair_bases(count):
    return list(range(count - 2, -1, -2))


def peer_order(count):
    far = [base + b for base in pair_bases(count) if base >= count // 2 for b in range(2)]
    near = [base + b for base in pair_bases(count) if 0 < base < count // 2 for b in range(2)]
    return tuple(far[:2]), tuple(far[2:3] + near + far[3:] + [1, 0])


def hbm(array):
    return pltpu.with_memory_space_constraint(array, pltpu.MemorySpace.HBM)


def body(x_field, data, u_bases, v_bases, ranks, onset):
    count = lax.axis_size("tile")
    freqs = lax.axis_size("freq")
    table = ranks[0]
    u = hbm(u_bases[0, 0])
    v = hbm(v_bases[0, :, 0])
    x = hbm(x_field[0])
    late = count // 2
    early = tuple(base for base in pair_bases(count) if base != late)
    first, rest = peer_order(count)
    *blocks, field, rest_factors, rest_masks = coeff_first(hbm(table), v, x, first, rest)
    arrived = exchange(first, blocks)
    blocks = coeff_rest(rest_masks, field, rest_factors, rest)
    arrived |= exchange(rest, blocks)
    u_turned, u_rows, masks = prepare(u, table, blocks[0], True)
    partial = partial_sum(u_turned, early, pick(arrived, early))
    *blocks, stacked = residual_blocks(
        masks, u_rows, u_turned, data[0], partial, late, pick(arrived, (late,)), first
    )
    returned = exchange(first, blocks)
    blocks = adjoint_blocks(masks, u_rows, stacked, rest)
    returned |= exchange(rest, blocks)
    (v_turned,) = prepare(v, table, stacked, False)
    partial = partial_sum(v_turned, early, pick(returned, early))
    spectra = []
    for chunk in range(CHUNKS):
        blocks = spectrum_blocks(
            v_turned, partial, late, pick(returned, (late,)), freqs, chunk
        )
        spectra.append([send_freq(b, k) if k else b for k, b in enumerate(blocks)])
    result = None
    for chunk, blocks in enumerate(spectra):
        result = gated_traces(onset, blocks, chunk, result)
    return result


def solution(mesh):
    in_specs = (
        P("freq", None, "tile", None),
        P("freq", None, "tile", None),
        P("freq", "tile", None, None, None, None),
        P("freq", None, "tile", None, None, None),
        P("freq", None, None),
        P(("tile", "freq"), None),
    )
    out_specs = P(None, ("tile", "freq"), None)

    return jax.shard_map(body, mesh=mesh, in_specs=in_specs, out_specs=out_specs, check_vma=False)
```

```python
import functools
import math

import jax
import jax.numpy as jnp
from jax import lax
from jax.experimental import pallas as pl
from jax.experimental.pallas import tpu as pltpu
from jax.sharding import PartitionSpec as P


RMAX = 96
LANES = 128
CHUNKS = 1
BF16 = jnp.bfloat16
F32 = jnp.float32
VMEM = pl.BlockSpec(memory_space=pltpu.VMEM)
SMEM = pl.BlockSpec(memory_space=pltpu.SMEM)
ANY = pl.BlockSpec(memory_space=pl.ANY)
HBM = pl.BlockSpec(memory_space=pltpu.MemorySpace.HBM)


def params():
    return pltpu.CompilerParams(vmem_limit_bytes=20 * 1024 * 1024)


def swapped(k, freqs):
    bits = freqs.bit_length() - 1
    if bits % 2:
        return k
    half = bits // 2
    return (k % (1 << half) << half) | (k >> half)


def freq_peer(k, freqs):
    turn = jnp.where(lax.axis_index("tile") % 2 == 0, k, swapped(k, freqs))
    return lax.axis_index("freq") ^ turn


def level_mask(rank):
    level = lax.broadcasted_iota(jnp.int32, (RMAX, LANES), 0)
    return (level < rank).astype(F32)


def masked(value, mask):
    copies = value.shape[1] // LANES
    return (value * jnp.concatenate([mask] * copies, axis=1)).astype(BF16)


def cost(flops):
    return pl.CostEstimate(flops=flops, bytes_accessed=10**7, transcendentals=0)


def coeff_outputs(ks, masks, factors, field, product, outs):
    stations = factors.shape[3]
    left = factors[...].reshape(len(ks) * 2 * RMAX, stations)
    half = field.shape[2] // LANES
    parts = 2 * half
    for p in range(2):
        result = jnp.dot(left, field[p], preferred_element_type=F32)
        for j in range(half):
            product[p * half + j] = result[:, j * LANES : (j + 1) * LANES]
    for i, k in enumerate(ks):
        mask = masks[i]
        base = i * 2 * RMAX
        even = [product[j, pl.ds(base, RMAX, stride=2), :] for j in range(parts)]
        odd = [product[j, pl.ds(base + 1, RMAX, stride=2), :] for j in range(parts)]
        for j in range(half):
            real = masked(even[j] + odd[half + j], mask)
            imag = masked(even[half + j] - odd[j], mask)
            outs[i][:, j * LANES : (j + 1) * LANES] = real
            outs[i][:, (half + j) * LANES : (half + j + 1) * LANES] = imag


def coeff_first_kernel(first, rest, *refs):
    rank_hbm, v_hbm, x_hbm = refs[:3]
    outs = refs[3 : 3 + len(first)]
    field, rest_factors, rest_masks = refs[3 + len(first) : 6 + len(first)]
    rank_ref, factors, product, sems, rest_sems, field_sem, rank_sem = refs[6 + len(first) :]
    me = lax.axis_index("tile")

    def load(k, target, sem):
        return pltpu.make_async_copy(v_hbm.at[me ^ k, pl.ds(0, RMAX)], target, sem)

    rank_copy = pltpu.make_async_copy(rank_hbm, rank_ref, rank_sem)
    field_copy = pltpu.make_async_copy(x_hbm, field, field_sem)
    copies = [load(k, factors.at[i], sems.at[i]) for i, k in enumerate(first)]
    rest_copies = [load(k, rest_factors.at[i], rest_sems.at[i]) for i, k in enumerate(rest)]
    field_copy.start()
    for copy in copies:
        copy.start()
    rank_copy.start()
    for copy in rest_copies:
        copy.start()
    rank_copy.wait()
    for i, k in enumerate(rest):
        rest_masks[i] = level_mask(rank_ref[me ^ k, me])
    masks = [level_mask(rank_ref[me ^ k, me]) for k in first]
    field_copy.wait()
    for copy in copies:
        copy.wait()
    coeff_outputs(first, masks, factors, field, product, outs)
    for copy in rest_copies:
        copy.wait()


def coeff_first(ranks, v, x, first, rest):
    stations, virtual = x.shape[1], x.shape[2]
    outs = [jax.ShapeDtypeStruct((RMAX, 2 * virtual), BF16) for _ in first]
    outs.append(jax.ShapeDtypeStruct(x.shape, BF16))
    outs.append(jax.ShapeDtypeStruct((len(rest), RMAX, 2, stations), BF16))
    outs.append(jax.ShapeDtypeStruct((len(rest), RMAX, LANES), F32))
    return pl.pallas_call(
        functools.partial(coeff_first_kernel, first, rest),
        out_shape=outs,
        in_specs=[HBM, HBM, HBM],
        out_specs=[VMEM for _ in outs],
        scratch_shapes=[
            pltpu.SMEM(ranks.shape, jnp.int32),
            pltpu.VMEM((len(first), RMAX, 2, stations), BF16),
            pltpu.VMEM((2 * virtual // LANES, len(first) * 2 * RMAX, LANES), F32),
            pltpu.SemaphoreType.DMA((len(first),)),
            pltpu.SemaphoreType.DMA((len(rest),)),
            pltpu.SemaphoreType.DMA,
            pltpu.SemaphoreType.DMA,
        ],
        compiler_params=params(),
        cost_estimate=cost(10**9),
        name="coeff_first",
    )(ranks, v, x)


def coeff_rest_kernel(rest, *refs):
    masks, field, factors = refs[:3]
    outs = refs[3 : 3 + len(rest)]
    coeff_outputs(rest, [masks[i] for i in range(len(rest))], factors, field, refs[-1], outs)


def coeff_rest(masks, field, factors, rest):
    width = 2 * field.shape[2]
    return pl.pallas_call(
        functools.partial(coeff_rest_kernel, rest),
        out_shape=[jax.ShapeDtypeStruct((RMAX, width), BF16) for _ in rest],
        in_specs=[VMEM, VMEM, VMEM],
        out_specs=[VMEM for _ in rest],
        scratch_shapes=[pltpu.VMEM((width // LANES, len(rest) * 2 * RMAX, LANES), F32)],
        compiler_params=params(),
        cost_estimate=cost(10**9),
        name="coeff_rest",
    )(masks, field, factors)


def prepare_kernel(want_rows, *refs):
    w_hbm, rank_ref = refs[:2]
    turned_ref = refs[3]
    if want_rows:
        rows_ref, masks = refs[4:6]
        factors, spread, paired, sems = refs[6:]
    else:
        rows_ref = masks = None
        factors, spread, paired, sems = refs[4:]
    me = lax.axis_index("tile")
    count = factors.shape[0]
    stations = factors.shape[3]
    columns = stations // LANES
    copies = [
        pltpu.make_async_copy(w_hbm.at[me ^ k, pl.ds(0, RMAX)], factors.at[k], sems.at[k])
        for k in range(count)
    ]
    for copy in copies:
        copy.start()
    if masks is not None:
        for k in range(count):
            masks[k] = level_mask(rank_ref[me, me ^ k])
    for k in range(count):
        copies[k].wait()
        flat = factors[k].reshape(2 * RMAX, stations).astype(F32)
        for j in range(columns):
            spread[j] = flat[:, j * LANES : (j + 1) * LANES]
        for p in range(2):
            for j in range(columns):
                piece = spread[j, pl.ds(p, RMAX, stride=2), :].astype(BF16)
                row = (2 * p + k % 2) * RMAX
                paired[row : row + RMAX, j * LANES : (j + 1) * LANES] = piece
                if rows_ref is not None:
                    column = p * stations + j * LANES
                    rows_ref[k * RMAX : (k + 1) * RMAX, column : column + LANES] = piece
        if k % 2:
            for i in range(4 * RMAX // LANES):
                block = paired[i * LANES : (i + 1) * LANES, :]
                turned_ref[k // 2, :, i * LANES : (i + 1) * LANES] = block.T


def prepare(w, ranks, after, want_rows):
    count, _, _, stations = w.shape
    outs = [jax.ShapeDtypeStruct((count // 2, stations, 4 * RMAX), BF16)]
    if want_rows:
        outs.append(jax.ShapeDtypeStruct((count * RMAX, 2 * stations), BF16))
        outs.append(jax.ShapeDtypeStruct((count, RMAX, LANES), F32))
    return pl.pallas_call(
        functools.partial(prepare_kernel, want_rows),
        out_shape=outs,
        in_specs=[HBM, SMEM, ANY],
        out_specs=[VMEM for _ in outs],
        scratch_shapes=[
            pltpu.VMEM((count, RMAX, 2, stations), BF16),
            pltpu.VMEM((stations // LANES, 2 * RMAX, LANES), F32),
            pltpu.VMEM((4 * RMAX, stations), BF16),
            pltpu.SemaphoreType.DMA((count,)),
        ],
        compiler_params=params(),
        cost_estimate=cost(10**9),
        name="prepare",
    )(w, ranks, after)


def apply_pairs(bases, blocks, turned_ref):
    virtual = blocks[0].shape[1] // 2
    total = None
    for i, base in enumerate(bases):
        pair = [blocks[2 * i][...], blocks[2 * i + 1][...]]
        turned = [jnp.concatenate([-b[:, virtual:], b[:, :virtual]], axis=1) for b in pair]
        stack = jnp.concatenate(pair + turned, axis=0)
        term = jnp.dot(turned_ref[base // 2], stack, preferred_element_type=F32)
        total = term if total is None else total + term
    return total


def partial_kernel(bases, *refs):
    turned_ref = refs[0]
    out_ref = refs[-1]
    out_ref[...] = apply_pairs(bases, refs[1:-1], turned_ref)


def partial_sum(turned, bases, blocks):
    stations = turned.shape[1]
    width = blocks[0].shape[1]
    return pl.pallas_call(
        functools.partial(partial_kernel, bases),
        out_shape=jax.ShapeDtypeStruct((stations, width), F32),
        in_specs=[VMEM] * (1 + len(blocks)),
        out_specs=VMEM,
        compiler_params=params(),
        cost_estimate=cost(10**9),
        name="partial_sum",
    )(turned, *blocks)


def adjoint_outputs(ks, masks, rows_ref, stacked, outs):
    low = min(ks)
    rows = rows_ref[low * RMAX : (low + len(ks)) * RMAX, :]
    product = jnp.dot(rows, stacked[...], preferred_element_type=F32)
    for i, k in enumerate(ks):
        block = product[(k - low) * RMAX : (k - low + 1) * RMAX, :]
        outs[i][...] = masked(block, masks[k])


def residual_kernel(base, ks, *refs):
    masks, rows_ref, turned_ref, data_ref, partial_ref = refs[:5]
    blocks = refs[5:7]
    outs = refs[7 : 7 + len(ks)]
    stacked = refs[7 + len(ks)]
    stations, virtual = data_ref.shape[1], data_ref.shape[2]
    predicted = partial_ref[...] + apply_pairs((base,), blocks, turned_ref)
    real = (predicted[:, :virtual] - data_ref[0].astype(F32)).astype(BF16)
    imag = (predicted[:, virtual:] - data_ref[1].astype(F32)).astype(BF16)
    stacked[:stations, :virtual] = real
    stacked[:stations, virtual:] = imag
    stacked[stations:, :virtual] = imag
    stacked[stations:, virtual:] = -real
    adjoint_outputs(ks, masks, rows_ref, stacked, outs)


def residual_blocks(masks, rows, turned, data, partial, base, blocks, ks):
    stations, virtual = data.shape[1], data.shape[2]
    outs = [jax.ShapeDtypeStruct((RMAX, 2 * virtual), BF16) for _ in ks]
    outs.append(jax.ShapeDtypeStruct((2 * stations, 2 * virtual), BF16))
    return pl.pallas_call(
        functools.partial(residual_kernel, base, ks),
        out_shape=outs,
        in_specs=[VMEM] * 7,
        out_specs=[VMEM for _ in outs],
        compiler_params=params(),
        cost_estimate=cost(10**9),
        name="residual_blocks",
    )(masks, rows, turned, data, partial, *blocks)


def adjoint_kernel(ks, *refs):
    adjoint_outputs(ks, *refs[:3], refs[3:])


def adjoint_blocks(masks, rows, stacked, ks):
    width = stacked.shape[1]
    return pl.pallas_call(
        functools.partial(adjoint_kernel, ks),
        out_shape=[jax.ShapeDtypeStruct((RMAX, width), BF16) for _ in ks],
        in_specs=[VMEM, VMEM, VMEM],
        out_specs=[VMEM for _ in ks],
        compiler_params=params(),
        cost_estimate=cost(10**9),
        name="adjoint_blocks",
    )(masks, rows, stacked)


def spectrum_kernel(base, freqs, chunk, *refs):
    turned_ref, partial_ref = refs[:2]
    pair = refs[2:4]
    outs = refs[4 : 4 + freqs]
    spectrum = refs[4 + freqs]
    virtual = partial_ref.shape[1] // 2
    width = outs[0].shape[1] // 2
    real = slice(chunk * width, (chunk + 1) * width)
    imag = slice(virtual + chunk * width, virtual + (chunk + 1) * width)
    stack = [jnp.concatenate([b[:, real], b[:, imag]], axis=1) for b in pair]
    stack += [jnp.concatenate([-b[:, imag], b[:, real]], axis=1) for b in pair]
    late = jnp.dot(
        turned_ref[base // 2], jnp.concatenate(stack, axis=0), preferred_element_type=F32
    )
    spectrum[:, :width] = partial_ref[:, real] + late[:, :width]
    spectrum[:, width:] = partial_ref[:, imag] + late[:, width:]
    share = outs[0].shape[0]
    for k in range(freqs):
        rows = pl.ds(pl.multiple_of(freq_peer(k, freqs) * share, 8), share)
        outs[k][...] = spectrum[rows, :].astype(BF16)


def spectrum_blocks(turned, partial, base, blocks, freqs, chunk):
    stations, columns = partial.shape
    columns //= CHUNKS
    return pl.pallas_call(
        functools.partial(spectrum_kernel, base, freqs, chunk),
        out_shape=[
            jax.ShapeDtypeStruct((stations // freqs, columns), BF16) for _ in range(freqs)
        ],
        in_specs=[VMEM] * 4,
        out_specs=[VMEM] * freqs,
        scratch_shapes=[pltpu.VMEM((stations, columns), F32)],
        compiler_params=params(),
        cost_estimate=cost(5 * 10**8),
        name="spectrum_blocks",
    )(turned, partial, *blocks)


def traces_kernel(freqs, chunk, *refs):
    onset_ref = refs[0]
    blocks = refs[1 : 1 + freqs]
    out_hbm, gathered, traces, sems = refs[-4:]
    for k in range(freqs):
        gathered[freq_peer(k, freqs)] = blocks[k][...]
    times = 2 * freqs
    scaling = 1.0 / math.sqrt(freqs)
    width = blocks[0].shape[1] // 2
    lanes = pl.ds(chunk * width, width)
    copies = [
        pltpu.make_async_copy(traces.at[t], out_hbm.at[t, :, lanes], sems.at[t])
        for t in range(times)
    ]
    onset = onset_ref[:, lanes]
    for t in range(freqs):
        sums = [None, None]
        for f in range(freqs):
            turn = (f + 1) * t % times
            angle = 2.0 * math.pi * turn / times
            quarter = 4 * turn % times == 0
            for part, weight in ((0, math.cos(angle)), (1, -math.sin(angle))):
                if quarter:
                    weight = float(round(weight))
                if weight != 0.0:
                    value = gathered[f, :, part * width : (part + 1) * width]
                    term = value.astype(F32) * (weight * scaling)
                    old = sums[f % 2]
                    sums[f % 2] = term if old is None else old + term
        odd, even = sums
        traces[t] = jnp.where(t >= onset, even + odd, 0.0)
        copies[t].start()
        traces[t + freqs] = jnp.where(t + freqs >= onset, even - odd, 0.0)
        copies[t + freqs].start()
    for copy in copies:
        copy.wait()


def gated_traces(onset, blocks, chunk, before):
    freqs = len(blocks)
    share, virtual = onset.shape
    operands = (onset, *blocks)
    specs = [VMEM] * (1 + freqs)
    aliases = {}
    if before is not None:
        aliases = {len(operands): 0}
        operands += (before,)
        specs.append(HBM)
    return pl.pallas_call(
        functools.partial(traces_kernel, freqs, chunk),
        out_shape=jax.ShapeDtypeStruct((2 * freqs, share, virtual), F32),
        in_specs=specs,
        out_specs=HBM,
        scratch_shapes=[
            pltpu.VMEM((freqs, *blocks[0].shape), BF16),
            pltpu.VMEM((2 * freqs, share, blocks[0].shape[1] // 2), F32),
            pltpu.SemaphoreType.DMA((2 * freqs,)),
        ],
        input_output_aliases=aliases,
        compiler_params=params(),
        cost_estimate=cost(5 * 10**8),
        name="gated_traces",
    )(*operands)


def send(block, axis, k):
    count = lax.axis_size(axis)
    return lax.ppermute(block, axis, [(i, i ^ k) for i in range(count)])


def send_freq(block, k):
    count = lax.axis_size("tile")
    freqs = lax.axis_size("freq")
    pairs = [
        (f * count + tile, (f ^ (swapped(k, freqs) if tile % 2 else k)) * count + tile)
        for f in range(freqs)
        for tile in range(count)
    ]
    return lax.ppermute(block, ("freq", "tile"), pairs)


def exchange(ks, blocks):
    return {k: send(b, "tile", k) if k else b for k, b in zip(ks, blocks)}


def pick(arrived, bases):
    return [arrived[base + b] for base in bases for b in range(2)]


def pair_bases(count):
    return list(range(count - 2, -1, -2))


def peer_order(count):
    far = [base + b for base in pair_bases(count) if base >= count // 2 for b in range(2)]
    near = [base + b for base in pair_bases(count) if 0 < base < count // 2 for b in range(2)]
    return tuple(far[:2]), tuple(far[2:3] + near + far[3:] + [1, 0])


def hbm(array):
    return pltpu.with_memory_space_constraint(array, pltpu.MemorySpace.HBM)


def body(x_field, data, u_bases, v_bases, ranks, onset):
    count = lax.axis_size("tile")
    freqs = lax.axis_size("freq")
    table = ranks[0]
    u = hbm(u_bases[0, 0])
    v = hbm(v_bases[0, :, 0])
    x = hbm(x_field[0])
    late = count // 2
    early = tuple(base for base in pair_bases(count) if base != late)
    first, rest = peer_order(count)
    alone, others = first[:1], first[1:] + rest
    *blocks, field, rest_factors, rest_masks = coeff_first(hbm(table), v, x, alone, others)
    arrived = exchange(alone, blocks)
    blocks = coeff_rest(rest_masks, field, rest_factors, others)
    arrived |= exchange(others, blocks)
    u_turned, u_rows, masks = prepare(u, table, blocks[0], True)
    partial = partial_sum(u_turned, early, pick(arrived, early))
    *blocks, stacked = residual_blocks(
        masks, u_rows, u_turned, data[0], partial, late, pick(arrived, (late,)), first
    )
    returned = exchange(first, blocks)
    blocks = adjoint_blocks(masks, u_rows, stacked, rest)
    returned |= exchange(rest, blocks)
    (v_turned,) = prepare(v, table, stacked, False)
    partial = partial_sum(v_turned, early, pick(returned, early))
    spectra = []
    for chunk in range(CHUNKS):
        blocks = spectrum_blocks(
            v_turned, partial, late, pick(returned, (late,)), freqs, chunk
        )
        spectra.append([send_freq(b, k) if k else b for k, b in enumerate(blocks)])
    result = None
    for chunk, blocks in enumerate(spectra):
        result = gated_traces(onset, blocks, chunk, result)
    return result


def solution(mesh):
    in_specs = (
        P("freq", None, "tile", None),
        P("freq", None, "tile", None),
        P("freq", "tile", None, None, None, None),
        P("freq", None, "tile", None, None, None),
        P("freq", None, None),
        P(("tile", "freq"), None),
    )
    out_specs = P(None, ("tile", "freq"), None)

    return jax.shard_map(body, mesh=mesh, in_specs=in_specs, out_specs=out_specs, check_vma=False)
```

```python
import functools
import math

import jax
import jax.numpy as jnp
from jax import lax
from jax.experimental import pallas as pl
from jax.experimental.pallas import tpu as pltpu
from jax.sharding import PartitionSpec as P


RMAX = 96
LANES = 128
CHUNKS = 1
BF16 = jnp.bfloat16
F32 = jnp.float32
VMEM = pl.BlockSpec(memory_space=pltpu.VMEM)
SMEM = pl.BlockSpec(memory_space=pltpu.SMEM)
ANY = pl.BlockSpec(memory_space=pl.ANY)
HBM = pl.BlockSpec(memory_space=pltpu.MemorySpace.HBM)


def params():
    return pltpu.CompilerParams(vmem_limit_bytes=20 * 1024 * 1024)


def level_mask(rank):
    level = lax.broadcasted_iota(jnp.int32, (RMAX, LANES), 0)
    return (level < rank).astype(F32)


def masked(value, mask):
    copies = value.shape[1] // LANES
    return (value * jnp.concatenate([mask] * copies, axis=1)).astype(BF16)


def cost(flops):
    return pl.CostEstimate(flops=flops, bytes_accessed=10**7, transcendentals=0)


def coeff_outputs(ks, masks, factors, field, product, outs):
    stations = factors.shape[3]
    left = factors[...].reshape(len(ks) * 2 * RMAX, stations)
    half = field.shape[2] // LANES
    parts = 2 * half
    for p in range(2):
        result = jnp.dot(left, field[p], preferred_element_type=F32)
        for j in range(half):
            product[p * half + j] = result[:, j * LANES : (j + 1) * LANES]
    for i, k in enumerate(ks):
        mask = masks[i]
        base = i * 2 * RMAX
        even = [product[j, pl.ds(base, RMAX, stride=2), :] for j in range(parts)]
        odd = [product[j, pl.ds(base + 1, RMAX, stride=2), :] for j in range(parts)]
        for j in range(half):
            real = masked(even[j] + odd[half + j], mask)
            imag = masked(even[half + j] - odd[j], mask)
            outs[i][:, j * LANES : (j + 1) * LANES] = real
            outs[i][:, (half + j) * LANES : (half + j + 1) * LANES] = imag


def coeff_first_kernel(first, rest, *refs):
    rank_hbm, v_hbm, x_hbm = refs[:3]
    outs = refs[3 : 3 + len(first)]
    field, rest_factors, rest_masks = refs[3 + len(first) : 6 + len(first)]
    rank_ref, factors, product, sems, rest_sems, field_sem, rank_sem = refs[6 + len(first) :]
    me = lax.axis_index("tile")

    def load(k, target, sem):
        return pltpu.make_async_copy(v_hbm.at[me ^ k, pl.ds(0, RMAX)], target, sem)

    rank_copy = pltpu.make_async_copy(rank_hbm, rank_ref, rank_sem)
    field_copy = pltpu.make_async_copy(x_hbm, field, field_sem)
    copies = [load(k, factors.at[i], sems.at[i]) for i, k in enumerate(first)]
    rest_copies = [load(k, rest_factors.at[i], rest_sems.at[i]) for i, k in enumerate(rest)]
    field_copy.start()
    for copy in copies:
        copy.start()
    rank_copy.start()
    for copy in rest_copies:
        copy.start()
    rank_copy.wait()
    for i, k in enumerate(rest):
        rest_masks[i] = level_mask(rank_ref[me ^ k, me])
    masks = [level_mask(rank_ref[me ^ k, me]) for k in first]
    field_copy.wait()
    for copy in copies:
        copy.wait()
    coeff_outputs(first, masks, factors, field, product, outs)
    for copy in rest_copies:
        copy.wait()


def coeff_first(ranks, v, x, first, rest):
    stations, virtual = x.shape[1], x.shape[2]
    outs = [jax.ShapeDtypeStruct((RMAX, 2 * virtual), BF16) for _ in first]
    outs.append(jax.ShapeDtypeStruct(x.shape, BF16))
    outs.append(jax.ShapeDtypeStruct((len(rest), RMAX, 2, stations), BF16))
    outs.append(jax.ShapeDtypeStruct((len(rest), RMAX, LANES), F32))
    return pl.pallas_call(
        functools.partial(coeff_first_kernel, first, rest),
        out_shape=outs,
        in_specs=[HBM, HBM, HBM],
        out_specs=[VMEM for _ in outs],
        scratch_shapes=[
            pltpu.SMEM(ranks.shape, jnp.int32),
            pltpu.VMEM((len(first), RMAX, 2, stations), BF16),
            pltpu.VMEM((2 * virtual // LANES, len(first) * 2 * RMAX, LANES), F32),
            pltpu.SemaphoreType.DMA((len(first),)),
            pltpu.SemaphoreType.DMA((len(rest),)),
            pltpu.SemaphoreType.DMA,
            pltpu.SemaphoreType.DMA,
        ],
        compiler_params=params(),
        cost_estimate=cost(10**9),
        name="coeff_first",
    )(ranks, v, x)


def coeff_rest_kernel(rest, *refs):
    masks, field, factors = refs[:3]
    outs = refs[3 : 3 + len(rest)]
    coeff_outputs(rest, [masks[i] for i in range(len(rest))], factors, field, refs[-1], outs)


def coeff_rest(masks, field, factors, rest):
    width = 2 * field.shape[2]
    return pl.pallas_call(
        functools.partial(coeff_rest_kernel, rest),
        out_shape=[jax.ShapeDtypeStruct((RMAX, width), BF16) for _ in rest],
        in_specs=[VMEM, VMEM, VMEM],
        out_specs=[VMEM for _ in rest],
        scratch_shapes=[pltpu.VMEM((width // LANES, len(rest) * 2 * RMAX, LANES), F32)],
        compiler_params=params(),
        cost_estimate=cost(10**9),
        name="coeff_rest",
    )(masks, field, factors)


def prepare_kernel(want_rows, *refs):
    w_hbm, rank_ref = refs[:2]
    turned_ref = refs[3]
    if want_rows:
        rows_ref, masks = refs[4:6]
        factors, spread, paired, sems = refs[6:]
    else:
        rows_ref = masks = None
        factors, spread, paired, sems = refs[4:]
    me = lax.axis_index("tile")
    count = factors.shape[0]
    stations = factors.shape[3]
    columns = stations // LANES
    copies = [
        pltpu.make_async_copy(w_hbm.at[me ^ k, pl.ds(0, RMAX)], factors.at[k], sems.at[k])
        for k in range(count)
    ]
    for copy in copies:
        copy.start()
    if masks is not None:
        for k in range(count):
            masks[k] = level_mask(rank_ref[me, me ^ k])
    for k in range(count):
        copies[k].wait()
        flat = factors[k].reshape(2 * RMAX, stations).astype(F32)
        for j in range(columns):
            spread[j] = flat[:, j * LANES : (j + 1) * LANES]
        for p in range(2):
            for j in range(columns):
                piece = spread[j, pl.ds(p, RMAX, stride=2), :].astype(BF16)
                row = (2 * p + k % 2) * RMAX
                paired[row : row + RMAX, j * LANES : (j + 1) * LANES] = piece
                if rows_ref is not None:
                    column = p * stations + j * LANES
                    rows_ref[k * RMAX : (k + 1) * RMAX, column : column + LANES] = piece
        if k % 2:
            for i in range(4 * RMAX // LANES):
                block = paired[i * LANES : (i + 1) * LANES, :]
                turned_ref[k // 2, :, i * LANES : (i + 1) * LANES] = block.T


def prepare(w, ranks, after, want_rows):
    count, _, _, stations = w.shape
    outs = [jax.ShapeDtypeStruct((count // 2, stations, 4 * RMAX), BF16)]
    if want_rows:
        outs.append(jax.ShapeDtypeStruct((count * RMAX, 2 * stations), BF16))
        outs.append(jax.ShapeDtypeStruct((count, RMAX, LANES), F32))
    return pl.pallas_call(
        functools.partial(prepare_kernel, want_rows),
        out_shape=outs,
        in_specs=[HBM, SMEM, ANY],
        out_specs=[VMEM for _ in outs],
        scratch_shapes=[
            pltpu.VMEM((count, RMAX, 2, stations), BF16),
            pltpu.VMEM((stations // LANES, 2 * RMAX, LANES), F32),
            pltpu.VMEM((4 * RMAX, stations), BF16),
            pltpu.SemaphoreType.DMA((count,)),
        ],
        compiler_params=params(),
        cost_estimate=cost(10**9),
        name="prepare",
    )(w, ranks, after)


def apply_pairs(bases, blocks, turned_ref):
    virtual = blocks[0].shape[1] // 2
    total = None
    for i, base in enumerate(bases):
        pair = [blocks[2 * i][...], blocks[2 * i + 1][...]]
        turned = [jnp.concatenate([-b[:, virtual:], b[:, :virtual]], axis=1) for b in pair]
        stack = jnp.concatenate(pair + turned, axis=0)
        term = jnp.dot(turned_ref[base // 2], stack, preferred_element_type=F32)
        total = term if total is None else total + term
    return total


def partial_kernel(bases, *refs):
    turned_ref = refs[0]
    out_ref = refs[-1]
    out_ref[...] = apply_pairs(bases, refs[1:-1], turned_ref)


def partial_sum(turned, bases, blocks):
    stations = turned.shape[1]
    width = blocks[0].shape[1]
    return pl.pallas_call(
        functools.partial(partial_kernel, bases),
        out_shape=jax.ShapeDtypeStruct((stations, width), F32),
        in_specs=[VMEM] * (1 + len(blocks)),
        out_specs=VMEM,
        compiler_params=params(),
        cost_estimate=cost(10**9),
        name="partial_sum",
    )(turned, *blocks)


def adjoint_outputs(ks, masks, rows_ref, stacked, outs):
    low = min(ks)
    rows = rows_ref[low * RMAX : (low + len(ks)) * RMAX, :]
    product = jnp.dot(rows, stacked[...], preferred_element_type=F32)
    for i, k in enumerate(ks):
        block = product[(k - low) * RMAX : (k - low + 1) * RMAX, :]
        outs[i][...] = masked(block, masks[k])


def residual_kernel(base, ks, *refs):
    masks, rows_ref, turned_ref, data_ref, partial_ref = refs[:5]
    blocks = refs[5:7]
    outs = refs[7 : 7 + len(ks)]
    stacked = refs[7 + len(ks)]
    stations, virtual = data_ref.shape[1], data_ref.shape[2]
    predicted = partial_ref[...] + apply_pairs((base,), blocks, turned_ref)
    real = (predicted[:, :virtual] - data_ref[0].astype(F32)).astype(BF16)
    imag = (predicted[:, virtual:] - data_ref[1].astype(F32)).astype(BF16)
    stacked[:stations, :virtual] = real
    stacked[:stations, virtual:] = imag
    stacked[stations:, :virtual] = imag
    stacked[stations:, virtual:] = -real
    adjoint_outputs(ks, masks, rows_ref, stacked, outs)


def residual_blocks(masks, rows, turned, data, partial, base, blocks, ks):
    stations, virtual = data.shape[1], data.shape[2]
    outs = [jax.ShapeDtypeStruct((RMAX, 2 * virtual), BF16) for _ in ks]
    outs.append(jax.ShapeDtypeStruct((2 * stations, 2 * virtual), BF16))
    return pl.pallas_call(
        functools.partial(residual_kernel, base, ks),
        out_shape=outs,
        in_specs=[VMEM] * 7,
        out_specs=[VMEM for _ in outs],
        compiler_params=params(),
        cost_estimate=cost(10**9),
        name="residual_blocks",
    )(masks, rows, turned, data, partial, *blocks)


def adjoint_kernel(ks, *refs):
    adjoint_outputs(ks, *refs[:3], refs[3:])


def adjoint_blocks(masks, rows, stacked, ks):
    width = stacked.shape[1]
    return pl.pallas_call(
        functools.partial(adjoint_kernel, ks),
        out_shape=[jax.ShapeDtypeStruct((RMAX, width), BF16) for _ in ks],
        in_specs=[VMEM, VMEM, VMEM],
        out_specs=[VMEM for _ in ks],
        compiler_params=params(),
        cost_estimate=cost(10**9),
        name="adjoint_blocks",
    )(masks, rows, stacked)


def spectrum_kernel(base, freqs, chunk, *refs):
    turned_ref, partial_ref = refs[:2]
    pair = refs[2:4]
    outs = refs[4 : 4 + freqs]
    spectrum = refs[4 + freqs]
    mine = lax.axis_index("freq")
    virtual = partial_ref.shape[1] // 2
    width = outs[0].shape[1] // 2
    real = slice(chunk * width, (chunk + 1) * width)
    imag = slice(virtual + chunk * width, virtual + (chunk + 1) * width)
    stack = [jnp.concatenate([b[:, real], b[:, imag]], axis=1) for b in pair]
    stack += [jnp.concatenate([-b[:, imag], b[:, real]], axis=1) for b in pair]
    late = jnp.dot(
        turned_ref[base // 2], jnp.concatenate(stack, axis=0), preferred_element_type=F32
    )
    spectrum[:, :width] = partial_ref[:, real] + late[:, :width]
    spectrum[:, width:] = partial_ref[:, imag] + late[:, width:]
    share = outs[0].shape[0]
    for k in range(freqs):
        rows = pl.ds(pl.multiple_of((mine ^ k) * share, 8), share)
        outs[k][...] = spectrum[rows, :].astype(BF16)


def spectrum_blocks(turned, partial, base, blocks, freqs, chunk):
    stations, columns = partial.shape
    columns //= CHUNKS
    return pl.pallas_call(
        functools.partial(spectrum_kernel, base, freqs, chunk),
        out_shape=[
            jax.ShapeDtypeStruct((stations // freqs, columns), BF16) for _ in range(freqs)
        ],
        in_specs=[VMEM] * 4,
        out_specs=[VMEM] * freqs,
        scratch_shapes=[pltpu.VMEM((stations, columns), F32)],
        compiler_params=params(),
        cost_estimate=cost(5 * 10**8),
        name="spectrum_blocks",
    )(turned, partial, *blocks)


def traces_kernel(freqs, chunk, *refs):
    onset_ref = refs[0]
    blocks = refs[1 : 1 + freqs]
    out_hbm, gathered, traces, sems = refs[-4:]
    mine = lax.axis_index("freq")
    for k in range(freqs):
        gathered[mine ^ k] = blocks[k][...]
    times = 2 * freqs
    scaling = 1.0 / math.sqrt(freqs)
    width = blocks[0].shape[1] // 2
    lanes = pl.ds(chunk * width, width)
    copies = [
        pltpu.make_async_copy(traces.at[t], out_hbm.at[t, :, lanes], sems.at[t])
        for t in range(times)
    ]
    onset = onset_ref[:, lanes]
    for t in range(freqs):
        sums = [None, None]
        for f in range(freqs):
            turn = (f + 1) * t % times
            angle = 2.0 * math.pi * turn / times
            quarter = 4 * turn % times == 0
            for part, weight in ((0, math.cos(angle)), (1, -math.sin(angle))):
                if quarter:
                    weight = float(round(weight))
                if weight != 0.0:
                    value = gathered[f, :, part * width : (part + 1) * width]
                    term = value.astype(F32) * (weight * scaling)
                    old = sums[f % 2]
                    sums[f % 2] = term if old is None else old + term
        odd, even = sums
        traces[t] = jnp.where(t >= onset, even + odd, 0.0)
        copies[t].start()
        traces[t + freqs] = jnp.where(t + freqs >= onset, even - odd, 0.0)
        copies[t + freqs].start()
    for copy in copies:
        copy.wait()


def gated_traces(onset, blocks, chunk, before):
    freqs = len(blocks)
    share, virtual = onset.shape
    operands = (onset, *blocks)
    specs = [VMEM] * (1 + freqs)
    aliases = {}
    if before is not None:
        aliases = {len(operands): 0}
        operands += (before,)
        specs.append(HBM)
    return pl.pallas_call(
        functools.partial(traces_kernel, freqs, chunk),
        out_shape=jax.ShapeDtypeStruct((2 * freqs, share, virtual), F32),
        in_specs=specs,
        out_specs=HBM,
        scratch_shapes=[
            pltpu.VMEM((freqs, *blocks[0].shape), BF16),
            pltpu.VMEM((2 * freqs, share, blocks[0].shape[1] // 2), F32),
            pltpu.SemaphoreType.DMA((2 * freqs,)),
        ],
        input_output_aliases=aliases,
        compiler_params=params(),
        cost_estimate=cost(5 * 10**8),
        name="gated_traces",
    )(*operands)


def send(block, axis, k):
    count = lax.axis_size(axis)
    return lax.ppermute(block, axis, [(i, i ^ k) for i in range(count)])


def exchange(ks, blocks):
    return {k: send(b, "tile", k) if k else b for k, b in zip(ks, blocks)}


def pick(arrived, bases):
    return [arrived[base + b] for base in bases for b in range(2)]


def pair_bases(count):
    return list(range(count - 2, -1, -2))


def peer_order(count):
    far = [base + b for base in pair_bases(count) if base >= count // 2 for b in range(2)]
    near = [base + b for base in pair_bases(count) if 0 < base < count // 2 for b in range(2)]
    return tuple(far[:2]), tuple(far[2:3] + near + far[3:] + [1, 0])


def hbm(array):
    return pltpu.with_memory_space_constraint(array, pltpu.MemorySpace.HBM)


def body(x_field, data, u_bases, v_bases, ranks, onset):
    count = lax.axis_size("tile")
    freqs = lax.axis_size("freq")
    table = ranks[0]
    u = hbm(u_bases[0, 0])
    v = hbm(v_bases[0, :, 0])
    x = hbm(x_field[0])
    late = count // 2
    early = tuple(base for base in pair_bases(count) if base != late)
    first, rest = peer_order(count)
    *blocks, field, rest_factors, rest_masks = coeff_first(hbm(table), v, x, first, rest)
    arrived = exchange(first, blocks)
    blocks = coeff_rest(rest_masks, field, rest_factors, rest)
    arrived |= exchange(rest, blocks)
    u_turned, u_rows, masks = prepare(u, table, blocks[0], True)
    partial = partial_sum(u_turned, early, pick(arrived, early))
    *blocks, stacked = residual_blocks(
        masks, u_rows, u_turned, data[0], partial, late, pick(arrived, (late,)), first
    )
    returned = exchange(first, blocks)
    blocks = adjoint_blocks(masks, u_rows, stacked, rest)
    returned |= exchange(rest, blocks)
    (v_turned,) = prepare(v, table, stacked, False)
    late = first[0]
    early = tuple(base for base in pair_bases(count) if base != late)
    partial = partial_sum(v_turned, early, pick(returned, early))
    spectra = []
    for chunk in range(CHUNKS):
        blocks = spectrum_blocks(
            v_turned, partial, late, pick(returned, (late,)), freqs, chunk
        )
        spectra.append([send(b, "freq", k) if k else b for k, b in enumerate(blocks)])
    result = None
    for chunk, blocks in enumerate(spectra):
        result = gated_traces(onset, blocks, chunk, result)
    return result


def solution(mesh):
    in_specs = (
        P("freq", None, "tile", None),
        P("freq", None, "tile", None),
        P("freq", "tile", None, None, None, None),
        P("freq", None, "tile", None, None, None),
        P("freq", None, None),
        P(("tile", "freq"), None),
    )
    out_specs = P(None, ("tile", "freq"), None)

    return jax.shard_map(body, mesh=mesh, in_specs=in_specs, out_specs=out_specs, check_vma=False)
```

```python
import functools
import math

import jax
import jax.numpy as jnp
from jax import lax
from jax.experimental import pallas as pl
from jax.experimental.pallas import tpu as pltpu
from jax.sharding import PartitionSpec as P


RMAX = 96
LANES = 128
PARTS = 2
BF16 = jnp.bfloat16
F32 = jnp.float32
VMEM = pl.BlockSpec(memory_space=pltpu.VMEM)
SMEM = pl.BlockSpec(memory_space=pltpu.SMEM)
ANY = pl.BlockSpec(memory_space=pl.ANY)
HBM = pl.BlockSpec(memory_space=pltpu.MemorySpace.HBM)


def params():
    return pltpu.CompilerParams(vmem_limit_bytes=20 * 1024 * 1024)


def level_mask(rank):
    level = lax.broadcasted_iota(jnp.int32, (RMAX, LANES), 0)
    return (level < rank).astype(F32)


def masked(value, mask):
    copies = value.shape[1] // LANES
    return (value * jnp.concatenate([mask] * copies, axis=1)).astype(BF16)


def cost(flops):
    return pl.CostEstimate(flops=flops, bytes_accessed=10**7, transcendentals=0)


def coeff_outputs(ks, masks, factors, field, product, outs):
    stations = factors.shape[3]
    left = factors[...].reshape(len(ks) * 2 * RMAX, stations)
    half = field.shape[2] // LANES
    parts = 2 * half
    for p in range(2):
        result = jnp.dot(left, field[p], preferred_element_type=F32)
        for j in range(half):
            product[p * half + j] = result[:, j * LANES : (j + 1) * LANES]
    for i, k in enumerate(ks):
        mask = masks[i]
        base = i * 2 * RMAX
        even = [product[j, pl.ds(base, RMAX, stride=2), :] for j in range(parts)]
        odd = [product[j, pl.ds(base + 1, RMAX, stride=2), :] for j in range(parts)]
        for j in range(half):
            real = masked(even[j] + odd[half + j], mask)
            imag = masked(even[half + j] - odd[j], mask)
            outs[i][:, j * LANES : (j + 1) * LANES] = real
            outs[i][:, (half + j) * LANES : (half + j + 1) * LANES] = imag


def coeff_first_kernel(first, rest, *refs):
    rank_hbm, v_hbm, x_hbm = refs[:3]
    outs = refs[3 : 3 + len(first)]
    field, rest_factors, rest_masks = refs[3 + len(first) : 6 + len(first)]
    rank_ref, factors, product, sems, rest_sems, field_sem, rank_sem = refs[6 + len(first) :]
    me = lax.axis_index("tile")

    def load(k, target, sem):
        return pltpu.make_async_copy(v_hbm.at[me ^ k, pl.ds(0, RMAX)], target, sem)

    rank_copy = pltpu.make_async_copy(rank_hbm, rank_ref, rank_sem)
    field_copy = pltpu.make_async_copy(x_hbm, field, field_sem)
    copies = [load(k, factors.at[i], sems.at[i]) for i, k in enumerate(first)]
    rest_copies = [load(k, rest_factors.at[i], rest_sems.at[i]) for i, k in enumerate(rest)]
    field_copy.start()
    for copy in copies:
        copy.start()
    rank_copy.start()
    for copy in rest_copies:
        copy.start()
    rank_copy.wait()
    for i, k in enumerate(rest):
        rest_masks[i] = level_mask(rank_ref[me ^ k, me])
    masks = [level_mask(rank_ref[me ^ k, me]) for k in first]
    field_copy.wait()
    for copy in copies:
        copy.wait()
    coeff_outputs(first, masks, factors, field, product, outs)
    for copy in rest_copies:
        copy.wait()


def coeff_first(ranks, v, x, first, rest):
    stations, virtual = x.shape[1], x.shape[2]
    outs = [jax.ShapeDtypeStruct((RMAX, 2 * virtual), BF16) for _ in first]
    outs.append(jax.ShapeDtypeStruct(x.shape, BF16))
    outs.append(jax.ShapeDtypeStruct((len(rest), RMAX, 2, stations), BF16))
    outs.append(jax.ShapeDtypeStruct((len(rest), RMAX, LANES), F32))
    return pl.pallas_call(
        functools.partial(coeff_first_kernel, first, rest),
        out_shape=outs,
        in_specs=[HBM, HBM, HBM],
        out_specs=[VMEM for _ in outs],
        scratch_shapes=[
            pltpu.SMEM(ranks.shape, jnp.int32),
            pltpu.VMEM((len(first), RMAX, 2, stations), BF16),
            pltpu.VMEM((2 * virtual // LANES, len(first) * 2 * RMAX, LANES), F32),
            pltpu.SemaphoreType.DMA((len(first),)),
            pltpu.SemaphoreType.DMA((len(rest),)),
            pltpu.SemaphoreType.DMA,
            pltpu.SemaphoreType.DMA,
        ],
        compiler_params=params(),
        cost_estimate=cost(10**9),
        name="coeff_first",
    )(ranks, v, x)


def coeff_rest_kernel(rest, *refs):
    masks, field, factors = refs[:3]
    outs = refs[3 : 3 + len(rest)]
    coeff_outputs(rest, [masks[i] for i in range(len(rest))], factors, field, refs[-1], outs)


def coeff_rest(masks, field, factors, rest):
    width = 2 * field.shape[2]
    return pl.pallas_call(
        functools.partial(coeff_rest_kernel, rest),
        out_shape=[jax.ShapeDtypeStruct((RMAX, width), BF16) for _ in rest],
        in_specs=[VMEM, VMEM, VMEM],
        out_specs=[VMEM for _ in rest],
        scratch_shapes=[pltpu.VMEM((width // LANES, len(rest) * 2 * RMAX, LANES), F32)],
        compiler_params=params(),
        cost_estimate=cost(10**9),
        name="coeff_rest",
    )(masks, field, factors)


def prepare_kernel(want_rows, *refs):
    w_hbm, rank_ref = refs[:2]
    turned_ref = refs[3]
    if want_rows:
        rows_ref, masks = refs[4:6]
        factors, spread, paired, sems = refs[6:]
    else:
        rows_ref = masks = None
        factors, spread, paired, sems = refs[4:]
    me = lax.axis_index("tile")
    count = factors.shape[0]
    stations = factors.shape[3]
    columns = stations // LANES
    copies = [
        pltpu.make_async_copy(w_hbm.at[me ^ k, pl.ds(0, RMAX)], factors.at[k], sems.at[k])
        for k in range(count)
    ]
    for copy in copies:
        copy.start()
    if masks is not None:
        for k in range(count):
            masks[k] = level_mask(rank_ref[me, me ^ k])
    for k in range(count):
        copies[k].wait()
        flat = factors[k].reshape(2 * RMAX, stations).astype(F32)
        for j in range(columns):
            spread[j] = flat[:, j * LANES : (j + 1) * LANES]
        for p in range(2):
            for j in range(columns):
                piece = spread[j, pl.ds(p, RMAX, stride=2), :].astype(BF16)
                row = (2 * p + k % 2) * RMAX
                paired[row : row + RMAX, j * LANES : (j + 1) * LANES] = piece
                if rows_ref is not None:
                    column = p * stations + j * LANES
                    rows_ref[k * RMAX : (k + 1) * RMAX, column : column + LANES] = piece
        if k % 2:
            for i in range(4 * RMAX // LANES):
                block = paired[i * LANES : (i + 1) * LANES, :]
                turned_ref[k // 2, :, i * LANES : (i + 1) * LANES] = block.T


def prepare(w, ranks, after, want_rows):
    count, _, _, stations = w.shape
    outs = [jax.ShapeDtypeStruct((count // 2, stations, 4 * RMAX), BF16)]
    if want_rows:
        outs.append(jax.ShapeDtypeStruct((count * RMAX, 2 * stations), BF16))
        outs.append(jax.ShapeDtypeStruct((count, RMAX, LANES), F32))
    return pl.pallas_call(
        functools.partial(prepare_kernel, want_rows),
        out_shape=outs,
        in_specs=[HBM, SMEM, ANY],
        out_specs=[VMEM for _ in outs],
        scratch_shapes=[
            pltpu.VMEM((count, RMAX, 2, stations), BF16),
            pltpu.VMEM((stations // LANES, 2 * RMAX, LANES), F32),
            pltpu.VMEM((4 * RMAX, stations), BF16),
            pltpu.SemaphoreType.DMA((count,)),
        ],
        compiler_params=params(),
        cost_estimate=cost(10**9),
        name="prepare",
    )(w, ranks, after)


def apply_pairs(bases, blocks, turned_ref):
    virtual = blocks[0].shape[1] // 2
    total = None
    for i, base in enumerate(bases):
        pair = [blocks[2 * i][...], blocks[2 * i + 1][...]]
        turned = [jnp.concatenate([-b[:, virtual:], b[:, :virtual]], axis=1) for b in pair]
        stack = jnp.concatenate(pair + turned, axis=0)
        term = jnp.dot(turned_ref[base // 2], stack, preferred_element_type=F32)
        total = term if total is None else total + term
    return total


def partial_kernel(bases, *refs):
    turned_ref = refs[0]
    out_ref = refs[-1]
    out_ref[...] = apply_pairs(bases, refs[1:-1], turned_ref)


def partial_sum(turned, bases, blocks):
    stations = turned.shape[1]
    width = blocks[0].shape[1]
    return pl.pallas_call(
        functools.partial(partial_kernel, bases),
        out_shape=jax.ShapeDtypeStruct((stations, width), F32),
        in_specs=[VMEM] * (1 + len(blocks)),
        out_specs=VMEM,
        compiler_params=params(),
        cost_estimate=cost(10**9),
        name="partial_sum",
    )(turned, *blocks)


def adjoint_outputs(ks, masks, rows_ref, stacked, outs):
    low = min(ks)
    rows = rows_ref[low * RMAX : (low + len(ks)) * RMAX, :]
    product = jnp.dot(rows, stacked[...], preferred_element_type=F32)
    for i, k in enumerate(ks):
        block = product[(k - low) * RMAX : (k - low + 1) * RMAX, :]
        outs[i][...] = masked(block, masks[k])


def residual_kernel(base, ks, *refs):
    masks, rows_ref, turned_ref, data_ref, partial_ref = refs[:5]
    blocks = refs[5:7]
    outs = refs[7 : 7 + len(ks)]
    stacked = refs[7 + len(ks)]
    stations, virtual = data_ref.shape[1], data_ref.shape[2]
    predicted = partial_ref[...] + apply_pairs((base,), blocks, turned_ref)
    real = (predicted[:, :virtual] - data_ref[0].astype(F32)).astype(BF16)
    imag = (predicted[:, virtual:] - data_ref[1].astype(F32)).astype(BF16)
    stacked[:stations, :virtual] = real
    stacked[:stations, virtual:] = imag
    stacked[stations:, :virtual] = imag
    stacked[stations:, virtual:] = -real
    adjoint_outputs(ks, masks, rows_ref, stacked, outs)


def residual_blocks(masks, rows, turned, data, partial, base, blocks, ks):
    stations, virtual = data.shape[1], data.shape[2]
    outs = [jax.ShapeDtypeStruct((RMAX, 2 * virtual), BF16) for _ in ks]
    outs.append(jax.ShapeDtypeStruct((2 * stations, 2 * virtual), BF16))
    return pl.pallas_call(
        functools.partial(residual_kernel, base, ks),
        out_shape=outs,
        in_specs=[VMEM] * 7,
        out_specs=[VMEM for _ in outs],
        compiler_params=params(),
        cost_estimate=cost(10**9),
        name="residual_blocks",
    )(masks, rows, turned, data, partial, *blocks)


def adjoint_kernel(ks, *refs):
    adjoint_outputs(ks, *refs[:3], refs[3:])


def adjoint_blocks(masks, rows, stacked, ks):
    width = stacked.shape[1]
    return pl.pallas_call(
        functools.partial(adjoint_kernel, ks),
        out_shape=[jax.ShapeDtypeStruct((RMAX, width), BF16) for _ in ks],
        in_specs=[VMEM, VMEM, VMEM],
        out_specs=[VMEM for _ in ks],
        compiler_params=params(),
        cost_estimate=cost(10**9),
        name="adjoint_blocks",
    )(masks, rows, stacked)


def row_parts(share):
    small = -(-share // 40) * 16
    return [(0, share - small), (share - small, small)]


def spectrum_kernel(base, freqs, parts, *refs):
    turned_ref, partial_ref = refs[:2]
    outs = refs[4:-1]
    spectrum = refs[-1]
    mine = lax.axis_index("freq")
    spectrum[...] = partial_ref[...] + apply_pairs((base,), refs[2:4], turned_ref)
    share = spectrum.shape[0] // freqs
    for p, (start, size) in enumerate(parts):
        for k in range(freqs):
            rows = pl.ds(pl.multiple_of((mine ^ k) * share + start, 8), size)
            outs[p * freqs + k][...] = spectrum[rows, :].astype(BF16)


def spectrum_blocks(turned, partial, base, blocks, freqs):
    stations, width = partial.shape
    parts = row_parts(stations // freqs)
    outs = [jax.ShapeDtypeStruct((size, width), BF16) for _, size in parts for _ in range(freqs)]
    return pl.pallas_call(
        functools.partial(spectrum_kernel, base, freqs, parts),
        out_shape=outs,
        in_specs=[VMEM] * 4,
        out_specs=[VMEM for _ in outs],
        scratch_shapes=[pltpu.VMEM((stations, width), F32)],
        compiler_params=params(),
        cost_estimate=cost(5 * 10**8),
        name="spectrum_blocks",
    )(turned, partial, *blocks)


def traces_kernel(freqs, start, *refs):
    onset_ref = refs[0]
    blocks = refs[1 : 1 + freqs]
    out_hbm, gathered, traces, sems = refs[-4:]
    mine = lax.axis_index("freq")
    for k in range(freqs):
        gathered[mine ^ k] = blocks[k][...]
    times = 2 * freqs
    scaling = 1.0 / math.sqrt(freqs)
    size, width = blocks[0].shape
    width //= 2
    rows = pl.ds(start, size)
    copies = [
        pltpu.make_async_copy(traces.at[t], out_hbm.at[t, rows], sems.at[t])
        for t in range(times)
    ]
    onset = onset_ref[rows, :]
    for t in range(freqs):
        sums = [None, None]
        for f in range(freqs):
            turn = (f + 1) * t % times
            angle = 2.0 * math.pi * turn / times
            quarter = 4 * turn % times == 0
            for part, weight in ((0, math.cos(angle)), (1, -math.sin(angle))):
                if quarter:
                    weight = float(round(weight))
                if weight != 0.0:
                    value = gathered[f, :, part * width : (part + 1) * width]
                    term = value.astype(F32) * (weight * scaling)
                    old = sums[f % 2]
                    sums[f % 2] = term if old is None else old + term
        odd, even = sums
        traces[t] = jnp.where(t >= onset, even + odd, 0.0)
        copies[t].start()
        traces[t + freqs] = jnp.where(t + freqs >= onset, even - odd, 0.0)
        copies[t + freqs].start()
    for copy in copies:
        copy.wait()


def gated_traces(onset, blocks, start, before):
    freqs = len(blocks)
    share, virtual = onset.shape
    operands = (onset, *blocks)
    specs = [VMEM] * (1 + freqs)
    aliases = {}
    if before is not None:
        aliases = {len(operands): 0}
        operands += (before,)
        specs.append(HBM)
    return pl.pallas_call(
        functools.partial(traces_kernel, freqs, start),
        out_shape=jax.ShapeDtypeStruct((2 * freqs, share, virtual), F32),
        in_specs=specs,
        out_specs=HBM,
        scratch_shapes=[
            pltpu.VMEM((freqs, *blocks[0].shape), BF16),
            pltpu.VMEM((2 * freqs, blocks[0].shape[0], virtual), F32),
            pltpu.SemaphoreType.DMA((2 * freqs,)),
        ],
        input_output_aliases=aliases,
        compiler_params=params(),
        cost_estimate=cost(5 * 10**8),
        name="gated_traces",
    )(*operands)


def send(block, axis, k):
    count = lax.axis_size(axis)
    return lax.ppermute(block, axis, [(i, i ^ k) for i in range(count)])


def exchange(ks, blocks):
    return {k: send(b, "tile", k) if k else b for k, b in zip(ks, blocks)}


def pick(arrived, bases):
    return [arrived[base + b] for base in bases for b in range(2)]


def pair_bases(count):
    return list(range(count - 2, -1, -2))


def peer_order(count):
    far = [base + b for base in pair_bases(count) if base >= count // 2 for b in range(2)]
    near = [base + b for base in pair_bases(count) if 0 < base < count // 2 for b in range(2)]
    return tuple(far[:2]), tuple(far[2:3] + near + far[3:] + [1, 0])


def hbm(array):
    return pltpu.with_memory_space_constraint(array, pltpu.MemorySpace.HBM)


def body(x_field, data, u_bases, v_bases, ranks, onset):
    count = lax.axis_size("tile")
    freqs = lax.axis_size("freq")
    table = ranks[0]
    u = hbm(u_bases[0, 0])
    v = hbm(v_bases[0, :, 0])
    x = hbm(x_field[0])
    late = count // 2
    early = tuple(base for base in pair_bases(count) if base != late)
    first, rest = peer_order(count)
    *blocks, field, rest_factors, rest_masks = coeff_first(hbm(table), v, x, first, rest)
    arrived = exchange(first, blocks)
    blocks = coeff_rest(rest_masks, field, rest_factors, rest)
    arrived |= exchange(rest, blocks)
    u_turned, u_rows, masks = prepare(u, table, blocks[0], True)
    partial = partial_sum(u_turned, early, pick(arrived, early))
    *blocks, stacked = residual_blocks(
        masks, u_rows, u_turned, data[0], partial, late, pick(arrived, (late,)), first
    )
    returned = exchange(first, blocks)
    blocks = adjoint_blocks(masks, u_rows, stacked, rest)
    returned |= exchange(rest, blocks)
    (v_turned,) = prepare(v, table, stacked, False)
    late = first[0]
    early = tuple(base for base in pair_bases(count) if base != late)
    partial = partial_sum(v_turned, early, pick(returned, early))
    blocks = spectrum_blocks(v_turned, partial, late, pick(returned, (late,)), freqs)
    spectra = []
    for p in range(PARTS):
        part = blocks[p * freqs : (p + 1) * freqs]
        spectra.append([send(b, "freq", k) if k else b for k, b in enumerate(part)])
    result = None
    for p, (start, _) in enumerate(row_parts(onset.shape[0])):
        result = gated_traces(onset, spectra[p], start, result)
    return result


def solution(mesh):
    in_specs = (
        P("freq", None, "tile", None),
        P("freq", None, "tile", None),
        P("freq", "tile", None, None, None, None),
        P("freq", None, "tile", None, None, None),
        P("freq", None, None),
        P(("tile", "freq"), None),
    )
    out_specs = P(None, ("tile", "freq"), None)

    return jax.shard_map(body, mesh=mesh, in_specs=in_specs, out_specs=out_specs, check_vma=False)
```

```python
import functools
import math

import jax
import jax.numpy as jnp
from jax import lax
from jax.experimental import pallas as pl
from jax.experimental.pallas import tpu as pltpu
from jax.sharding import PartitionSpec as P


RMAX = 96
LANES = 128
PARTS = 2
BF16 = jnp.bfloat16
F32 = jnp.float32
VMEM = pl.BlockSpec(memory_space=pltpu.VMEM)
SMEM = pl.BlockSpec(memory_space=pltpu.SMEM)
ANY = pl.BlockSpec(memory_space=pl.ANY)
HBM = pl.BlockSpec(memory_space=pltpu.MemorySpace.HBM)


def params():
    return pltpu.CompilerParams(vmem_limit_bytes=20 * 1024 * 1024)


def swapped(k, freqs):
    bits = freqs.bit_length() - 1
    if bits % 2:
        return k
    half = bits // 2
    return (k % (1 << half) << half) | (k >> half)


def freq_peer(k, freqs):
    turn = jnp.where(lax.axis_index("tile") % 2 == 1, k, swapped(k, freqs))
    return lax.axis_index("freq") ^ turn


def level_mask(rank):
    level = lax.broadcasted_iota(jnp.int32, (RMAX, LANES), 0)
    return (level < rank).astype(F32)


def masked(value, mask):
    copies = value.shape[1] // LANES
    return (value * jnp.concatenate([mask] * copies, axis=1)).astype(BF16)


def cost(flops):
    return pl.CostEstimate(flops=flops, bytes_accessed=10**7, transcendentals=0)


def coeff_outputs(ks, masks, factors, field, product, outs):
    stations = factors.shape[3]
    left = factors[...].reshape(len(ks) * 2 * RMAX, stations)
    half = field.shape[2] // LANES
    parts = 2 * half
    for p in range(2):
        result = jnp.dot(left, field[p], preferred_element_type=F32)
        for j in range(half):
            product[p * half + j] = result[:, j * LANES : (j + 1) * LANES]
    for i, k in enumerate(ks):
        mask = masks[i]
        base = i * 2 * RMAX
        even = [product[j, pl.ds(base, RMAX, stride=2), :] for j in range(parts)]
        odd = [product[j, pl.ds(base + 1, RMAX, stride=2), :] for j in range(parts)]
        for j in range(half):
            real = masked(even[j] + odd[half + j], mask)
            imag = masked(even[half + j] - odd[j], mask)
            outs[i][:, j * LANES : (j + 1) * LANES] = real
            outs[i][:, (half + j) * LANES : (half + j + 1) * LANES] = imag


def coeff_first_kernel(first, rest, *refs):
    rank_hbm, v_hbm, x_hbm = refs[:3]
    outs = refs[3 : 3 + len(first)]
    field, rest_factors, rest_masks = refs[3 + len(first) : 6 + len(first)]
    rank_ref, factors, product, sems, rest_sems, field_sem, rank_sem = refs[6 + len(first) :]
    me = lax.axis_index("tile")

    def load(k, target, sem):
        return pltpu.make_async_copy(v_hbm.at[me ^ k, pl.ds(0, RMAX)], target, sem)

    rank_copy = pltpu.make_async_copy(rank_hbm, rank_ref, rank_sem)
    field_copy = pltpu.make_async_copy(x_hbm, field, field_sem)
    copies = [load(k, factors.at[i], sems.at[i]) for i, k in enumerate(first)]
    rest_copies = [load(k, rest_factors.at[i], rest_sems.at[i]) for i, k in enumerate(rest)]
    field_copy.start()
    for copy in copies:
        copy.start()
    rank_copy.start()
    for copy in rest_copies:
        copy.start()
    rank_copy.wait()
    for i, k in enumerate(rest):
        rest_masks[i] = level_mask(rank_ref[me ^ k, me])
    masks = [level_mask(rank_ref[me ^ k, me]) for k in first]
    field_copy.wait()
    for copy in copies:
        copy.wait()
    coeff_outputs(first, masks, factors, field, product, outs)
    for copy in rest_copies:
        copy.wait()


def coeff_first(ranks, v, x, first, rest):
    stations, virtual = x.shape[1], x.shape[2]
    outs = [jax.ShapeDtypeStruct((RMAX, 2 * virtual), BF16) for _ in first]
    outs.append(jax.ShapeDtypeStruct(x.shape, BF16))
    outs.append(jax.ShapeDtypeStruct((len(rest), RMAX, 2, stations), BF16))
    outs.append(jax.ShapeDtypeStruct((len(rest), RMAX, LANES), F32))
    return pl.pallas_call(
        functools.partial(coeff_first_kernel, first, rest),
        out_shape=outs,
        in_specs=[HBM, HBM, HBM],
        out_specs=[VMEM for _ in outs],
        scratch_shapes=[
            pltpu.SMEM(ranks.shape, jnp.int32),
            pltpu.VMEM((len(first), RMAX, 2, stations), BF16),
            pltpu.VMEM((2 * virtual // LANES, len(first) * 2 * RMAX, LANES), F32),
            pltpu.SemaphoreType.DMA((len(first),)),
            pltpu.SemaphoreType.DMA((len(rest),)),
            pltpu.SemaphoreType.DMA,
            pltpu.SemaphoreType.DMA,
        ],
        compiler_params=params(),
        cost_estimate=cost(10**9),
        name="coeff_first",
    )(ranks, v, x)


def coeff_rest_kernel(rest, *refs):
    masks, field, factors = refs[:3]
    outs = refs[3 : 3 + len(rest)]
    coeff_outputs(rest, [masks[i] for i in range(len(rest))], factors, field, refs[-1], outs)


def coeff_rest(masks, field, factors, rest):
    width = 2 * field.shape[2]
    return pl.pallas_call(
        functools.partial(coeff_rest_kernel, rest),
        out_shape=[jax.ShapeDtypeStruct((RMAX, width), BF16) for _ in rest],
        in_specs=[VMEM, VMEM, VMEM],
        out_specs=[VMEM for _ in rest],
        scratch_shapes=[pltpu.VMEM((width // LANES, len(rest) * 2 * RMAX, LANES), F32)],
        compiler_params=params(),
        cost_estimate=cost(10**9),
        name="coeff_rest",
    )(masks, field, factors)


def prepare_kernel(want_rows, *refs):
    w_hbm, rank_ref = refs[:2]
    turned_ref = refs[3]
    if want_rows:
        rows_ref, masks = refs[4:6]
        factors, spread, paired, sems = refs[6:]
    else:
        rows_ref = masks = None
        factors, spread, paired, sems = refs[4:]
    me = lax.axis_index("tile")
    count = factors.shape[0]
    stations = factors.shape[3]
    columns = stations // LANES
    copies = [
        pltpu.make_async_copy(w_hbm.at[me ^ k, pl.ds(0, RMAX)], factors.at[k], sems.at[k])
        for k in range(count)
    ]
    for copy in copies:
        copy.start()
    if masks is not None:
        for k in range(count):
            masks[k] = level_mask(rank_ref[me, me ^ k])
    for k in range(count):
        copies[k].wait()
        flat = factors[k].reshape(2 * RMAX, stations).astype(F32)
        for j in range(columns):
            spread[j] = flat[:, j * LANES : (j + 1) * LANES]
        for p in range(2):
            for j in range(columns):
                piece = spread[j, pl.ds(p, RMAX, stride=2), :].astype(BF16)
                row = (2 * p + k % 2) * RMAX
                paired[row : row + RMAX, j * LANES : (j + 1) * LANES] = piece
                if rows_ref is not None:
                    column = p * stations + j * LANES
                    rows_ref[k * RMAX : (k + 1) * RMAX, column : column + LANES] = piece
        if k % 2:
            for i in range(4 * RMAX // LANES):
                block = paired[i * LANES : (i + 1) * LANES, :]
                turned_ref[k // 2, :, i * LANES : (i + 1) * LANES] = block.T


def prepare(w, ranks, after, want_rows):
    count, _, _, stations = w.shape
    outs = [jax.ShapeDtypeStruct((count // 2, stations, 4 * RMAX), BF16)]
    if want_rows:
        outs.append(jax.ShapeDtypeStruct((count * RMAX, 2 * stations), BF16))
        outs.append(jax.ShapeDtypeStruct((count, RMAX, LANES), F32))
    return pl.pallas_call(
        functools.partial(prepare_kernel, want_rows),
        out_shape=outs,
        in_specs=[HBM, SMEM, ANY],
        out_specs=[VMEM for _ in outs],
        scratch_shapes=[
            pltpu.VMEM((count, RMAX, 2, stations), BF16),
            pltpu.VMEM((stations // LANES, 2 * RMAX, LANES), F32),
            pltpu.VMEM((4 * RMAX, stations), BF16),
            pltpu.SemaphoreType.DMA((count,)),
        ],
        compiler_params=params(),
        cost_estimate=cost(10**9),
        name="prepare",
    )(w, ranks, after)


def apply_pairs(bases, blocks, turned_ref):
    virtual = blocks[0].shape[1] // 2
    total = None
    for i, base in enumerate(bases):
        pair = [blocks[2 * i][...], blocks[2 * i + 1][...]]
        turned = [jnp.concatenate([-b[:, virtual:], b[:, :virtual]], axis=1) for b in pair]
        stack = jnp.concatenate(pair + turned, axis=0)
        term = jnp.dot(turned_ref[base // 2], stack, preferred_element_type=F32)
        total = term if total is None else total + term
    return total


def partial_kernel(bases, *refs):
    turned_ref = refs[0]
    out_ref = refs[-1]
    out_ref[...] = apply_pairs(bases, refs[1:-1], turned_ref)


def partial_sum(turned, bases, blocks):
    stations = turned.shape[1]
    width = blocks[0].shape[1]
    return pl.pallas_call(
        functools.partial(partial_kernel, bases),
        out_shape=jax.ShapeDtypeStruct((stations, width), F32),
        in_specs=[VMEM] * (1 + len(blocks)),
        out_specs=VMEM,
        compiler_params=params(),
        cost_estimate=cost(10**9),
        name="partial_sum",
    )(turned, *blocks)


def adjoint_outputs(ks, masks, rows_ref, stacked, outs):
    low = min(ks)
    rows = rows_ref[low * RMAX : (low + len(ks)) * RMAX, :]
    product = jnp.dot(rows, stacked[...], preferred_element_type=F32)
    for i, k in enumerate(ks):
        block = product[(k - low) * RMAX : (k - low + 1) * RMAX, :]
        outs[i][...] = masked(block, masks[k])


def residual_kernel(base, ks, *refs):
    masks, rows_ref, turned_ref, data_ref, partial_ref = refs[:5]
    blocks = refs[5:7]
    outs = refs[7 : 7 + len(ks)]
    stacked = refs[7 + len(ks)]
    stations, virtual = data_ref.shape[1], data_ref.shape[2]
    predicted = partial_ref[...] + apply_pairs((base,), blocks, turned_ref)
    real = (predicted[:, :virtual] - data_ref[0].astype(F32)).astype(BF16)
    imag = (predicted[:, virtual:] - data_ref[1].astype(F32)).astype(BF16)
    stacked[:stations, :virtual] = real
    stacked[:stations, virtual:] = imag
    stacked[stations:, :virtual] = imag
    stacked[stations:, virtual:] = -real
    adjoint_outputs(ks, masks, rows_ref, stacked, outs)


def residual_blocks(masks, rows, turned, data, partial, base, blocks, ks):
    stations, virtual = data.shape[1], data.shape[2]
    outs = [jax.ShapeDtypeStruct((RMAX, 2 * virtual), BF16) for _ in ks]
    outs.append(jax.ShapeDtypeStruct((2 * stations, 2 * virtual), BF16))
    return pl.pallas_call(
        functools.partial(residual_kernel, base, ks),
        out_shape=outs,
        in_specs=[VMEM] * 7,
        out_specs=[VMEM for _ in outs],
        compiler_params=params(),
        cost_estimate=cost(10**9),
        name="residual_blocks",
    )(masks, rows, turned, data, partial, *blocks)


def adjoint_kernel(ks, *refs):
    adjoint_outputs(ks, *refs[:3], refs[3:])


def adjoint_blocks(masks, rows, stacked, ks):
    width = stacked.shape[1]
    return pl.pallas_call(
        functools.partial(adjoint_kernel, ks),
        out_shape=[jax.ShapeDtypeStruct((RMAX, width), BF16) for _ in ks],
        in_specs=[VMEM, VMEM, VMEM],
        out_specs=[VMEM for _ in ks],
        compiler_params=params(),
        cost_estimate=cost(10**9),
        name="adjoint_blocks",
    )(masks, rows, stacked)


def row_parts(share):
    small = -(-share // 40) * 16
    return [(0, share - small), (share - small, small)]


def spectrum_kernel(base, freqs, parts, *refs):
    turned_ref, partial_ref = refs[:2]
    outs = refs[4:-1]
    spectrum = refs[-1]
    spectrum[...] = partial_ref[...] + apply_pairs((base,), refs[2:4], turned_ref)
    share = spectrum.shape[0] // freqs
    for p, (start, size) in enumerate(parts):
        for k in range(freqs):
            rows = pl.ds(pl.multiple_of(freq_peer(k, freqs) * share + start, 8), size)
            outs[p * freqs + k][...] = spectrum[rows, :].astype(BF16)


def spectrum_blocks(turned, partial, base, blocks, freqs):
    stations, width = partial.shape
    parts = row_parts(stations // freqs)
    outs = [jax.ShapeDtypeStruct((size, width), BF16) for _, size in parts for _ in range(freqs)]
    return pl.pallas_call(
        functools.partial(spectrum_kernel, base, freqs, parts),
        out_shape=outs,
        in_specs=[VMEM] * 4,
        out_specs=[VMEM for _ in outs],
        scratch_shapes=[pltpu.VMEM((stations, width), F32)],
        compiler_params=params(),
        cost_estimate=cost(5 * 10**8),
        name="spectrum_blocks",
    )(turned, partial, *blocks)


def traces_kernel(freqs, start, *refs):
    onset_ref = refs[0]
    blocks = refs[1 : 1 + freqs]
    out_hbm, gathered, traces, sems = refs[-4:]
    for k in range(freqs):
        gathered[freq_peer(k, freqs)] = blocks[k][...]
    times = 2 * freqs
    scaling = 1.0 / math.sqrt(freqs)
    size, width = blocks[0].shape
    width //= 2
    rows = pl.ds(start, size)
    copies = [
        pltpu.make_async_copy(traces.at[t], out_hbm.at[t, rows], sems.at[t])
        for t in range(times)
    ]
    onset = onset_ref[rows, :]
    for t in range(freqs):
        sums = [None, None]
        for f in range(freqs):
            turn = (f + 1) * t % times
            angle = 2.0 * math.pi * turn / times
            quarter = 4 * turn % times == 0
            for part, weight in ((0, math.cos(angle)), (1, -math.sin(angle))):
                if quarter:
                    weight = float(round(weight))
                if weight != 0.0:
                    value = gathered[f, :, part * width : (part + 1) * width]
                    term = value.astype(F32) * (weight * scaling)
                    old = sums[f % 2]
                    sums[f % 2] = term if old is None else old + term
        odd, even = sums
        traces[t] = jnp.where(t >= onset, even + odd, 0.0)
        copies[t].start()
        traces[t + freqs] = jnp.where(t + freqs >= onset, even - odd, 0.0)
        copies[t + freqs].start()
    for copy in copies:
        copy.wait()


def gated_traces(onset, blocks, start, before):
    freqs = len(blocks)
    share, virtual = onset.shape
    operands = (onset, *blocks)
    specs = [VMEM] * (1 + freqs)
    aliases = {}
    if before is not None:
        aliases = {len(operands): 0}
        operands += (before,)
        specs.append(HBM)
    return pl.pallas_call(
        functools.partial(traces_kernel, freqs, start),
        out_shape=jax.ShapeDtypeStruct((2 * freqs, share, virtual), F32),
        in_specs=specs,
        out_specs=HBM,
        scratch_shapes=[
            pltpu.VMEM((freqs, *blocks[0].shape), BF16),
            pltpu.VMEM((2 * freqs, blocks[0].shape[0], virtual), F32),
            pltpu.SemaphoreType.DMA((2 * freqs,)),
        ],
        input_output_aliases=aliases,
        compiler_params=params(),
        cost_estimate=cost(5 * 10**8),
        name="gated_traces",
    )(*operands)


def send(block, axis, k):
    count = lax.axis_size(axis)
    return lax.ppermute(block, axis, [(i, i ^ k) for i in range(count)])


def send_freq(block, k):
    count = lax.axis_size("tile")
    freqs = lax.axis_size("freq")
    pairs = [
        (f * count + tile, (f ^ (k if tile % 2 else swapped(k, freqs))) * count + tile)
        for f in range(freqs)
        for tile in range(count)
    ]
    return lax.ppermute(block, ("freq", "tile"), pairs)


def exchange(ks, blocks):
    return {k: send(b, "tile", k) if k else b for k, b in zip(ks, blocks)}


def pick(arrived, bases):
    return [arrived[base + b] for base in bases for b in range(2)]


def pair_bases(count):
    return list(range(count - 2, -1, -2))


def peer_order(count):
    far = [base + b for base in pair_bases(count) if base >= count // 2 for b in range(2)]
    near = [base + b for base in pair_bases(count) if 0 < base < count // 2 for b in range(2)]
    return tuple(far[:2]), tuple(far[2:3] + near + far[3:] + [1, 0])


def hbm(array):
    return pltpu.with_memory_space_constraint(array, pltpu.MemorySpace.HBM)


def body(x_field, data, u_bases, v_bases, ranks, onset):
    count = lax.axis_size("tile")
    freqs = lax.axis_size("freq")
    table = ranks[0]
    u = hbm(u_bases[0, 0])
    v = hbm(v_bases[0, :, 0])
    x = hbm(x_field[0])
    late = count // 2
    early = tuple(base for base in pair_bases(count) if base != late)
    first, rest = peer_order(count)
    *blocks, field, rest_factors, rest_masks = coeff_first(hbm(table), v, x, first, rest)
    arrived = exchange(first, blocks)
    blocks = coeff_rest(rest_masks, field, rest_factors, rest)
    arrived |= exchange(rest, blocks)
    u_turned, u_rows, masks = prepare(u, table, blocks[0], True)
    partial = partial_sum(u_turned, early, pick(arrived, early))
    *blocks, stacked = residual_blocks(
        masks, u_rows, u_turned, data[0], partial, late, pick(arrived, (late,)), first
    )
    returned = exchange(first, blocks)
    blocks = adjoint_blocks(masks, u_rows, stacked, rest)
    returned |= exchange(rest, blocks)
    (v_turned,) = prepare(v, table, stacked, False)
    late = first[0]
    early = tuple(base for base in pair_bases(count) if base != late)
    partial = partial_sum(v_turned, early, pick(returned, early))
    blocks = spectrum_blocks(v_turned, partial, late, pick(returned, (late,)), freqs)
    spectra = []
    for p in range(PARTS):
        part = blocks[p * freqs : (p + 1) * freqs]
        spectra.append([send_freq(b, k) if k else b for k, b in enumerate(part)])
    result = None
    for p, (start, _) in enumerate(row_parts(onset.shape[0])):
        result = gated_traces(onset, spectra[p], start, result)
    return result


def solution(mesh):
    in_specs = (
        P("freq", None, "tile", None),
        P("freq", None, "tile", None),
        P("freq", "tile", None, None, None, None),
        P("freq", None, "tile", None, None, None),
        P("freq", None, None),
        P(("tile", "freq"), None),
    )
    out_specs = P(None, ("tile", "freq"), None)

    return jax.shard_map(body, mesh=mesh, in_specs=in_specs, out_specs=out_specs, check_vma=False)
```
